256 devices in a mesh: section: 8 (over y, core), dp: 32 (over z, x).
Axes of the slice: x: 4, y: 4, z: 8, core: 2. Of those that a mesh axis runs over, the one named last changes fastest.
Arguments:
- hidden_in: bfloat16 [4, 1024, 8192], P(None, 'dp'), may hold values from -6 to 6
- cotangent: bfloat16 [4, 1024, 8192], P(None, 'dp'), may hold values from -6 to 6
- adapter_in: bfloat16 [8, 8192, 128], P('section', 'dp'), may hold values from -0.0625 to 0.0625
- adapter_out: bfloat16 [8, 128, 8192], P('section', None, 'dp'), may hold values from -0.5 to 0.5
- norm_gain: bfloat16 [8, 8192], P('section', 'dp'), may hold values from 0.5 to 1.5
- user_of_row: int32 [4, 1024], P(None, 'dp'), may hold values from 0 to 63, as said below
- included: int32 [4, 64], P(None, 'dp'), may hold values 0 or 1
Outputs:
- grad_in: float32 [8, 8192, 128], P('section', 'dp')
- grad_out: float32 [8, 128, 8192], P('section', None, 'dp')
- user_weights: float32 [4, 64], P(None, 'dp')
The draws below stay inside these ranges and needn't reach their ends.
Inputs may be any that keep to these rules, and one draw needn't show every extreme that they name: `user_of_row`: within one micro-batch, the rows of the j-th block of 32 rows belong to users j * 2 to j * 2 + 1, in rising order, each of them with one row or more.
All inputs are finite; a program needn't handle non-finite values. No bound on the sum of `included` on one device may be relied on, other than what follows from the above.
Results may differ from the reference program's by a relative error of at most 0.018.
Values may be sent and summed in bfloat16 or wider, within the bound.
A program may use at most 64 MiB of HBM per device.

```python
import math
import jax
import jax.numpy as jnp
from jax import lax

D = 8192
RANK = 128
ROWS = 32
USERS_DEV = 2
MICRO = 4
LAYERS = 8
USERS = 64
N_SECTION = 8
N_DP = 32


def draw_user_of_row(key, part):
    scores = jax.random.randint(key, (MICRO, N_DP, ROWS - 1), 0, 1 << 20)
    scores = scores * ROWS + jnp.arange(ROWS - 1, dtype=jnp.int32)[None, None, :]
    unused, picked = lax.top_k(scores, USERS_DEV - 1)
    cuts = picked + 1
    places = jnp.arange(ROWS, dtype=jnp.int32)
    local = jnp.sum((cuts[:, :, None, :] <= places[None, None, :, None]).astype(jnp.int32), -1)
    owners = local + (jnp.arange(N_DP, dtype=jnp.int32) * USERS_DEV)[None, :, None]
    return owners.reshape(MICRO, N_DP * ROWS).astype(jnp.int32)


def block_rows(key):
    noise_key, shared_key, weight_key = jax.random.split(key, 3)
    noise = jax.random.normal(noise_key, (MICRO, N_DP, ROWS, D), jnp.float32)
    shared = jax.random.normal(shared_key, (MICRO, N_DP, 1, D), jnp.float32)
    weight = jax.random.uniform(weight_key, (MICRO, N_DP, ROWS, 1), jnp.float32, 0.8, 1.2)
    values = jnp.clip(noise + weight * shared, -6.0, 6.0)
    return values.reshape(MICRO, N_DP * ROWS, D).astype(jnp.bfloat16)


def draw_hidden_in(key, part):
    return block_rows(jax.random.fold_in(key, 11))


def draw_cotangent(key, part):
    return block_rows(jax.random.fold_in(key, 23))


def touch_ends(array, key, least, largest):
    longest = array.shape.index(max(array.shape))
    spots = []
    for shift in (0, 1):
        where = [jax.random.randint(jax.random.fold_in(key, axis), (), 0, length) for axis, length in enumerate(array.shape)]
        where[longest] = (where[longest] + shift) % array.shape[longest]
        spots.append(tuple(where))
    return array.at[spots[0]].set(least).at[spots[1]].set(largest)


def shard_levels(own_key, dims, pieces, least, top_value):
    def one(axis_at, shards_of):
        heights = jax.random.uniform(jax.random.fold_in(jax.random.fold_in(own_key, 6), axis_at), (shards_of,), jnp.float32, least / len(pieces), top_value / len(pieces))
        return jnp.repeat(jnp.exp(heights), dims[axis_at] // shards_of).reshape((-1,) + (1,) * (len(dims) - axis_at - 1))

    level = one(*pieces[0])
    for cut in pieces[1:]:
        level = level * one(*cut)
    return level


def gaussian(rng, dims, scale, most, cuts=(), held_as=jnp.bfloat16):
    values = jax.random.normal(rng, dims, jnp.float32) * scale
    if len(cuts) > 0:
        values = shard_levels(rng, dims, cuts, -0.22, 0.18) * values
    return jnp.clip(values, min=-most, max=most).astype(held_as)


def setup_inputs(seed: int = 0) -> dict:
    keys = jax.random.split(jax.random.key(seed), 8)
    return {
        "hidden_in": draw_hidden_in(jax.random.fold_in(keys[7], 71), 0),
        "cotangent": draw_cotangent(jax.random.fold_in(keys[7], 71), 0),
        "adapter_in": gaussian(keys[2], (LAYERS, D, RANK), D ** -0.5, 0.0625, ((0, 8), (1, 32))),
        "adapter_out": gaussian(keys[3], (LAYERS, RANK, D), RANK ** -0.5, 0.5, ((0, 8), (2, 32))),
        "norm_gain": jnp.clip(1.0 + 0.1 * jax.random.normal(keys[4], (LAYERS, D), jnp.float32), 0.5, 1.5).astype(jnp.bfloat16),
        "user_of_row": draw_user_of_row(jax.random.fold_in(keys[7], 71), 0),
        "included": touch_ends((jax.random.randint(keys[6], (MICRO, USERS), 0, 4) < 3).astype(jnp.int32), jax.random.fold_in(keys[6], 1), 0, 1),
    }


def normalize(stream_in, gain):
    stream = stream_in.astype(jnp.float32)
    scale = lax.rsqrt(lax.optimization_barrier(jnp.mean(stream * stream, -1, keepdims=True)) + 1e-05)
    unit = stream * scale
    normed = (unit * gain.astype(jnp.float32)).astype(jnp.bfloat16)
    return (stream, scale, unit, normed)

def flatten(values):
    return values.reshape(-1, values.shape[-1])

def pair_products(values):
    blocks = values.reshape(MICRO * N_DP, ROWS, values.shape[-1]).astype(jnp.float32)
    return jnp.einsum('bik,bjk->bij', blocks, blocks)

def ghost(normed, err, low, delta, user_of_row, onehot):
    owners = user_of_row.reshape(MICRO * N_DP, ROWS)
    same = owners[:, :, None] == owners[:, None, :]
    pairs = pair_products(normed) * pair_products(err) + pair_products(low) * pair_products(delta)
    pairs = jnp.where(same, pairs, jnp.zeros_like(pairs))
    rowsum = lax.optimization_barrier(jnp.sum(pairs, -1)).reshape(MICRO, N_DP * ROWS)
    return jnp.einsum('mr,mru->mu', rowsum, onehot)

def reference(hidden_in, cotangent, adapter_in, adapter_out, norm_gain, user_of_row, included):
    shape3 = hidden_in.shape
    onehot = (user_of_row[:, :, None] == jnp.arange(N_DP * USERS_DEV, dtype=jnp.int32)[None, None, :]).astype(jnp.float32)
    saved = []
    current = hidden_in
    for layer in range(N_SECTION):
        stream, scale, unit, normed = normalize(current, norm_gain[layer])
        low = jnp.dot(flatten(normed), adapter_in[layer], preferred_element_type=jnp.float32).astype(jnp.bfloat16)
        upper = jnp.dot(low, adapter_out[layer], preferred_element_type=jnp.float32).reshape(shape3)
        saved.append((current, normed, low.reshape(MICRO, N_DP * ROWS, RANK)))
        current = (stream + upper).astype(jnp.bfloat16)
    delta = cotangent
    total = jnp.zeros((MICRO, N_DP * USERS_DEV), jnp.float32)
    backs = [None] * N_SECTION
    for layer in range(N_SECTION - 1, -1, -1):
        entering, normed, low = saved[layer]
        stream, scale, unit, unused = normalize(entering, norm_gain[layer])
        err = jnp.dot(flatten(delta), adapter_out[layer].T, preferred_element_type=jnp.float32).astype(jnp.bfloat16)
        back = jnp.dot(err, adapter_in[layer].T, preferred_element_type=jnp.float32).reshape(shape3)
        slope = back * norm_gain[layer].astype(jnp.float32)
        grad_h = scale * (slope - unit * lax.optimization_barrier(jnp.mean(slope * unit, -1, keepdims=True)))
        err = err.reshape(MICRO, N_DP * ROWS, RANK)
        total = total + ghost(normed, err, low, delta, user_of_row, onehot)
        backs[layer] = (err, delta)
        delta = (delta.astype(jnp.float32) + grad_h).astype(jnp.bfloat16)
    bound = 0.8 * math.sqrt(N_SECTION * (ROWS // USERS_DEV) * D * D)
    user_weights = included.astype(jnp.float32) * (bound / jnp.maximum(jnp.sqrt(total), bound))
    row_weight = jnp.einsum('mru,mu->mr', onehot, user_weights)[:, :, None]
    grads_in = []
    grads_out = []
    for layer in range(N_SECTION):
        entering, normed, low = saved[layer]
        err, delta_next = backs[layer]
        weighted_err = (row_weight * err.astype(jnp.float32)).astype(jnp.bfloat16)
        weighted_delta = (row_weight * delta_next.astype(jnp.float32)).astype(jnp.bfloat16)
        grads_in.append(jnp.dot(flatten(normed).T, flatten(weighted_err), preferred_element_type=jnp.float32))
        grads_out.append(jnp.dot(flatten(low).T, flatten(weighted_delta), preferred_element_type=jnp.float32))
    return (jnp.stack(grads_in), jnp.stack(grads_out), user_weights)
```

```python
import math

import jax
import jax.numpy as jnp
from jax import lax
from jax.sharding import Mesh
from jax.sharding import PartitionSpec as P

F32 = jnp.float32
BF = jnp.bfloat16


def mm(a, b, ca, cb):
    return lax.dot_general(a, b, (((ca,), (cb,)), ((), ())), preferred_element_type=F32)


def swap_route(n, m):
    return [(i * m + j, j * m + i) for i in range(n) for j in range(m)]


def recurrence(z0, y0, c0, norm0, gram, width):
    layers, rows, rank = z0.shape
    z = [z0[l] for l in range(layers)]
    y = [y0[l] for l in range(layers)]
    c = [c0[l] for l in range(layers)]
    square = norm0
    lows, rinvs, fulls, seen = [], [], [], []
    for l in range(layers):
        rinv = lax.rsqrt(square / width + 1e-05)
        full = z[l] * rinv
        low = full.astype(BF)
        seen.append(list(y))
        for j in range(layers):
            both = mm(low, gram[l, j], 1, 0)
            z[j] = z[j] + both[:, :rank]
            y[j] = y[j] + both[:, rank:]
        square = square + jnp.sum(low.astype(F32) * (seen[l][l] + y[l]), -1, keepdims=True)
        lows.append(low)
        rinvs.append(rinv)
        fulls.append(full)
    errs, cors = [None] * layers, [None] * layers
    for l in range(layers - 1, -1, -1):
        err = c[l].astype(BF)
        mean = jnp.sum(err.astype(F32) * fulls[l], -1, keepdims=True) / width
        cor = rinvs[l] * rinvs[l] * mean
        for j in range(l):
            c[j] = c[j] + rinvs[l] * mm(err, gram[j, l][:, :rank], 1, 1) - cor * seen[l][j]
        errs[l] = err
        cors[l] = cor
    return lows, errs, rinvs, cors


def shards(hidden_in, cotangent, adapter_in, adapter_out, norm_gain, user_of_row, included):
    n_s, n_z, n_x = (lax.axis_size(a) for a in ("section", "z", "x"))
    s, zi, xi = (lax.axis_index(a) for a in ("section", "z", "x"))
    plane = ("section", "x")
    layers = n_s
    micro, rows, width = hidden_in.shape
    cols, rank = adapter_in.shape[1:]
    users = included.shape[1]
    dev_rows = micro * rows
    group_rows = dev_rows * n_x
    own_rows = group_rows // (n_s * n_x)
    gain = norm_gain[0]
    a = adapter_in[0]
    bt = adapter_out[0].T
    g = (a.astype(F32) * gain.astype(F32)[:, None]).astype(BF)
    w = jnp.concatenate([jnp.concatenate([g, bt], 1), jnp.broadcast_to(gain[None], (16, cols))], 0)
    w = lax.ppermute(w, ("section", "z"), swap_route(n_s, n_z))
    w = lax.all_gather(w, "z")
    gains = w[:, cols].astype(F32)
    w = w[:, :cols]
    base = (zi * n_x + xi) * users
    key = ((user_of_row - base) + users * jnp.arange(micro, dtype=jnp.int32)[:, None]).reshape(dev_rows)
    onehot = (user_of_row - base)[:, :, None] == jnp.arange(users, dtype=jnp.int32)
    inc = jnp.sum(jnp.where(onehot, included[:, None, :], 0), -1).reshape(dev_rows)
    info = jnp.stack([key, inc]).astype(BF)
    info_all = lax.all_gather(info, "x")
    span = n_x * cols
    both = jnp.concatenate([hidden_in.reshape(dev_rows, width), cotangent.reshape(dev_rows, width)], 0)
    both = lax.dynamic_slice_in_dim(both, s * span, span, 1)
    both = jnp.moveaxis(both.reshape(2 * dev_rows, n_x, cols), 1, 0)
    both = lax.all_to_all(both, "x", 0, 0, tiled=True)
    x = both[:, :dev_rows].reshape(group_rows, cols)
    cot = both[:, dev_rows:].reshape(group_rows, cols)
    own = lax.dynamic_index_in_dim(w, zi, 0, keepdims=False)[:, rank:]
    zy = jnp.stack([mm(x, w[l], 1, 0) for l in range(layers)])
    ct = jnp.stack([mm(cot, w[l][:, rank:], 1, 0) for l in range(layers)])
    proj = jnp.concatenate([zy, ct], -1).astype(BF)
    gram = jnp.stack([mm(own, w[l], 0, 0) for l in range(layers)]).astype(BF)
    n_plane = n_s * n_x
    proj = jnp.moveaxis(proj.reshape(layers, n_plane, own_rows, 3 * rank), 1, 0)
    gram = gram.reshape(n_plane, rank // n_x, 2 * rank)
    xf = x.astype(F32)
    norm0 = jnp.sum(xf * xf, -1).reshape(n_plane, own_rows, 1)
    proj = jnp.sum(lax.all_to_all(proj, plane, 0, 0, tiled=True).astype(F32), 0)
    gram = jnp.sum(lax.all_to_all(gram, plane, 0, 0, tiled=True).astype(F32), 0).astype(BF)
    norm0 = jnp.sum(lax.all_to_all(norm0, plane, 0, 0, tiled=True), 0)
    gram = lax.all_gather(gram, ("z", "section", "x"))
    gram = gram.reshape(layers, layers, rank, 2 * rank)
    lows, errs, rinvs, cors = recurrence(
        proj[..., :rank], proj[..., rank : 2 * rank], proj[..., 2 * rank :], norm0, gram, width
    )
    pack = jnp.stack(lows + errs)
    scal = jnp.concatenate(rinvs + cors, 1)
    pack = lax.all_gather(pack, plane, axis=1, tiled=True)
    scal = lax.all_gather(scal, plane, axis=0, tiled=True)
    low, err = pack[:layers], pack[layers:]
    h = x.astype(F32)
    normed = []
    hs = []
    for l in range(layers):
        hs.append(h.astype(BF))
        normed.append((h * scal[:, l : l + 1] * gains[l][None]).astype(BF))
        h = h + mm(low[l], w[l][:, rank:], 1, 1)
    delta = cot.astype(F32)
    deltas = [None] * layers
    for l in range(layers - 1, -1, -1):
        deltas[l] = delta.astype(BF)
        delta = (
            delta
            + scal[:, l : l + 1] * mm(err[l], w[l][:, :rank], 1, 1)
            - scal[:, layers + l : layers + l + 1] * hs[l].astype(F32)
        )
    totals = []
    for i in range(n_x):
        at = slice(i * dev_rows, (i + 1) * dev_rows)
        keys = info_all[i, 0]
        same = keys[:, None] == keys[None, :]
        pairs = 0.0
        for l in range(layers):
            n, e, lo, d = normed[l][at], err[l][at], low[l][at], deltas[l][at]
            pairs = pairs + mm(n, n, 1, 1) * mm(e, e, 1, 1) + mm(lo, lo, 1, 1) * mm(d, d, 1, 1)
        rowsum = jnp.sum(jnp.where(same, pairs, 0.0), -1)
        totals.append(jnp.sum(jnp.where(same, rowsum[None, :], 0.0), -1))
    totals = lax.psum(jnp.stack(totals), plane)
    bound = 0.8 * math.sqrt(layers * (rows // users) * width * width)
    row_w = info_all[:, 1].astype(F32) * (bound / jnp.maximum(jnp.sqrt(totals), bound))
    mine = lax.dynamic_index_in_dim(row_w, xi, 0, keepdims=False).reshape(micro, rows)
    user_weights = jnp.max(jnp.where(onehot, mine[:, :, None], 0.0), 1)
    row_w = row_w.reshape(group_rows, 1)
    grads = []
    for l in range(layers):
        we = (row_w * err[l].astype(F32)).astype(BF)
        wl = (row_w * low[l].astype(F32)).astype(BF)
        grads.append(jnp.concatenate([mm(normed[l], we, 0, 0), mm(deltas[l], wl, 0, 0)], 1))
    grads = jnp.stack(grads).astype(BF)
    grads = jnp.sum(lax.all_to_all(grads, "z", 0, 0, tiled=True).astype(F32), 0)
    grads = lax.ppermute(grads, ("section", "z"), swap_route(n_s, n_z))
    return (grads[None, :, :rank], grads[:, rank:].T[None], user_weights)


def solution(mesh):
    torus = Mesh(mesh.devices.reshape(mesh.shape["section"], 8, 4), ("section", "z", "x"))
    dp = ("z", "x")
    return jax.shard_map(
        shards,
        mesh=torus,
        in_specs=(
            P(None, dp, None),
            P(None, dp, None),
            P("section", dp, None),
            P("section", None, dp),
            P("section", dp),
            P(None, dp),
            P(None, dp),
        ),
        out_specs=(P("section", dp, None), P("section", None, dp), P(None, dp)),
        check_vma=False,
    )
```

```python
import functools
import math

import jax
import jax.numpy as jnp
from jax import lax
from jax.experimental import pallas as pl
from jax.experimental.pallas import tpu as pltpu
from jax.sharding import Mesh
from jax.sharding import PartitionSpec as P

F32 = jnp.float32
BF = jnp.bfloat16
MESH = pl.DeviceIdType.MESH
VMEM = pl.BlockSpec(memory_space=pltpu.VMEM)
ANY = pl.BlockSpec(memory_space=pl.ANY)
LIMIT = 60 * 1024 * 1024


def mm(a, b, ca, cb):
    return lax.dot_general(a, b, (((ca,), (cb,)), ((), ())), preferred_element_type=F32)


def loop(n, body):
    lax.fori_loop(0, n, lambda i, c: (body(i), c)[1], 0)


def remote(src, dst, send, recv, device):
    return pltpu.make_async_remote_copy(
        src_ref=src, dst_ref=dst, send_sem=send, recv_sem=recv, device_id=device, device_id_type=MESH
    )


def params(cid):
    return pltpu.CompilerParams(collective_id=cid, has_side_effects=True, vmem_limit_bytes=LIMIT)


def where_am_i():
    return tuple(lax.axis_index(a) for a in ("section", "z", "x"))


def exchange_kernel(sizes, w_ref, act_ref, w_all, act_all, ws, wr, asend, arecv, lsem):
    n_s, n_z, n_x = sizes
    s, z, x = where_am_i()
    barrier = pltpu.get_barrier_semaphore()
    diag = s == z

    def greet(k):
        @pl.when(jnp.logical_not(jnp.logical_and(k == z, diag)))
        def _():
            pl.semaphore_signal(barrier, inc=1, device_id=(z, k, x), device_id_type=MESH)
            pl.semaphore_signal(barrier, inc=1, device_id=(k, s, x), device_id_type=MESH)

    loop(n_z, greet)
    for k in range(1, n_x):
        pl.semaphore_signal(
            barrier, inc=1, device_id=(s, z, lax.rem(x + k, n_x)), device_id_type=MESH
        )
    pl.semaphore_wait(barrier, 2 * n_z + n_x - 1 - jnp.where(diag, 2, 0))

    def w_copy(to, slot):
        return remote(w_ref, w_all.at[slot], ws.at[to], wr.at[slot], (z, to, x))

    def a_copy(to, slot):
        return remote(act_ref.at[to], act_all.at[slot], asend.at[to], arecv.at[slot], (s, z, to))

    def each(n, skip, fn):
        def body(k):
            @pl.when(jnp.logical_not(skip(k)))
            def _():
                fn(k)

        loop(n, body)

    def is_me(k):
        return jnp.logical_and(k == z, diag)

    def from_me(k):
        return jnp.logical_and(k == s, diag)

    each(n_z, is_me, lambda k: w_copy(k, s).start())
    each(n_x, lambda k: k == x, lambda k: a_copy(k, x).start())
    own = pltpu.make_async_copy(act_ref.at[x], act_all.at[x], lsem.at[0])
    own.start()

    @pl.when(diag)
    def _():
        mine = pltpu.make_async_copy(w_ref, w_all.at[s], lsem.at[1])
        mine.start()
        mine.wait()

    own.wait()
    each(n_x, lambda k: k == x, lambda k: a_copy(k, k).wait_recv())
    each(n_s, from_me, lambda k: w_copy(lax.rem(z + 1, n_z), k).wait_recv())
    each(n_x, lambda k: k == x, lambda k: a_copy(k, x).wait_send())
    each(n_z, is_me, lambda k: w_copy(k, s).wait_send())


def exchange(sizes, w, act):
    n_s, n_z, n_x = sizes
    dma = pltpu.SemaphoreType.DMA
    return pl.pallas_call(
        functools.partial(exchange_kernel, sizes),
        out_shape=(
            jax.ShapeDtypeStruct((n_s, *w.shape), w.dtype),
            jax.ShapeDtypeStruct(act.shape, act.dtype),
        ),
        in_specs=[ANY, ANY],
        out_specs=(ANY, ANY),
        scratch_shapes=[dma((n_z,)), dma((n_s,)), dma((n_x,)), dma((n_x,)), dma((2,))],
        compiler_params=params(0),
        name="exchange",
    )(w, act)


class Plane:
    def __init__(self, sizes):
        n_s, n_z, n_x = sizes
        self.n_x = n_x
        self.chips = (n_s // 2) * n_x
        self.s, self.z, self.x = where_am_i()
        self.core = lax.rem(self.s, 2)
        self.chip = (self.s // 2) * n_x + self.x
        self.partner = (self.s + 1 - 2 * self.core, self.z, self.x)

    def peer(self, chip):
        return (2 * (chip // self.n_x) + self.core, self.z, lax.rem(chip, self.n_x))

    def ahead(self, k):
        return lax.rem(self.chip + k, self.chips)

    def behind(self, k):
        return lax.rem(self.chip + self.chips - k, self.chips)

    def others(self, fn):
        loop(self.chips - 1, lambda k: fn(k + 1))

    def greet_all(self, barrier):
        def one(chip):
            s2, z2, x2 = self.peer(chip)
            pl.semaphore_signal(barrier, inc=1, device_id=(s2, z2, x2), device_id_type=MESH)
            pl.semaphore_signal(
                barrier, inc=1, device_id=(s2 + 1 - 2 * self.core, z2, x2), device_id_type=MESH
            )

        self.others(lambda k: one(self.ahead(k)))
        pl.semaphore_signal(barrier, inc=1, device_id=self.partner, device_id_type=MESH)
        return 2 * self.chips - 1


class Cast:
    def __init__(self, plane, view, sems):
        self.p, self.view, self.sems = plane, view, sems

    def far(self, chip, owner):
        send, recv = self.sems[0].at[chip], self.sems[1].at[owner]
        ref = self.view(owner, self.p.core)
        return remote(ref, ref, send, recv, self.p.peer(chip))

    def near(self, chip, core):
        ref = self.view(chip, core)
        return remote(ref, ref, self.sems[2].at[chip], self.sems[3].at[chip], self.p.partner)

    def start(self):
        p = self.p
        p.others(lambda k: self.far(p.ahead(k), p.chip).start())
        self.near(p.chip, p.core).start()

    def relay(self):
        p = self.p

        def one(k):
            chip = p.behind(k)
            self.far(chip, chip).wait_recv()
            self.near(chip, p.core).start()

        p.others(one)

    def finish(self):
        p = self.p
        loop(p.chips, lambda i: self.near(i, 1 - p.core).wait_recv())
        loop(p.chips, lambda i: self.near(i, p.core).wait_send())
        p.others(lambda k: self.far(p.ahead(k), p.chip).wait_send())


def solve_kernel(
    sizes, dims, w_all, act_all, low_out, err_out,
    gsend, grecv, gz, gram, pbuf, prev, psum, crev, state, snap, full, rin,
    gs, gr, zs, zr, ps, pr, cs, cr, m0, m1, m2, m3, l0, l1, l2, l3, e0, e1, e2, e3,
):
    n_s, n_z, n_x = sizes
    rows, cols, rank, width = dims
    layers = n_s
    own = rows // n_s
    part = rank // n_x
    p = Plane(sizes)
    barrier = pltpu.get_barrier_semaphore()
    count = p.greet_all(barrier)
    for k in range(1, n_z):
        pl.semaphore_signal(
            barrier, inc=1, device_id=(p.s, lax.rem(p.z + k, n_z), p.x), device_id_type=MESH
        )
    mine = w_all[p.z, :cols, rank:]
    for l in range(layers):
        g = mm(mine, w_all[l, :cols], 0, 0).astype(BF)
        gsend[l] = g.reshape(n_x, part, 2 * rank)
    pl.semaphore_wait(barrier, count + n_z - 1)
    n_plane = 2 * p.chips
    me = p.s * n_x + p.x

    def g_copy(to, slot):
        return remote(
            gsend.at[to // n_x, lax.rem(to, n_x)], grecv.at[slot], gs.at[to], gr.at[slot],
            (to // n_x, p.z, lax.rem(to, n_x)),
        )

    loop(n_plane - 1, lambda k: g_copy(lax.rem(me + 1 + k, n_plane), me).start())
    for l in range(layers):
        for i in range(n_x):
            zy = mm(act_all[i, :rows], w_all[l, :cols], 1, 0).astype(BF)
            ct = mm(act_all[i, rows : 2 * rows], w_all[l, :cols, rank:], 1, 0).astype(BF)
            at = slice(i * n_s, (i + 1) * n_s)
            for c, value in enumerate((zy[:, :rank], zy[:, rank:], ct)):
                r0 = (c * layers + l) * own
                pbuf[at, r0 : r0 + own, :] = value.reshape(n_s, own, rank)
    for i in range(n_x):
        xf = act_all[i, :rows].astype(F32)
        sq = jnp.broadcast_to(jnp.sum(xf * xf, -1, keepdims=True), (rows, rank)).astype(BF)
        pbuf[i * n_s : (i + 1) * n_s, 3 * layers * own :, :] = sq.reshape(n_s, own, rank)

    def block(chip, core):
        return (2 * (chip // n_x) + core) * n_x + lax.rem(chip, n_x)

    def pre(i):
        return remote(pbuf.at[block(i, 1 - p.core)], prev.at[i], ps.at[i], pr.at[i], p.partner)

    def pre_wait(i):
        return remote(pbuf.at[block(i, p.core)], prev.at[i], ps.at[i], pr.at[i], p.partner)

    def c_copy(to, slot):
        return remote(psum.at[to], crev.at[slot], cs.at[to], cr.at[slot], p.peer(to))

    loop(p.chips, lambda k: pre(p.ahead(k)).start())

    loop(n_plane - 1, lambda k: g_copy(me, lax.rem(me + n_plane - 1 - k, n_plane)).wait_recv())
    grecv[me] = gsend[p.s, p.x]
    gsum = grecv[0].astype(F32)
    for k in range(1, n_plane):
        gsum = gsum + grecv[k].astype(F32)
    gz[...] = gsum.astype(BF)

    def z_copy(to, slot):
        return remote(
            gz, gram.at[p.s, p.x, slot], zs.at[to], zr.at[slot], (p.s, to, p.x)
        )

    loop(n_z - 1, lambda k: z_copy(lax.rem(p.z + 1 + k, n_z), p.z).start())
    gram[p.s, p.x, p.z] = gz[...]

    def forward(k):
        i = p.ahead(k)
        pre_wait(i).wait_recv()
        total = pbuf[block(i, p.core)].astype(F32) + prev[i].astype(F32)
        psum[i] = total.astype(BF)

        @pl.when(i != p.chip)
        def _():
            c_copy(i, p.chip).start()

    loop(p.chips, lambda k: forward(lax.rem(k + 1, p.chips)))

    loop(n_z - 1, lambda k: z_copy(p.z, lax.rem(p.z + n_z - 1 - k, n_z)).wait_recv())

    def gram_view(chip, core):
        return gram.at[2 * (chip // n_x) + core, lax.rem(chip, n_x)]

    spread = Cast(p, gram_view, (m0, m1, m2, m3))
    spread.start()
    p.others(lambda k: c_copy(p.chip, p.behind(k)).wait_recv())
    total = psum[p.chip].astype(F32)

    crev[p.chip] = psum[p.chip]
    total = crev[0].astype(F32)
    for k in range(1, p.chips):
        total = total + crev[k].astype(F32)
    state[...] = total.reshape(3 * layers + 1, own, rank)
    spread.relay()
    spread.finish()

    def low_view(chip, core):
        dev = block(chip, core)
        return low_out.at[:, pl.ds(pl.multiple_of(dev * own, own), own), :]

    def err_view(chip, core):
        dev = block(chip, core)
        return err_out.at[:, pl.ds(pl.multiple_of(dev * own, own), own), :]

    here = pl.ds(pl.multiple_of(me * own, own), own)
    square = state[3 * layers]
    zero = jnp.zeros((own, rank), F32)
    lane = lax.broadcasted_iota(jnp.int32, (own, rank), 1)
    scal = zero
    for l in range(layers):
        rinv = lax.rsqrt(square / width + 1e-05)
        u = state[l] * rinv
        low = u.astype(BF)
        full[l] = u
        rin[l] = rinv
        low_out[l, here, :] = low
        before = state[layers + l]
        for j in range(layers):
            snap[l, j] = state[layers + j]
            if j > l:
                both = mm(low, gram[j, :, l].reshape(rank, 2 * rank), 1, 0)
                state[j] = state[j] + both[:, :rank]
                state[layers + j] = state[layers + j] + both[:, rank:]
            else:
                one = mm(low, gram[j, :, l, :, rank:].reshape(rank, rank), 1, 0)
                state[layers + j] = state[layers + j] + one
        after = state[layers + l]
        square = square + jnp.sum(low.astype(F32) * (before + after), -1, keepdims=True)
        high = rinv.astype(BF).astype(F32)
        scal = jnp.where(lane == l, high, scal)
        scal = jnp.where(lane == layers + l, rinv - high, scal)
    lows = Cast(p, low_view, (l0, l1, l2, l3))
    lows.start()
    for l in range(layers - 1, -1, -1):
        err = state[2 * layers + l].astype(BF)
        mean = jnp.sum(err.astype(F32) * full[l], -1, keepdims=True) / width
        rinv = rin[l]
        cor = rinv * rinv * mean
        for j in range(l):
            back = mm(err, gram[l, :, j, :, :rank].reshape(rank, rank), 1, 1)
            state[2 * layers + j] = state[2 * layers + j] + rinv * back - cor * snap[l, j]
        err_out[l, here, :] = err
        scal = jnp.where(lane == 2 * layers + l, cor, scal)
    err_out[layers, here, :] = scal.astype(BF)
    errs = Cast(p, err_view, (e0, e1, e2, e3))
    errs.start()
    lows.relay()
    errs.relay()
    lows.finish()
    errs.finish()
    loop(n_plane - 1, lambda k: g_copy(lax.rem(me + 1 + k, n_plane), me).wait_send())
    loop(n_z - 1, lambda k: z_copy(lax.rem(p.z + 1 + k, n_z), p.z).wait_send())
    loop(p.chips, lambda k: pre(p.ahead(k)).wait_send())
    p.others(lambda k: c_copy(p.ahead(k), p.chip).wait_send())


def solve(sizes, dims, w_all, act_all):
    n_s, n_z, n_x = sizes
    rows, cols, rank, width = dims
    layers = n_s
    chips = (n_s // 2) * n_x
    plane = n_s * n_x
    own = rows // n_s
    group = rows * n_x
    part = rank // n_x
    high = (3 * layers + 1) * own
    dma = pltpu.SemaphoreType.DMA
    v = pltpu.VMEM
    return pl.pallas_call(
        functools.partial(solve_kernel, sizes, dims),
        out_shape=(
            jax.ShapeDtypeStruct((layers, group, rank), BF),
            jax.ShapeDtypeStruct((layers + 1, group, rank), BF),
        ),
        in_specs=[VMEM, VMEM],
        out_specs=(VMEM, VMEM),
        scratch_shapes=[
            v((n_s, n_x, part, 2 * rank), BF),
            v((plane, part, 2 * rank), BF),
            v((part, 2 * rank), BF),
            v((n_s, n_x, n_z, part, 2 * rank), BF),
            v((plane, high, rank), BF),
            v((chips, high, rank), BF),
            v((chips, high, rank), BF),
            v((chips, high, rank), BF),
            v((3 * layers + 1, own, rank), F32),
            v((layers, layers, own, rank), F32),
            v((layers, own, rank), F32),
            v((layers, own, rank), F32),
            dma((plane,)), dma((plane,)), dma((n_z,)), dma((n_z,)),
        ]
        + [dma((chips,))] * 16,
        compiler_params=params(1),
        name="solve",
    )(w_all, act_all)


def finish_kernel(
    sizes, dims, bound, w_all, act_all, low_ref, err_ref, gi_out, go_out, uw_out,
    normed, deltas, hold, tot, gbuf, grecv, ts, tr, gs, gr, lsem,
):
    n_s, n_z, n_x = sizes
    rows, cols, rank, width, users = dims
    layers = n_s
    p = Plane(sizes)
    s, z, x = p.s, p.z, p.x
    barrier = pltpu.get_barrier_semaphore()
    count = p.greet_all(barrier)
    to_me = jnp.logical_and(s == z, True)

    def greet(k):
        @pl.when(jnp.logical_not(jnp.logical_and(to_me, k == s)))
        def _():
            pl.semaphore_signal(barrier, inc=1, device_id=(k, s, x), device_id_type=MESH)
            pl.semaphore_signal(barrier, inc=1, device_id=(z, k, x), device_id_type=MESH)

    loop(n_s, greet)
    count = count + 2 * n_s - jnp.where(to_me, 2, 0)

    sums = []
    for i in range(n_x):
        at = slice(i * rows, (i + 1) * rows)
        keyrow = act_all[i, 2 * rows : 2 * rows + 8].astype(F32)[0:1, :rows]
        keys = jnp.broadcast_to(keyrow, (rows, rows))
        same = keys == keys.T
        scal = err_ref[layers, at].astype(F32)
        h = act_all[i, :rows].astype(F32)
        pairs = jnp.zeros((rows, rows), F32)
        for l in range(layers):
            gain = w_all[l, cols : cols + 8].astype(F32)[0:1, :]
            rinv = scal[:, l : l + 1] + scal[:, layers + l : layers + l + 1]
            n = (h * rinv * gain).astype(BF)
            e = err_ref[l, at]
            normed[l, at] = n
            hold[l] = h.astype(BF)
            pairs = pairs + mm(n, n, 1, 1) * mm(e, e, 1, 1)
            if l + 1 < layers:
                h = h + mm(low_ref[l, at], w_all[l, :cols, rank:], 1, 1)
        d = act_all[i, rows : 2 * rows].astype(F32)
        for l in range(layers - 1, -1, -1):
            db = d.astype(BF)
            deltas[l, at] = db
            lo = low_ref[l, at]
            pairs = pairs + mm(lo, lo, 1, 1) * mm(db, db, 1, 1)
            if l > 0:
                rinv = scal[:, l : l + 1] + scal[:, layers + l : layers + l + 1]
                cor = scal[:, 2 * layers + l : 2 * layers + l + 1]
                d = d + rinv * mm(err_ref[l, at], w_all[l, :cols, :rank], 1, 1)
                d = d - cor * hold[l].astype(F32)
        pairs = jnp.where(same, pairs, 0.0)
        rowsum = jnp.broadcast_to(jnp.sum(pairs, -1, keepdims=True), (rows, rows))
        sums.append(jnp.sum(jnp.where(same, rowsum, 0.0), 0, keepdims=True))
    me = s * n_x + x
    n_plane = n_s * n_x
    pad = [jnp.zeros((8 - n_x, rows), F32)] if n_x < 8 else []
    tot[me] = jnp.concatenate(sums + pad, 0)
    pl.semaphore_wait(barrier, count)

    def t_copy(to, slot):
        return remote(
            tot.at[slot], tot.at[slot], ts.at[to], tr.at[slot], (to // n_x, z, lax.rem(to, n_x))
        )

    loop(n_plane - 1, lambda k: t_copy(lax.rem(me + 1 + k, n_plane), me).start())
    loop(n_plane - 1, lambda k: t_copy(me, lax.rem(me + n_plane - 1 - k, n_plane)).wait_recv())
    total = tot[0]
    for k in range(1, n_plane):
        total = total + tot[k]
    clip = bound / jnp.maximum(jnp.sqrt(total), bound)

    weights = []
    for i in range(n_x):
        inc = act_all[i, 2 * rows : 2 * rows + 8].astype(F32)[1:2, :rows]
        w = jnp.broadcast_to(inc * clip[i : i + 1], (rows, rows))
        weights.append(w.T[:, :rank])

        @pl.when(x == i)
        def _(w=w, i=i):
            keyrow = act_all[i, 2 * rows : 2 * rows + 8].astype(F32)[0:1, :rows]
            which = lax.broadcasted_iota(jnp.int32, (users, rows), 0).astype(F32)
            mine = jnp.where(which == keyrow, w[:users], 0.0)
            uw_out[...] = jnp.broadcast_to(jnp.max(mine, -1, keepdims=True), (users, rows))

    weight = jnp.concatenate(weights, 0)

    def g_copy(to, slot):
        return remote(gbuf.at[to], grecv.at[slot], gs.at[to], gr.at[slot], (to, s, x))

    for l in range(layers):
        we = (weight * err_ref[l].astype(F32)).astype(BF)
        wl = (weight * low_ref[l].astype(F32)).astype(BF)
        gbuf[l, :, :rank] = mm(normed[l], we, 0, 0).astype(BF)
        gbuf[l, :, rank:] = mm(deltas[l], wl, 0, 0).astype(BF)

        @pl.when(jnp.logical_not(jnp.logical_and(to_me, s == l)))
        def _(l=l):
            g_copy(l, z).start()

    @pl.when(to_me)
    def _():
        mine = pltpu.make_async_copy(gbuf.at[s], grecv.at[z], lsem.at[0])
        mine.start()
        mine.wait()

    def others(fn):
        def body(k):
            @pl.when(jnp.logical_not(jnp.logical_and(to_me, k == s)))
            def _():
                fn(k)

        loop(n_s, body)

    others(lambda k: g_copy(lax.rem(s + 1, n_s), k).wait_recv())
    grad = grecv[0].astype(F32)
    for k in range(1, n_z):
        grad = grad + grecv[k].astype(F32)
    gi_out[...] = grad[:, :rank]
    go_out[...] = grad[:, rank:].T
    others(lambda k: g_copy(k, z).wait_send())
    loop(n_plane - 1, lambda k: t_copy(lax.rem(me + 1 + k, n_plane), me).wait_send())


def finish(sizes, dims, bound, w_all, act_all, low, err):
    n_s, n_z, n_x = sizes
    rows, cols, rank, width, users = dims
    layers = n_s
    plane = n_s * n_x
    dma = pltpu.SemaphoreType.DMA
    v = pltpu.VMEM
    return pl.pallas_call(
        functools.partial(finish_kernel, sizes, dims, bound),
        out_shape=(
            jax.ShapeDtypeStruct((cols, rank), F32),
            jax.ShapeDtypeStruct((rank, cols), F32),
            jax.ShapeDtypeStruct((users, rows), F32),
        ),
        in_specs=[VMEM] * 4,
        out_specs=(VMEM,) * 3,
        scratch_shapes=[
            v((layers, rows * n_x, cols), BF),
            v((layers, rows * n_x, cols), BF),
            v((layers, rows, cols), BF),
            v((plane, 8, rows), F32),
            v((layers, cols, 2 * rank), BF),
            v((n_z, cols, 2 * rank), BF),
            dma((plane,)), dma((plane,)), dma((n_s,)), dma((n_z,)), dma((1,)),
        ],
        compiler_params=params(2),
        name="finish",
    )(w_all, act_all, low, err)


def shards(hidden_in, cotangent, adapter_in, adapter_out, norm_gain, user_of_row, included):
    sizes = tuple(lax.axis_size(a) for a in ("section", "z", "x"))
    n_s, n_z, n_x = sizes
    s, zi, xi = where_am_i()
    micro, rows, width = hidden_in.shape
    cols, rank = adapter_in.shape[1:]
    users = included.shape[1]
    dev_rows = micro * rows
    a = adapter_in[0]
    g = (a.astype(F32) * norm_gain[0].astype(F32)[:, None]).astype(BF)
    w = jnp.concatenate([g, adapter_out[0].T], 1)
    w = jnp.concatenate([w, jnp.broadcast_to(norm_gain, (16, cols))], 0)
    base = (zi * n_x + xi) * users
    local = user_of_row - base
    key = (local + users * jnp.arange(micro, dtype=jnp.int32)[:, None]).reshape(1, dev_rows)
    onehot = local[:, :, None] == jnp.arange(users, dtype=jnp.int32)
    inc = jnp.sum(jnp.where(onehot, included[:, None, :], 0), -1).reshape(1, dev_rows)
    info = jnp.pad(jnp.concatenate([key, inc], 0).astype(BF), ((0, 14), (0, cols - dev_rows)))
    span = n_x * cols

    def slab(array):
        flat = lax.dynamic_slice_in_dim(array.reshape(dev_rows, width), s * span, span, 1)
        return jnp.moveaxis(flat.reshape(dev_rows, n_x, cols), 1, 0)

    act = jnp.concatenate(
        [slab(hidden_in), slab(cotangent), jnp.broadcast_to(info, (n_x, 16, cols))], 1
    )
    w_all, act_all = exchange(sizes, w, act)
    low, err = solve(sizes, (dev_rows, cols, rank, width), w_all, act_all)
    bound = 0.8 * math.sqrt(n_s * (rows // users) * width * width)
    gi, go, uw = finish(
        sizes, (dev_rows, cols, rank, width, micro * users), bound, w_all, act_all, low, err
    )
    return (gi[None], go[None], uw[:, 0].reshape(micro, users))


def build(torus):
    dp = ("z", "x")
    return jax.shard_map(
        shards,
        mesh=torus,
        in_specs=(
            P(None, dp, None),
            P(None, dp, None),
            P("section", dp, None),
            P("section", None, dp),
            P("section", dp),
            P(None, dp),
            P(None, dp),
        ),
        out_specs=(P("section", dp, None), P("section", None, dp), P(None, dp)),
        check_vma=False,
    )


def solution(mesh):
    return build(Mesh(mesh.devices.reshape(mesh.shape["section"], 8, 4), ("section", "z", "x")))
```

```python
import functools
import math

import jax
import jax.numpy as jnp
from jax import lax
from jax.experimental import pallas as pl
from jax.experimental.pallas import tpu as pltpu
from jax.sharding import Mesh
from jax.sharding import PartitionSpec as P

F32 = jnp.float32
BF = jnp.bfloat16
MESH = pl.DeviceIdType.MESH
VMEM = pl.BlockSpec(memory_space=pltpu.VMEM)
ANY = pl.BlockSpec(memory_space=pl.ANY)
LIMIT = 60 * 1024 * 1024


def mm(a, b, ca, cb):
    return lax.dot_general(a, b, (((ca,), (cb,)), ((), ())), preferred_element_type=F32)


def loop(n, body):
    lax.fori_loop(0, n, lambda i, c: (body(i), c)[1], 0)


def remote(src, dst, send, recv, device):
    return pltpu.make_async_remote_copy(
        src_ref=src, dst_ref=dst, send_sem=send, recv_sem=recv, device_id=device, device_id_type=MESH
    )


def params(cid):
    return pltpu.CompilerParams(collective_id=cid, has_side_effects=True, vmem_limit_bytes=LIMIT)


def where_am_i():
    return tuple(lax.axis_index(a) for a in ("section", "z", "x"))


class Ring:
    def __init__(self, n, me, place, view, pieces, sems):
        self.n, self.me, self.place, self.view, self.pieces, self.sems = n, me, place, view, pieces, sems
        self.steps = (n // 2, n - 1 - n // 2)

    def copy(self, way, step, piece, from_me):
        n, me = self.n, self.me
        sign = 1 - 2 * way
        block = (me - sign * step) if from_me else (me - sign * (step + 1))
        ref = self.view(lax.rem(block + 2 * n, n), piece)
        send, recv = self.sems[2 * way].at[step, piece], self.sems[2 * way + 1].at[step, piece]
        return remote(ref, ref, send, recv, self.place(lax.rem(me + sign + n, n)))

    def start(self):
        for piece in range(self.pieces):
            for way in (0, 1):
                self.copy(way, 0, piece, True).start()

    def run(self, arrived):
        for step in range(self.steps[0]):
            for piece in range(self.pieces):
                for way in (0, 1):
                    if step < self.steps[way]:
                        self.copy(way, step, piece, False).wait_recv()
                        if step + 1 < self.steps[way]:
                            self.copy(way, step + 1, piece, True).start()
                        sign = 1 - 2 * way
                        block = lax.rem(self.me - sign * (step + 1) + 2 * self.n, self.n)
                        arrived(block, piece)

    def finish(self):
        for way in (0, 1):
            for step in range(self.steps[way]):
                for piece in range(self.pieces):
                    self.copy(way, step, piece, True).wait_send()


def exchange_kernel(
    sizes, a_ref, b_ref, g_ref, hid_ref, cot_ref, info_ref, w_all, h_all, c_all, i_all,
    column, rs, rr, ls, lr, ys, yr, asend, arecv, lsem,
):
    n_s, n_z, n_x = sizes
    s, z, x = where_am_i()
    cols, rank = a_ref.shape
    barrier = pltpu.get_barrier_semaphore()
    for k in range(1, n_s):
        pl.semaphore_signal(
            barrier, inc=1, device_id=(lax.rem(s + k, n_s), z, x), device_id_type=MESH
        )
    for k in (1, n_z - 1):
        pl.semaphore_signal(
            barrier, inc=1, device_id=(s, lax.rem(z + k, n_z), x), device_id_type=MESH
        )
    for k in range(1, n_x):
        pl.semaphore_signal(
            barrier, inc=1, device_id=(s, z, lax.rem(x + k, n_x)), device_id_type=MESH
        )
    gain = jnp.broadcast_to(g_ref[...].astype(F32), (rank, cols))
    column[z, :cols, :rank] = (a_ref[...].astype(F32) * gain.T).astype(BF)
    column[z, :cols, rank:] = b_ref[...].astype(F32).T.astype(BF)
    column[z, cols:, :] = jnp.broadcast_to(g_ref[...].astype(F32), (16, cols)).astype(BF)
    pl.semaphore_wait(barrier, n_s - 1 + 2 + n_x - 1)

    def act(which, to, slot):
        at = pl.ds(pl.multiple_of((s * n_x + to) * cols, cols), cols)
        src = (hid_ref.at[:, :, at], cot_ref.at[:, :, at], info_ref)[which]
        dst = (h_all, c_all, i_all)[which].at[slot]
        return src, dst

    def a_copy(which, to, slot):
        src, dst = act(which, to, slot)
        return remote(src, dst, asend.at[which, to], arecv.at[which, slot], (s, z, to))

    split = cols // 2

    def view(block, piece):
        return column.at[block, :split] if piece == 0 else column.at[block, split:]

    ring = Ring(n_z, z, lambda to: (s, to, x), view, 2, (rs, rr, ls, lr))
    ring.start()
    for which in range(3):
        for k in range(1, n_x):
            a_copy(which, lax.rem(x + k, n_x), x).start()
    for which in range(3):
        src, dst = act(which, x, x)
        pltpu.make_async_copy(src, dst, lsem.at[which]).start()

    def y_copy(block, slot):
        return remote(column.at[block], w_all.at[slot], ys.at[block], yr.at[slot], (block, z, x))

    def keep():
        return pltpu.make_async_copy(column.at[s], w_all.at[s], lsem.at[3])

    def onward(block):
        @pl.when(block == s)
        def _():
            keep().start()

        @pl.when(block != s)
        def _():
            y_copy(block, s).start()

    onward(z)

    def arrived(block, piece):
        if piece == 1:
            onward(block)

    ring.run(arrived)
    for which in range(3):
        src, dst = act(which, x, x)
        pltpu.make_async_copy(src, dst, lsem.at[which]).wait()
        for k in range(1, n_x):
            a_copy(which, x, lax.rem(x + n_x - k, n_x)).wait_recv()
    keep().wait()

    def not_me(fn):
        def body(k):
            fn(lax.rem(s + 1 + k, n_s))

        loop(n_s - 1, body)

    not_me(lambda k: y_copy(s, k).wait_recv())
    not_me(lambda k: y_copy(k, s).wait_send())
    for which in range(3):
        for k in range(1, n_x):
            a_copy(which, lax.rem(x + k, n_x), x).wait_send()
    ring.finish()


def exchange(sizes, a, b, g, hidden, cot, info):
    n_s, n_z, n_x = sizes
    cols, rank = a.shape
    dma = pltpu.SemaphoreType.DMA
    part = (n_x, *hidden.shape[:2], cols)
    return pl.pallas_call(
        functools.partial(exchange_kernel, sizes),
        out_shape=(
            jax.ShapeDtypeStruct((n_s, cols + 16, 2 * rank), BF),
            jax.ShapeDtypeStruct(part, BF),
            jax.ShapeDtypeStruct(part, BF),
            jax.ShapeDtypeStruct((n_x, *info.shape), BF),
        ),
        in_specs=[VMEM, VMEM, VMEM, ANY, ANY, ANY],
        out_specs=(ANY,) * 4,
        scratch_shapes=[
            pltpu.VMEM((n_z, cols + 16, 2 * rank), BF),
            dma((n_z, 2)), dma((n_z, 2)), dma((n_z, 2)), dma((n_z, 2)),
            dma((n_z,)), dma((n_s,)), dma((3, n_x)), dma((3, n_x)), dma((4,)),
        ],
        compiler_params=params(0),
        name="exchange",
    )(a, b, g, hidden, cot, info)


class Plane:
    def __init__(self, sizes):
        n_s, n_z, n_x = sizes
        self.n_x = n_x
        self.chips = (n_s // 2) * n_x
        self.s, self.z, self.x = where_am_i()
        self.core = lax.rem(self.s, 2)
        self.chip = (self.s // 2) * n_x + self.x
        self.partner = (self.s + 1 - 2 * self.core, self.z, self.x)

    def peer(self, chip):
        return (2 * (chip // self.n_x) + self.core, self.z, lax.rem(chip, self.n_x))

    def ahead(self, k):
        return lax.rem(self.chip + k, self.chips)

    def behind(self, k):
        return lax.rem(self.chip + self.chips - k, self.chips)

    def others(self, fn):
        loop(self.chips - 1, lambda k: fn(k + 1))

    def greet_all(self, barrier):
        def one(chip):
            s2, z2, x2 = self.peer(chip)
            pl.semaphore_signal(barrier, inc=1, device_id=(s2, z2, x2), device_id_type=MESH)
            pl.semaphore_signal(
                barrier, inc=1, device_id=(s2 + 1 - 2 * self.core, z2, x2), device_id_type=MESH
            )

        self.others(lambda k: one(self.ahead(k)))
        pl.semaphore_signal(barrier, inc=1, device_id=self.partner, device_id_type=MESH)
        return 2 * self.chips - 1


class Cast:
    def __init__(self, plane, view, sems):
        self.p, self.view, self.sems = plane, view, sems

    def far(self, chip, owner):
        send, recv = self.sems[0].at[chip], self.sems[1].at[owner]
        ref = self.view(owner, self.p.core)
        return remote(ref, ref, send, recv, self.p.peer(chip))

    def near(self, chip, core):
        ref = self.view(chip, core)
        return remote(ref, ref, self.sems[2].at[chip], self.sems[3].at[chip], self.p.partner)

    def start(self):
        p = self.p
        p.others(lambda k: self.far(p.ahead(k), p.chip).start())
        self.near(p.chip, p.core).start()

    def relay(self):
        p = self.p

        def one(k):
            chip = p.behind(k)
            self.far(chip, chip).wait_recv()
            self.near(chip, p.core).start()

        p.others(one)

    def finish(self):
        p = self.p
        loop(p.chips, lambda i: self.near(i, 1 - p.core).wait_recv())
        loop(p.chips, lambda i: self.near(i, p.core).wait_send())
        p.others(lambda k: self.far(p.ahead(k), p.chip).wait_send())


def solve_kernel(
    sizes, dims, w_all, h_all, c_all, low_out, err_out,
    gsend, grecv, gram, pbuf, prev, psum, crev, state, snap, full, rin,
    gs, gr, rs, rr, ls, lr, ns, nr, ps, pr, cs, cr, m0, m1, m2, m3, l0, l1, l2, l3, e0, e1, e2, e3,
):
    n_s, n_z, n_x = sizes
    rows, cols, rank, width = dims
    layers = n_s
    own = rows // n_s
    part = rank // n_x
    p = Plane(sizes)
    barrier = pltpu.get_barrier_semaphore()
    count = p.greet_all(barrier)
    for k in (1, n_z - 1):
        pl.semaphore_signal(
            barrier, inc=1, device_id=(p.s, lax.rem(p.z + k, n_z), p.x), device_id_type=MESH
        )
    mine = w_all[p.z, :cols, rank:]
    for l in range(layers):
        g = mm(mine, w_all[l, :cols], 0, 0).astype(BF)
        gsend[l] = g.reshape(n_x, part, 2 * rank)
    pl.semaphore_wait(barrier, count + 2)
    n_plane = 2 * p.chips
    me = p.s * n_x + p.x

    def g_copy(to, slot):
        return remote(
            gsend.at[to // n_x, lax.rem(to, n_x)], grecv.at[slot], gs.at[to], gr.at[slot],
            (to // n_x, p.z, lax.rem(to, n_x)),
        )

    loop(n_plane - 1, lambda k: g_copy(lax.rem(me + 1 + k, n_plane), me).start())
    for l in range(layers):
        for i in range(n_x):
            zy = mm(h_all[i], w_all[l, :cols], 1, 0).astype(BF)
            ct = mm(c_all[i], w_all[l, :cols, rank:], 1, 0).astype(BF)
            at = slice(i * n_s, (i + 1) * n_s)
            for c, value in enumerate((zy[:, :rank], zy[:, rank:], ct)):
                r0 = (c * layers + l) * own
                pbuf[at, r0 : r0 + own, :] = value.reshape(n_s, own, rank)
    for i in range(n_x):
        xf = h_all[i].astype(F32)
        sq = jnp.broadcast_to(jnp.sum(xf * xf, -1, keepdims=True), (rows, rank)).astype(BF)
        pbuf[i * n_s : (i + 1) * n_s, 3 * layers * own :, :] = sq.reshape(n_s, own, rank)

    def block(chip, core):
        return (2 * (chip // n_x) + core) * n_x + lax.rem(chip, n_x)

    def pre(i):
        return remote(pbuf.at[block(i, 1 - p.core)], prev.at[i], ps.at[i], pr.at[i], p.partner)

    def pre_wait(i):
        return remote(pbuf.at[block(i, p.core)], prev.at[i], ps.at[i], pr.at[i], p.partner)

    def c_copy(to, slot):
        return remote(psum.at[to], crev.at[slot], cs.at[to], cr.at[slot], p.peer(to))

    loop(p.chips, lambda k: pre(p.ahead(k)).start())

    loop(n_plane - 1, lambda k: g_copy(me, lax.rem(me + n_plane - 1 - k, n_plane)).wait_recv())
    grecv[me] = gsend[p.s, p.x]
    gsum = grecv[0].astype(F32)
    for k in range(1, n_plane):
        gsum = gsum + grecv[k].astype(F32)
    gram[p.z, p.s, p.x] = gsum.astype(BF)

    def gram_view(chip, core):
        return gram.at[p.z, 2 * (chip // n_x) + core, lax.rem(chip, n_x)]

    spread = Cast(p, gram_view, (m0, m1, m2, m3))
    spread.start()
    spread.relay()
    spread.finish()

    half = layers // 2

    def ring_view(block, piece):
        return gram.at[block, half * p.core + piece]

    ring = Ring(n_z, p.z, lambda to: (p.s, to, p.x), ring_view, half, (rs, rr, ls, lr))
    ring.start()

    def forward(k):
        i = p.ahead(k)
        pre_wait(i).wait_recv()
        total = pbuf[block(i, p.core)].astype(F32) + prev[i].astype(F32)
        psum[i] = total.astype(BF)

        @pl.when(i != p.chip)
        def _():
            c_copy(i, p.chip).start()

    loop(p.chips, lambda k: forward(lax.rem(k + 1, p.chips)))

    def share(layer, piece, core):
        ref = gram.at[layer, half * core + piece]
        return remote(ref, ref, ns.at[layer, piece], nr.at[layer, piece], p.partner)

    ring.run(lambda layer, piece: share(layer, piece, p.core).start())
    p.others(lambda k: c_copy(p.chip, p.behind(k)).wait_recv())
    crev[p.chip] = psum[p.chip]
    total = crev[0].astype(F32)
    for k in range(1, p.chips):
        total = total + crev[k].astype(F32)
    state[...] = total.reshape(3 * layers + 1, own, rank)

    def each_share(fn):
        def body(k):
            layer = lax.rem(p.z + 1 + k, n_z)
            for piece in range(half):
                fn(layer, piece)

        loop(n_z - 1, body)

    each_share(lambda layer, piece: share(layer, piece, 1 - p.core).wait_recv())

    def low_view(chip, core):
        dev = block(chip, core)
        return low_out.at[:, pl.ds(pl.multiple_of(dev * own, own), own), :]

    def err_view(chip, core):
        dev = block(chip, core)
        return err_out.at[:, pl.ds(pl.multiple_of(dev * own, own), own), :]

    here = pl.ds(pl.multiple_of(me * own, own), own)
    square = state[3 * layers]
    zero = jnp.zeros((own, rank), F32)
    lane = lax.broadcasted_iota(jnp.int32, (own, rank), 1)
    scal = zero
    for l in range(layers):
        rinv = lax.rsqrt(square / width + 1e-05)
        u = state[l] * rinv
        low = u.astype(BF)
        full[l] = u
        rin[l] = rinv
        low_out[l, here, :] = low
        before = state[layers + l]
        for j in range(layers):
            snap[l, j] = state[layers + j]
            if j > l:
                both = mm(low, gram[l, j].reshape(rank, 2 * rank), 1, 0)
                state[j] = state[j] + both[:, :rank]
                state[layers + j] = state[layers + j] + both[:, rank:]
            else:
                one = mm(low, gram[l, j, :, :, rank:].reshape(rank, rank), 1, 0)
                state[layers + j] = state[layers + j] + one
        after = state[layers + l]
        square = square + jnp.sum(low.astype(F32) * (before + after), -1, keepdims=True)
        high = rinv.astype(BF).astype(F32)
        scal = jnp.where(lane == l, high, scal)
        scal = jnp.where(lane == layers + l, rinv - high, scal)
    lows = Cast(p, low_view, (l0, l1, l2, l3))
    lows.start()
    for l in range(layers - 1, -1, -1):
        err = state[2 * layers + l].astype(BF)
        mean = jnp.sum(err.astype(F32) * full[l], -1, keepdims=True) / width
        rinv = rin[l]
        cor = rinv * rinv * mean
        for j in range(l):
            back = mm(err, gram[j, l, :, :, :rank].reshape(rank, rank), 1, 1)
            state[2 * layers + j] = state[2 * layers + j] + rinv * back - cor * snap[l, j]
        err_out[l, here, :] = err
        scal = jnp.where(lane == 2 * layers + l, cor, scal)
    err_out[layers, here, :] = scal.astype(BF)
    errs = Cast(p, err_view, (e0, e1, e2, e3))
    errs.start()
    lows.relay()
    errs.relay()
    lows.finish()
    errs.finish()
    loop(n_plane - 1, lambda k: g_copy(lax.rem(me + 1 + k, n_plane), me).wait_send())
    ring.finish()
    each_share(lambda layer, piece: share(layer, piece, p.core).wait_send())
    loop(p.chips, lambda k: pre(p.ahead(k)).wait_send())
    p.others(lambda k: c_copy(p.ahead(k), p.chip).wait_send())


def solve(sizes, dims, w_all, h_all, c_all):
    n_s, n_z, n_x = sizes
    rows, cols, rank, width = dims
    layers = n_s
    chips = (n_s // 2) * n_x
    plane = n_s * n_x
    own = rows // n_s
    group = rows * n_x
    part = rank // n_x
    high = (3 * layers + 1) * own
    dma = pltpu.SemaphoreType.DMA
    v = pltpu.VMEM
    return pl.pallas_call(
        functools.partial(solve_kernel, sizes, dims),
        out_shape=(
            jax.ShapeDtypeStruct((layers, group, rank), BF),
            jax.ShapeDtypeStruct((layers + 1, group, rank), BF),
        ),
        in_specs=[VMEM, VMEM, VMEM],
        out_specs=(VMEM, VMEM),
        scratch_shapes=[
            v((n_s, n_x, part, 2 * rank), BF),
            v((plane, part, 2 * rank), BF),
            v((n_z, n_s, n_x, part, 2 * rank), BF),
            v((plane, high, rank), BF),
            v((chips, high, rank), BF),
            v((chips, high, rank), BF),
            v((chips, high, rank), BF),
            v((3 * layers + 1, own, rank), F32),
            v((layers, layers, own, rank), F32),
            v((layers, own, rank), F32),
            v((layers, own, rank), F32),
            dma((plane,)), dma((plane,)),
        ]
        + [dma((n_z, layers // 2))] * 6
        + [dma((chips,))] * 16,
        compiler_params=params(1),
        name="solve",
    )(w_all, h_all, c_all)


def finish_kernel(
    sizes, dims, bound, w_all, h_all, c_all, i_all, low_ref, err_ref, gi_out, go_out, uw_out,
    normed, deltas, hold, tot, gbuf, mid, grecv, ts, tr, gs, gr, zs, zr, lsem,
):
    n_s, n_z, n_x = sizes
    rows, cols, rank, width, users = dims
    layers = n_s
    p = Plane(sizes)
    s, z, x = p.s, p.z, p.x
    barrier = pltpu.get_barrier_semaphore()
    count = p.greet_all(barrier)
    for k in range(1, n_z):
        pl.semaphore_signal(barrier, inc=1, device_id=(s, lax.rem(z + k, n_z), x), device_id_type=MESH)
    count = count + n_z - 1

    sums = []
    for i in range(n_x):
        at = slice(i * rows, (i + 1) * rows)
        keyrow = i_all[i].astype(F32)[0:1, :rows]
        keys = jnp.broadcast_to(keyrow, (rows, rows))
        same = keys == keys.T
        scal = err_ref[layers, at].astype(F32)
        h = h_all[i].astype(F32)
        pairs = jnp.zeros((rows, rows), F32)
        for l in range(layers):
            gain = w_all[l, cols : cols + 8].astype(F32)[0:1, :]
            rinv = scal[:, l : l + 1] + scal[:, layers + l : layers + l + 1]
            n = (h * rinv * gain).astype(BF)
            e = err_ref[l, at]
            normed[l, at] = n
            hold[l] = h.astype(BF)
            pairs = pairs + mm(n, n, 1, 1) * mm(e, e, 1, 1)
            if l + 1 < layers:
                h = h + mm(low_ref[l, at], w_all[l, :cols, rank:], 1, 1)
        d = c_all[i].astype(F32)
        for l in range(layers - 1, -1, -1):
            db = d.astype(BF)
            deltas[l, at] = db
            lo = low_ref[l, at]
            pairs = pairs + mm(lo, lo, 1, 1) * mm(db, db, 1, 1)
            if l > 0:
                rinv = scal[:, l : l + 1] + scal[:, layers + l : layers + l + 1]
                cor = scal[:, 2 * layers + l : 2 * layers + l + 1]
                d = d + rinv * mm(err_ref[l, at], w_all[l, :cols, :rank], 1, 1)
                d = d - cor * hold[l].astype(F32)
        pairs = jnp.where(same, pairs, 0.0)
        rowsum = jnp.broadcast_to(jnp.sum(pairs, -1, keepdims=True), (rows, rows))
        sums.append(jnp.sum(jnp.where(same, rowsum, 0.0), 0, keepdims=True))
    me = s * n_x + x
    n_plane = n_s * n_x
    pad = [jnp.zeros((8 - n_x, rows), F32)] if n_x < 8 else []
    tot[me] = jnp.concatenate(sums + pad, 0)
    pl.semaphore_wait(barrier, count)

    def t_copy(to, slot):
        return remote(
            tot.at[slot], tot.at[slot], ts.at[to], tr.at[slot], (to // n_x, z, lax.rem(to, n_x))
        )

    loop(n_plane - 1, lambda k: t_copy(lax.rem(me + 1 + k, n_plane), me).start())
    loop(n_plane - 1, lambda k: t_copy(me, lax.rem(me + n_plane - 1 - k, n_plane)).wait_recv())
    total = tot[0]
    for k in range(1, n_plane):
        total = total + tot[k]
    clip = bound / jnp.maximum(jnp.sqrt(total), bound)

    weights = []
    for i in range(n_x):
        inc = i_all[i].astype(F32)[1:2, :rows]
        w = jnp.broadcast_to(inc * clip[i : i + 1], (rows, rows))
        weights.append(w.T[:, :rank])

        @pl.when(x == i)
        def _(w=w, i=i):
            keyrow = i_all[i].astype(F32)[0:1, :rows]
            which = lax.broadcasted_iota(jnp.int32, (users, rows), 0).astype(F32)
            mine = jnp.where(which == keyrow, w[:users], 0.0)
            uw_out[...] = jnp.broadcast_to(jnp.max(mine, -1, keepdims=True), (users, rows))

    weight = jnp.concatenate(weights, 0)

    def g_copy(to, slot):
        return remote(gbuf.at[to], mid.at[slot], gs.at[to], gr.at[slot], (to, z, x))

    def z_copy(to, slot):
        return remote(mid.at[to], grecv.at[slot], zs.at[to], zr.at[slot], (s, to, x))

    for l in range(layers):
        we = (weight * err_ref[l].astype(F32)).astype(BF)
        wl = (weight * low_ref[l].astype(F32)).astype(BF)
        gbuf[l, :, :rank] = mm(normed[l], we, 0, 0).astype(BF)
        gbuf[l, :, rank:] = mm(deltas[l], wl, 0, 0).astype(BF)

        @pl.when(s != l)
        def _(l=l):
            g_copy(l, s).start()

    local = pltpu.make_async_copy(gbuf.at[s], mid.at[s], lsem.at[0])
    local.start()
    local.wait()

    def onward(k):
        @pl.when(k == z)
        def _():
            pltpu.make_async_copy(mid.at[z], grecv.at[z], lsem.at[1]).start()

        @pl.when(k != z)
        def _():
            z_copy(k, z).start()

    onward(s)

    def relay(k):
        at = lax.rem(s + 1 + k, n_s)
        g_copy(s, at).wait_recv()
        onward(at)

    loop(n_s - 1, relay)
    pltpu.make_async_copy(mid.at[z], grecv.at[z], lsem.at[1]).wait()
    loop(n_z - 1, lambda k: z_copy(z, lax.rem(z + 1 + k, n_z)).wait_recv())
    grad = grecv[0].astype(F32)
    for k in range(1, n_z):
        grad = grad + grecv[k].astype(F32)
    gi_out[...] = grad[:, :rank]
    go_out[...] = grad[:, rank:].T
    loop(n_s - 1, lambda k: g_copy(lax.rem(s + 1 + k, n_s), s).wait_send())
    loop(n_z - 1, lambda k: z_copy(lax.rem(z + 1 + k, n_z), z).wait_send())
    loop(n_plane - 1, lambda k: t_copy(lax.rem(me + 1 + k, n_plane), me).wait_send())


def finish(sizes, dims, bound, *arrays):
    n_s, n_z, n_x = sizes
    rows, cols, rank, width, users = dims
    layers = n_s
    plane = n_s * n_x
    dma = pltpu.SemaphoreType.DMA
    v = pltpu.VMEM
    return pl.pallas_call(
        functools.partial(finish_kernel, sizes, dims, bound),
        out_shape=(
            jax.ShapeDtypeStruct((cols, rank), F32),
            jax.ShapeDtypeStruct((rank, cols), F32),
            jax.ShapeDtypeStruct((users, rows), F32),
        ),
        in_specs=[VMEM] * 6,
        out_specs=(VMEM,) * 3,
        scratch_shapes=[
            v((layers, rows * n_x, cols), BF),
            v((layers, rows * n_x, cols), BF),
            v((layers, rows, cols), BF),
            v((plane, 8, rows), F32),
            v((layers, cols, 2 * rank), BF),
            v((n_s, cols, 2 * rank), BF),
            v((n_z, cols, 2 * rank), BF),
            dma((plane,)), dma((plane,)), dma((n_s,)), dma((n_s,)), dma((n_z,)), dma((n_z,)), dma((2,)),
        ],
        compiler_params=params(2),
        name="finish",
    )(*arrays)


def shards(hidden_in, cotangent, adapter_in, adapter_out, norm_gain, user_of_row, included):
    sizes = tuple(lax.axis_size(a) for a in ("section", "z", "x"))
    n_s, n_z, n_x = sizes
    _, zi, xi = where_am_i()
    micro, rows, width = hidden_in.shape
    cols, rank = adapter_in.shape[1:]
    users = included.shape[1]
    dev_rows = micro * rows
    base = (zi * n_x + xi) * users
    local = user_of_row - base
    key = (local + users * jnp.arange(micro, dtype=jnp.int32)[:, None]).reshape(1, dev_rows)
    onehot = local[:, :, None] == jnp.arange(users, dtype=jnp.int32)
    inc = jnp.sum(jnp.where(onehot, included[:, None, :], 0), -1).reshape(1, dev_rows)
    info = jnp.pad(jnp.concatenate([key, inc], 0).astype(BF), ((0, 14), (0, cols - dev_rows)))
    w_all, h_all, c_all, i_all = exchange(
        sizes, adapter_in[0], adapter_out[0], norm_gain, hidden_in, cotangent, info
    )
    h_all = h_all.reshape(n_x, dev_rows, cols)
    c_all = c_all.reshape(n_x, dev_rows, cols)
    low, err = solve(sizes, (dev_rows, cols, rank, width), w_all, h_all, c_all)
    bound = 0.8 * math.sqrt(n_s * (rows // users) * width * width)
    gi, go, uw = finish(
        sizes, (dev_rows, cols, rank, width, micro * users), bound, w_all, h_all, c_all, i_all, low, err
    )
    return (gi[None], go[None], uw[:, 0].reshape(micro, users))


def build(torus):
    dp = ("z", "x")
    return jax.shard_map(
        shards,
        mesh=torus,
        in_specs=(
            P(None, dp, None),
            P(None, dp, None),
            P("section", dp, None),
            P("section", None, dp),
            P("section", dp),
            P(None, dp),
            P(None, dp),
        ),
        out_specs=(P("section", dp, None), P("section", None, dp), P(None, dp)),
        check_vma=False,
    )


def solution(mesh):
    return build(Mesh(mesh.devices.reshape(mesh.shape["section"], 8, 4), ("section", "z", "x")))
```

```python
import functools
import math

import jax
import jax.numpy as jnp
from jax import lax
from jax.experimental import pallas as pl
from jax.experimental.pallas import tpu as pltpu
from jax.sharding import Mesh
from jax.sharding import PartitionSpec as P

F32 = jnp.float32
BF = jnp.bfloat16
MESH = pl.DeviceIdType.MESH
VMEM = pl.BlockSpec(memory_space=pltpu.VMEM)
ANY = pl.BlockSpec(memory_space=pl.ANY)
LIMIT = 60 * 1024 * 1024


def mm(a, b, ca, cb):
    return lax.dot_general(a, b, (((ca,), (cb,)), ((), ())), preferred_element_type=F32)


def loop(n, body):
    lax.fori_loop(0, n, lambda i, c: (body(i), c)[1], 0)


def remote(src, dst, send, recv, device):
    return pltpu.make_async_remote_copy(
        src_ref=src, dst_ref=dst, send_sem=send, recv_sem=recv, device_id=device, device_id_type=MESH
    )


def params(cid):
    return pltpu.CompilerParams(collective_id=cid, has_side_effects=True, vmem_limit_bytes=LIMIT)


def where_am_i():
    return tuple(lax.axis_index(a) for a in ("section", "z", "x"))


class Ring:
    def __init__(self, n, me, place, view, pieces, sems):
        self.n, self.me, self.place, self.view, self.pieces, self.sems = n, me, place, view, pieces, sems
        self.steps = (n // 2, n - 1 - n // 2)

    def copy(self, way, step, piece, from_me):
        n, me = self.n, self.me
        sign = 1 - 2 * way
        block = (me - sign * step) if from_me else (me - sign * (step + 1))
        ref = self.view(lax.rem(block + 2 * n, n), piece)
        send, recv = self.sems[2 * way].at[step, piece], self.sems[2 * way + 1].at[step, piece]
        return remote(ref, ref, send, recv, self.place(lax.rem(me + sign + n, n)))

    def start(self):
        for piece in range(self.pieces):
            for way in (0, 1):
                self.copy(way, 0, piece, True).start()

    def run(self, arrived):
        for step in range(self.steps[0]):
            for piece in range(self.pieces):
                for way in (0, 1):
                    if step < self.steps[way]:
                        self.copy(way, step, piece, False).wait_recv()
                        if step + 1 < self.steps[way]:
                            self.copy(way, step + 1, piece, True).start()
                        sign = 1 - 2 * way
                        block = lax.rem(self.me - sign * (step + 1) + 2 * self.n, self.n)
                        arrived(block, piece)

    def finish(self):
        for way in (0, 1):
            for step in range(self.steps[way]):
                for piece in range(self.pieces):
                    self.copy(way, step, piece, True).wait_send()


def exchange_phase(
    sizes, a_ref, b_ref, g_ref, hid_ref, cot_ref, user_ref, inc_ref, w_all, h_all, c_all, i_all, ready,
    column, info, rs, rr, ls, lr, ys, yr, asend, arecv, lsem,
):
    n_s, n_z, n_x = sizes
    s, z, x = where_am_i()
    cols, rank = a_ref.shape
    micro, rows = user_ref.shape
    users = inc_ref.shape[1]
    gain = jnp.broadcast_to(g_ref[...].astype(F32), (rank, cols))
    column[z, :cols, :rank] = (a_ref[...].astype(F32) * gain.T).astype(BF)
    column[z, :cols, rank:] = b_ref[...].astype(F32).T.astype(BF)
    column[z, cols:, :] = jnp.broadcast_to(g_ref[...].astype(F32), (16, cols)).astype(BF)
    local = user_ref[...] - (z * n_x + x) * users
    included = jnp.zeros((micro, rows), F32)
    for u in range(users):
        included = jnp.where(local == u, inc_ref[:, u : u + 1].astype(F32), included)
    key = (local + users * lax.broadcasted_iota(jnp.int32, (micro, rows), 0)).astype(F32)
    dev_rows = micro * rows
    lane = lax.broadcasted_iota(jnp.int32, (rows, dev_rows), 1)
    row = lax.broadcasted_iota(jnp.int32, (rows, dev_rows), 0)
    place = sum(jnp.where(lane == row + m * rows, 1.0, 0.0) for m in range(micro)).astype(BF)
    top = lax.broadcasted_iota(jnp.int32, (micro, dev_rows), 0)
    along = lax.broadcasted_iota(jnp.int32, (micro, dev_rows), 1)
    mine = jnp.logical_and(along >= top * rows, along < (top + 1) * rows)

    def flat(v):
        wide = mm(v.astype(BF), place, 1, 0)
        return jnp.sum(jnp.where(mine, wide, 0.0), 0, keepdims=True)

    which_row = lax.broadcasted_iota(jnp.int32, (16, dev_rows), 0)
    info[...] = jnp.where(which_row == 0, flat(key), flat(included)).astype(BF)
    ready()

    def act(which, to, slot):
        at = pl.ds(pl.multiple_of((s * n_x + to) * cols, cols), cols)
        src = (hid_ref.at[:, :, at], cot_ref.at[:, :, at], info)[which]
        dst = (h_all, c_all, i_all)[which].at[slot]
        return src, dst

    def a_copy(which, to, slot):
        src, dst = act(which, to, slot)
        return remote(src, dst, asend.at[which, to], arecv.at[which, slot], (s, z, to))

    split = cols // 2
    half = (slice(0, split), slice(split, cols + 16))

    def view(block, piece):
        return column.at[block, half[piece]]

    ring = Ring(n_z, z, lambda to: (s, to, x), view, 2, (rs, rr, ls, lr))
    ring.start()
    for which in range(3):
        for k in range(1, n_x):
            a_copy(which, lax.rem(x + k, n_x), x).start()
    for which in range(3):
        src, dst = act(which, x, x)
        pltpu.make_async_copy(src, dst, lsem.at[which]).start()

    def y_copy(block, slot, piece):
        return remote(
            column.at[block, half[piece]], w_all.at[slot, half[piece]],
            ys.at[block, piece], yr.at[slot, piece], (block, z, x),
        )

    def keep(piece):
        return pltpu.make_async_copy(
            column.at[s, half[piece]], w_all.at[s, half[piece]], lsem.at[3 + piece]
        )

    def onward(block, piece):
        @pl.when(block == s)
        def _():
            keep(piece).start()

        @pl.when(block != s)
        def _():
            y_copy(block, s, piece).start()

    for piece in (0, 1):
        onward(z, piece)
    ring.run(onward)
    for which in range(3):
        src, dst = act(which, x, x)
        pltpu.make_async_copy(src, dst, lsem.at[which]).wait()
        for k in range(1, n_x):
            a_copy(which, x, lax.rem(x + n_x - k, n_x)).wait_recv()

    def not_me(fn):
        def body(k):
            for piece in (0, 1):
                fn(lax.rem(s + 1 + k, n_s), piece)

        loop(n_s - 1, body)

    for piece in (0, 1):
        keep(piece).wait()
    not_me(lambda k, piece: y_copy(s, k, piece).wait_recv())

    def drain():
        not_me(lambda k, piece: y_copy(k, s, piece).wait_send())
        for which in range(3):
            for k in range(1, n_x):
                a_copy(which, lax.rem(x + k, n_x), x).wait_send()
        ring.finish()

    return drain


class Plane:
    def __init__(self, sizes):
        n_s, n_z, n_x = sizes
        self.n_x = n_x
        self.chips = (n_s // 2) * n_x
        self.s, self.z, self.x = where_am_i()
        self.core = lax.rem(self.s, 2)
        self.chip = (self.s // 2) * n_x + self.x
        self.partner = (self.s + 1 - 2 * self.core, self.z, self.x)

    def peer(self, chip):
        return (2 * (chip // self.n_x) + self.core, self.z, lax.rem(chip, self.n_x))

    def ahead(self, k):
        return lax.rem(self.chip + k, self.chips)

    def behind(self, k):
        return lax.rem(self.chip + self.chips - k, self.chips)

    def others(self, fn):
        loop(self.chips - 1, lambda k: fn(k + 1))

    def greet_all(self, barrier):
        def one(chip):
            s2, z2, x2 = self.peer(chip)
            pl.semaphore_signal(barrier, inc=1, device_id=(s2, z2, x2), device_id_type=MESH)
            pl.semaphore_signal(
                barrier, inc=1, device_id=(s2 + 1 - 2 * self.core, z2, x2), device_id_type=MESH
            )

        self.others(lambda k: one(self.ahead(k)))
        pl.semaphore_signal(barrier, inc=1, device_id=self.partner, device_id_type=MESH)
        return 2 * self.chips - 1


class Cast:
    def __init__(self, plane, view, sems):
        self.p, self.view, self.sems = plane, view, sems

    def far(self, chip, owner):
        send, recv = self.sems[0].at[chip], self.sems[1].at[owner]
        ref = self.view(owner, self.p.core)
        return remote(ref, ref, send, recv, self.p.peer(chip))

    def near(self, chip, core):
        ref = self.view(chip, core)
        return remote(ref, ref, self.sems[2].at[chip], self.sems[3].at[chip], self.p.partner)

    def start(self):
        p = self.p
        p.others(lambda k: self.far(p.ahead(k), p.chip).start())
        self.near(p.chip, p.core).start()

    def relay(self):
        p = self.p

        def one(k):
            chip = p.behind(k)
            self.far(chip, chip).wait_recv()
            self.near(chip, p.core).start()

        p.others(one)

    def finish(self):
        p = self.p
        loop(p.chips, lambda i: self.near(i, 1 - p.core).wait_recv())
        loop(p.chips, lambda i: self.near(i, p.core).wait_send())
        p.others(lambda k: self.far(p.ahead(k), p.chip).wait_send())


def solve_phase(
    sizes, dims, w_all, h_all, c_all, low_out, err_out,
    gsend, grecv, gram, pbuf, prev, psum, crev, state, snap, full, rin,
    gs, gr, rs, rr, ls, lr, ns, nr, ps, pr, cs, cr, m0, m1, m2, m3, l0, l1, l2, l3, e0, e1, e2, e3,
):
    n_s, n_z, n_x = sizes
    rows, cols, rank, width = dims
    layers = n_s
    own = rows // n_s
    part = rank // n_x
    p = Plane(sizes)
    mine = w_all[p.z, :cols, rank:]
    for l in range(layers):
        g = mm(mine, w_all[l, :cols], 0, 0).astype(BF)
        gsend[l] = g.reshape(n_x, part, 2 * rank)
    n_plane = 2 * p.chips
    me = p.s * n_x + p.x

    def g_copy(to, slot):
        return remote(
            gsend.at[to // n_x, lax.rem(to, n_x)], grecv.at[slot], gs.at[to], gr.at[slot],
            (to // n_x, p.z, lax.rem(to, n_x)),
        )

    loop(n_plane - 1, lambda k: g_copy(lax.rem(me + 1 + k, n_plane), me).start())
    for l in range(layers):
        for i in range(n_x):
            zy = mm(h_all[i].reshape(rows, cols), w_all[l, :cols], 1, 0).astype(BF)
            ct = mm(c_all[i].reshape(rows, cols), w_all[l, :cols, rank:], 1, 0).astype(BF)
            at = slice(i * n_s, (i + 1) * n_s)
            for c, value in enumerate((zy[:, :rank], zy[:, rank:], ct)):
                r0 = (c * layers + l) * own
                pbuf[at, r0 : r0 + own, :] = value.reshape(n_s, own, rank)
    for i in range(n_x):
        xf = h_all[i].reshape(rows, cols).astype(F32)
        sq = jnp.broadcast_to(jnp.sum(xf * xf, -1, keepdims=True), (rows, rank)).astype(BF)
        pbuf[i * n_s : (i + 1) * n_s, 3 * layers * own :, :] = sq.reshape(n_s, own, rank)

    def block(chip, core):
        return (2 * (chip // n_x) + core) * n_x + lax.rem(chip, n_x)

    def pre(i):
        return remote(pbuf.at[block(i, 1 - p.core)], prev.at[i], ps.at[i], pr.at[i], p.partner)

    def pre_wait(i):
        return remote(pbuf.at[block(i, p.core)], prev.at[i], ps.at[i], pr.at[i], p.partner)

    def c_copy(to, slot):
        return remote(psum.at[to], crev.at[slot], cs.at[to], cr.at[slot], p.peer(to))

    loop(p.chips, lambda k: pre(p.ahead(k)).start())

    loop(n_plane - 1, lambda k: g_copy(me, lax.rem(me + n_plane - 1 - k, n_plane)).wait_recv())
    grecv[me] = gsend[p.s, p.x]
    gsum = grecv[0].astype(F32)
    for k in range(1, n_plane):
        gsum = gsum + grecv[k].astype(F32)
    gram[p.z, p.s, p.x] = gsum.astype(BF)

    def gram_view(chip, core):
        return gram.at[p.z, 2 * (chip // n_x) + core, lax.rem(chip, n_x)]

    spread = Cast(p, gram_view, (m0, m1, m2, m3))
    spread.start()
    spread.relay()
    spread.finish()

    half = layers // 2

    def ring_view(block, piece):
        return gram.at[block, half * p.core + piece]

    ring = Ring(n_z, p.z, lambda to: (p.s, to, p.x), ring_view, half, (rs, rr, ls, lr))
    ring.start()

    def forward(k):
        i = p.ahead(k)
        pre_wait(i).wait_recv()
        total = pbuf[block(i, p.core)].astype(F32) + prev[i].astype(F32)
        psum[i] = total.astype(BF)

        @pl.when(i != p.chip)
        def _():
            c_copy(i, p.chip).start()

    loop(p.chips, lambda k: forward(lax.rem(k + 1, p.chips)))

    def share(layer, piece, core):
        ref = gram.at[layer, half * core + piece]
        return remote(ref, ref, ns.at[layer, piece], nr.at[layer, piece], p.partner)

    ring.run(lambda layer, piece: share(layer, piece, p.core).start())
    p.others(lambda k: c_copy(p.chip, p.behind(k)).wait_recv())
    crev[p.chip] = psum[p.chip]
    total = crev[0].astype(F32)
    for k in range(1, p.chips):
        total = total + crev[k].astype(F32)
    state[...] = total.reshape(3 * layers + 1, own, rank)

    def each_share(fn):
        def body(k):
            layer = lax.rem(p.z + 1 + k, n_z)
            for piece in range(half):
                fn(layer, piece)

        loop(n_z - 1, body)

    each_share(lambda layer, piece: share(layer, piece, 1 - p.core).wait_recv())

    def low_view(chip, core):
        dev = block(chip, core)
        return low_out.at[:, pl.ds(pl.multiple_of(dev * own, own), own), :]

    def err_view(chip, core):
        dev = block(chip, core)
        return err_out.at[:, pl.ds(pl.multiple_of(dev * own, own), own), :]

    here = pl.ds(pl.multiple_of(me * own, own), own)
    square = state[3 * layers]
    zero = jnp.zeros((own, rank), F32)
    lane = lax.broadcasted_iota(jnp.int32, (own, rank), 1)
    scal = zero
    for l in range(layers):
        rinv = lax.rsqrt(square / width + 1e-05)
        u = state[l] * rinv
        low = u.astype(BF)
        full[l] = u
        rin[l] = rinv
        low_out[l, here, :] = low
        before = state[layers + l]
        for j in range(layers):
            snap[l, j] = state[layers + j]
            if j > l:
                both = mm(low, gram[l, j].reshape(rank, 2 * rank), 1, 0)
                state[j] = state[j] + both[:, :rank]
                state[layers + j] = state[layers + j] + both[:, rank:]
            else:
                one = mm(low, gram[l, j, :, :, rank:].reshape(rank, rank), 1, 0)
                state[layers + j] = state[layers + j] + one
        after = state[layers + l]
        square = square + jnp.sum(low.astype(F32) * (before + after), -1, keepdims=True)
        high = rinv.astype(BF).astype(F32)
        scal = jnp.where(lane == l, high, scal)
        scal = jnp.where(lane == layers + l, rinv - high, scal)
    lows = Cast(p, low_view, (l0, l1, l2, l3))
    lows.start()
    for l in range(layers - 1, -1, -1):
        err = state[2 * layers + l].astype(BF)
        mean = jnp.sum(err.astype(F32) * full[l], -1, keepdims=True) / width
        rinv = rin[l]
        cor = rinv * rinv * mean
        for j in range(l):
            back = mm(err, gram[j, l, :, :, :rank].reshape(rank, rank), 1, 1)
            state[2 * layers + j] = state[2 * layers + j] + rinv * back - cor * snap[l, j]
        err_out[l, here, :] = err
        scal = jnp.where(lane == 2 * layers + l, cor, scal)
    err_out[layers, here, :] = scal.astype(BF)
    errs = Cast(p, err_view, (e0, e1, e2, e3))
    errs.start()
    lows.relay()
    errs.relay()
    lows.finish()
    errs.finish()

    def drain():
        loop(n_plane - 1, lambda k: g_copy(lax.rem(me + 1 + k, n_plane), me).wait_send())
        ring.finish()
        each_share(lambda layer, piece: share(layer, piece, p.core).wait_send())
        loop(p.chips, lambda k: pre(p.ahead(k)).wait_send())
        p.others(lambda k: c_copy(p.ahead(k), p.chip).wait_send())

    return drain


def finish_phase(
    sizes, dims, bound, w_all, h_all, c_all, i_all, low_ref, err_ref, grad_out, row_out,
    normed, deltas, hold, tot, gbuf, mid, acc, rbuf, lbuf, ts, tr, gs, gr, zs, zr, us, ur, lsem,
):
    n_s, n_z, n_x = sizes
    rows, cols, rank, width = dims
    layers = n_s
    p = Plane(sizes)
    s, z, x = p.s, p.z, p.x
    sums = []
    for i in range(n_x):
        at = slice(i * rows, (i + 1) * rows)
        keyrow = i_all[i].astype(F32)[0:1, :]
        keys = jnp.broadcast_to(keyrow, (rows, rows))
        same = keys == keys.T
        scal = err_ref[layers, at].astype(F32)
        h = h_all[i].reshape(rows, cols).astype(F32)
        pairs = jnp.zeros((rows, rows), F32)
        for l in range(layers):
            gain = w_all[l, cols : cols + 8].astype(F32)[0:1, :]
            rinv = scal[:, l : l + 1] + scal[:, layers + l : layers + l + 1]
            n = (h * rinv * gain).astype(BF)
            e = err_ref[l, at]
            normed[l, at] = n
            hold[l] = h.astype(BF)
            pairs = pairs + mm(n, n, 1, 1) * mm(e, e, 1, 1)
            if l + 1 < layers:
                h = h + mm(low_ref[l, at], w_all[l, :cols, rank:], 1, 1)
        d = c_all[i].reshape(rows, cols).astype(F32)
        for l in range(layers - 1, -1, -1):
            db = d.astype(BF)
            deltas[l, at] = db
            lo = low_ref[l, at]
            pairs = pairs + mm(lo, lo, 1, 1) * mm(db, db, 1, 1)
            if l > 0:
                rinv = scal[:, l : l + 1] + scal[:, layers + l : layers + l + 1]
                cor = scal[:, 2 * layers + l : 2 * layers + l + 1]
                d = d + rinv * mm(err_ref[l, at], w_all[l, :cols, :rank], 1, 1)
                d = d - cor * hold[l].astype(F32)
        pairs = jnp.where(same, pairs, 0.0)
        rowsum = jnp.broadcast_to(jnp.sum(pairs, -1, keepdims=True), (rows, rows))
        sums.append(jnp.sum(jnp.where(same, rowsum, 0.0), 0, keepdims=True))
    me = s * n_x + x
    n_plane = n_s * n_x
    pad = [jnp.zeros((8 - n_x, rows), F32)] if n_x < 8 else []
    tot[me] = jnp.concatenate(sums + pad, 0)

    def t_copy(to, slot):
        return remote(
            tot.at[slot], tot.at[slot], ts.at[to], tr.at[slot], (to // n_x, z, lax.rem(to, n_x))
        )

    loop(n_plane - 1, lambda k: t_copy(lax.rem(me + 1 + k, n_plane), me).start())
    loop(n_plane - 1, lambda k: t_copy(me, lax.rem(me + n_plane - 1 - k, n_plane)).wait_recv())
    total = tot[0]
    for k in range(1, n_plane):
        total = total + tot[k]
    clip = bound / jnp.maximum(jnp.sqrt(total), bound)

    weights = []
    for i in range(n_x):
        inc = i_all[i].astype(F32)[1:2, :]
        w = jnp.broadcast_to(inc * clip[i : i + 1], (rows, rows))
        weights.append(w.T[:, :rank])

        @pl.when(x == i)
        def _(w=w, i=i):
            row_out[0:1, :] = w[0:1, :]
            row_out[1:2, :] = i_all[i].astype(F32)[0:1, :]

    weight = jnp.concatenate(weights, 0)

    def g_copy(to, slot):
        return remote(gbuf.at[to], mid.at[slot], gs.at[to], gr.at[slot], (to, z, x))

    def keep():
        return pltpu.make_async_copy(gbuf.at[s], mid.at[s], lsem.at[0])

    for l in range(layers):
        we = (weight * err_ref[l].astype(F32)).astype(BF)
        wl = (weight * low_ref[l].astype(F32)).astype(BF)
        gbuf[l, :, :rank] = mm(normed[l], we, 0, 0).astype(BF)
        gbuf[l, :, rank:] = mm(deltas[l], wl, 0, 0).astype(BF)

        @pl.when(s != l)
        def _(l=l):
            g_copy(l, s).start()

        @pl.when(s == l)
        def _():
            keep().start()

    def have(slot):
        @pl.when(slot == s)
        def _():
            keep().wait()

        @pl.when(slot != s)
        def _():
            g_copy(s, slot).wait_recv()

    right = n_z // 2
    left = n_z - 1 - right
    halves = (slice(0, cols // 2), slice(cols // 2, cols))

    def hop(way, step, piece, src):
        last = step + 1 == (right, left)[way]
        part = halves[piece]
        dst = grad_out.at[1 + way, part] if last else (rbuf, lbuf)[way].at[step, part]
        send, recv = ((zs, zr), (us, ur))[way]
        to = lax.rem(z + (1, n_z - 1)[way], n_z)
        return remote(src, dst, send.at[step, piece], recv.at[step, piece], (s, to, x))

    def source(way, step, piece, slot):
        part = halves[piece]
        return mid.at[slot, part] if step == 0 else acc.at[way, step - 1, part]

    def slot_of(way, step):
        gap = (right - step) if way == 0 else (n_z - left + step)
        return lax.rem(z + gap, n_z)

    for step in range(right):
        for way in (0, 1):
            if step < (right, left)[way]:
                have(slot_of(way, step))
        for piece in (0, 1):
            for way in (0, 1):
                if step >= (right, left)[way]:
                    continue
                slot = slot_of(way, step)
                part = halves[piece]
                src = source(way, step, piece, slot)
                if step > 0:
                    hop(way, step - 1, piece, source(way, step - 1, piece, slot)).wait_recv()
                    came = (rbuf, lbuf)[way][step - 1, part].astype(F32)
                    acc[way, step - 1, part] = (came + mid[slot, part].astype(F32)).astype(BF)
                hop(way, step, piece, src).start()
    have(z)
    grad_out[0] = mid[z]
    for way in (0, 1):
        step = (right, left)[way] - 1
        for piece in (0, 1):
            hop(way, step, piece, source(way, step, piece, z)).wait_recv()

    def drain():
        for way in (0, 1):
            for step in range((right, left)[way]):
                for piece in (0, 1):
                    hop(way, step, piece, source(way, step, piece, z)).wait_send()
        loop(n_s - 1, lambda k: g_copy(lax.rem(s + 1 + k, n_s), s).wait_send())
        loop(n_plane - 1, lambda k: t_copy(lax.rem(me + 1 + k, n_plane), me).wait_send())

    return drain


def main_kernel(
    sizes, dims, bound, n_ex, n_so, a_ref, b_ref, g_ref, hid_ref, cot_ref, user_ref, inc_ref,
    grad_out, row_out, w_all, h_all, c_all, i_all, low, err, *scratch,
):
    n_s, n_z, n_x = sizes
    p = Plane(sizes)
    barrier = pltpu.get_barrier_semaphore()
    count = p.greet_all(barrier)
    for k in (1, n_z - 1):
        pl.semaphore_signal(
            barrier, inc=1, device_id=(p.s, lax.rem(p.z + k, n_z), p.x), device_id_type=MESH
        )
    first = exchange_phase(
        sizes, a_ref, b_ref, g_ref, hid_ref, cot_ref, user_ref, inc_ref, w_all, h_all, c_all, i_all,
        lambda: pl.semaphore_wait(barrier, count + 2), *scratch[:n_ex],
    )
    second = solve_phase(sizes, dims, w_all, h_all, c_all, low, err, *scratch[n_ex : n_ex + n_so])
    third = finish_phase(
        sizes, dims, bound, w_all, h_all, c_all, i_all, low, err, grad_out, row_out,
        *scratch[n_ex + n_so :],
    )
    first()
    second()
    third()


def main(sizes, dims, bound, a, b, g, hidden, cot, users, inc):
    n_s, n_z, n_x = sizes
    rows, cols, rank, width = dims
    layers = n_s
    chips = (n_s // 2) * n_x
    plane = n_s * n_x
    own = rows // n_s
    group = rows * n_x
    part = rank // n_x
    high = (3 * layers + 1) * own
    dma = pltpu.SemaphoreType.DMA
    v = pltpu.VMEM
    slab = (n_x, *hidden.shape[:2], cols)
    shared = [
        v((n_s, cols + 16, 2 * rank), BF),
        v(slab, BF),
        v(slab, BF),
        v((n_x, 16, rows), BF),
        v((layers, group, rank), BF),
        v((layers + 1, group, rank), BF),
    ]
    ex = [
        v((n_z, cols + 16, 2 * rank), BF),
        v((16, rows), BF),
        dma((n_z, 2)), dma((n_z, 2)), dma((n_z, 2)), dma((n_z, 2)),
        dma((n_z, 2)), dma((n_s, 2)), dma((3, n_x)), dma((3, n_x)), dma((5,)),
    ]
    so = [
        v((n_s, n_x, part, 2 * rank), BF),
        v((plane, part, 2 * rank), BF),
        v((n_z, n_s, n_x, part, 2 * rank), BF),
        v((plane, high, rank), BF),
        v((chips, high, rank), BF),
        v((chips, high, rank), BF),
        v((chips, high, rank), BF),
        v((3 * layers + 1, own, rank), F32),
        v((layers, layers, own, rank), F32),
        v((layers, own, rank), F32),
        v((layers, own, rank), F32),
        dma((plane,)), dma((plane,)),
    ]
    so += [dma((n_z, layers // 2))] * 6 + [dma((chips,))] * 16
    fi = [
        v((layers, group, cols), BF),
        v((layers, group, cols), BF),
        v((layers, rows, cols), BF),
        v((plane, 8, rows), F32),
        v((layers, cols, 2 * rank), BF),
        v((n_s, cols, 2 * rank), BF),
        v((2, n_z // 2, cols, 2 * rank), BF),
        v((n_z // 2, cols, 2 * rank), BF),
        v((n_z // 2, cols, 2 * rank), BF),
        dma((plane,)), dma((plane,)), dma((n_s,)), dma((n_s,)),
    ]
    fi += [dma((n_z // 2, 2))] * 4 + [dma((1,))]
    return pl.pallas_call(
        functools.partial(main_kernel, sizes, dims, bound, len(ex), len(so)),
        out_shape=(
            jax.ShapeDtypeStruct((3, cols, 2 * rank), BF),
            jax.ShapeDtypeStruct((8, rows), F32),
        ),
        in_specs=[VMEM, VMEM, VMEM, ANY, ANY, VMEM, VMEM],
        out_specs=(VMEM, VMEM),
        scratch_shapes=shared + ex + so + fi,
        compiler_params=params(0),
        name="main",
    )(a, b, g, hidden, cot, users, inc)


def close_kernel(parts, row, gi_out, go_out, uw_out):
    rank = gi_out.shape[1]
    grad = parts[0].astype(F32) + parts[1].astype(F32) + parts[2].astype(F32)
    gi_out[...] = grad[:, :rank]
    go_out[...] = grad[:, rank:].T
    micro, users = uw_out.shape
    width = row.shape[1]
    weight = jnp.broadcast_to(row[0:1, :], (micro, width))
    key = jnp.broadcast_to(row[1:2, :], (micro, width))
    first = (lax.broadcasted_iota(jnp.int32, (micro, width), 0) * users).astype(F32)
    lane = lax.broadcasted_iota(jnp.int32, (micro, users), 1)
    result = jnp.zeros((micro, users), F32)
    for u in range(users):
        most = jnp.max(jnp.where(key == first + u, weight, 0.0), -1, keepdims=True)
        result = jnp.where(lane == u, most, result)
    uw_out[...] = result


def shards(hidden_in, cotangent, adapter_in, adapter_out, norm_gain, user_of_row, included):
    sizes = tuple(lax.axis_size(a) for a in ("section", "z", "x"))
    n_s = sizes[0]
    micro, rows, width = hidden_in.shape
    cols, rank = adapter_in.shape[1:]
    users = included.shape[1]
    bound = 0.8 * math.sqrt(n_s * (rows // users) * width * width)
    parts, row = main(
        sizes, (micro * rows, cols, rank, width), bound, adapter_in[0], adapter_out[0], norm_gain,
        hidden_in, cotangent, user_of_row, included,
    )
    gi, go, uw = pl.pallas_call(
        close_kernel,
        out_shape=(
            jax.ShapeDtypeStruct((cols, rank), F32),
            jax.ShapeDtypeStruct((rank, cols), F32),
            jax.ShapeDtypeStruct((micro, users), F32),
        ),
        in_specs=[VMEM, VMEM],
        out_specs=(VMEM,) * 3,
        name="close",
    )(parts, row)
    return (gi[None], go[None], uw)


def build(torus):
    dp = ("z", "x")
    return jax.shard_map(
        shards,
        mesh=torus,
        in_specs=(
            P(None, dp, None),
            P(None, dp, None),
            P("section", dp, None),
            P("section", None, dp),
            P("section", dp),
            P(None, dp),
            P(None, dp),
        ),
        out_specs=(P("section", dp, None), P("section", None, dp), P(None, dp)),
        check_vma=False,
    )


def solution(mesh):
    return build(Mesh(mesh.devices.reshape(mesh.shape["section"], 8, 4), ("section", "z", "x")))
```

```python
import functools
import math

import jax
import jax.numpy as jnp
from jax import lax
from jax.experimental import pallas as pl
from jax.experimental.pallas import tpu as pltpu
from jax.sharding import Mesh
from jax.sharding import PartitionSpec as P

F32 = jnp.float32
BF = jnp.bfloat16
MESH = pl.DeviceIdType.MESH
VMEM = pl.BlockSpec(memory_space=pltpu.VMEM)
ANY = pl.BlockSpec(memory_space=pl.ANY)
LIMIT = 60 * 1024 * 1024


def mm(a, b, ca, cb):
    return lax.dot_general(a, b, (((ca,), (cb,)), ((), ())), preferred_element_type=F32)


def loop(n, body):
    lax.fori_loop(0, n, lambda i, c: (body(i), c)[1], 0)


def remote(src, dst, send, recv, device):
    return pltpu.make_async_remote_copy(
        src_ref=src, dst_ref=dst, send_sem=send, recv_sem=recv, device_id=device, device_id_type=MESH
    )


def params(cid):
    return pltpu.CompilerParams(collective_id=cid, has_side_effects=True, vmem_limit_bytes=LIMIT)


def where_am_i():
    return tuple(lax.axis_index(a) for a in ("section", "z", "x"))


class Ring:
    def __init__(self, n, me, place, view, pieces, sems, want=None):
        self.n, self.me, self.place, self.view, self.pieces, self.sems = n, me, place, view, pieces, sems
        self.want = want
        self.far = n // 2

    def block(self, way, step):
        sign = 1 - 2 * way
        return lax.rem(self.me - sign * step + 2 * self.n, self.n)

    def copy(self, way, step, piece, block):
        sign = 1 - 2 * way
        ref = self.view(block, piece)
        send, recv = self.sems[2 * way].at[step, piece], self.sems[2 * way + 1].at[step, piece]
        return remote(ref, ref, send, recv, self.place(lax.rem(self.me + sign + self.n, self.n)))

    def guard(self, block, piece, fn):
        if self.want is None:
            fn()
        else:
            pl.when(self.want(block, piece))(fn)

    def each(self, step, fn):
        half = self.pieces // 2

        def body(i):
            if step + 1 < self.far:
                for way in (0, 1):
                    fn(way, i)
            else:
                fn(0, i)
                fn(1, i + half)

        count = self.pieces if step + 1 < self.far else half
        if self.want is None:
            for i in range(count):
                body(i)
        else:
            loop(count, body)

    def send(self, way, step, piece):
        block = self.block(way, step)
        self.guard(block, piece, lambda: self.copy(way, step, piece, block).start())

    def start(self):
        self.each(0, lambda way, piece: self.send(way, 0, piece))

    def run(self, arrived):
        half = self.pieces // 2

        def one(step, way, piece):
            block = self.block(way, step + 1)

            def take():
                self.copy(way, step, piece, block).wait_recv()
                if step + 2 < self.far:
                    self.copy(way, step + 1, piece, block).start()
                elif step + 2 == self.far:
                    onward = piece < half if way == 0 else piece >= half
                    if isinstance(onward, bool):
                        if onward:
                            self.copy(way, step + 1, piece, block).start()
                    else:
                        pl.when(onward)(lambda: self.copy(way, step + 1, piece, block).start())
                arrived(block, piece)

            self.guard(block, piece, take)

        for step in range(self.far):
            self.each(step, lambda way, piece: one(step, way, piece))

    def finish(self):
        def one(step, way, piece):
            block = self.block(way, step)
            self.guard(block, piece, lambda: self.copy(way, step, piece, block).wait_send())

        for step in range(self.far):
            self.each(step, lambda way, piece: one(step, way, piece))


def exchange_phase(
    sizes, a_ref, b_ref, g_ref, hid_ref, cot_ref, user_ref, inc_ref, w_all, h_all, c_all, i_all, ready,
    column, info, rs, rr, ls, lr, ys, yr, asend, arecv, lsem,
):
    n_s, n_z, n_x = sizes
    s, z, x = where_am_i()
    cols, rank = a_ref.shape
    micro, rows = user_ref.shape
    users = inc_ref.shape[0]
    gain = jnp.broadcast_to(g_ref[...].astype(F32), (rank, cols))
    column[z, :cols, :rank] = (a_ref[...].astype(F32) * gain.T).astype(BF)
    column[z, :cols, rank:] = b_ref[...].astype(F32).T.astype(BF)
    column[z, cols:, :] = jnp.broadcast_to(g_ref[...].astype(F32), (16, cols)).astype(BF)
    local = user_ref[...] - (z * n_x + x) * users
    included = jnp.zeros((micro, rows), F32)
    level = lax.broadcasted_iota(jnp.int32, (micro, rows), 0)
    for u in range(users):
        for m in range(micro):
            here = jnp.logical_and(local == u, level == m)
            included = jnp.where(here, inc_ref[u : u + 1, m : m + 1].astype(F32), included)
    key = (local + users * level).astype(F32)
    dev_rows = micro * rows
    lane = lax.broadcasted_iota(jnp.int32, (rows, dev_rows), 1)
    row = lax.broadcasted_iota(jnp.int32, (rows, dev_rows), 0)
    place = sum(jnp.where(lane == row + m * rows, 1.0, 0.0) for m in range(micro)).astype(BF)
    top = lax.broadcasted_iota(jnp.int32, (micro, dev_rows), 0)
    along = lax.broadcasted_iota(jnp.int32, (micro, dev_rows), 1)
    mine = jnp.logical_and(along >= top * rows, along < (top + 1) * rows)

    def flat(v):
        wide = mm(v.astype(BF), place, 1, 0)
        return jnp.sum(jnp.where(mine, wide, 0.0), 0, keepdims=True)

    which_row = lax.broadcasted_iota(jnp.int32, (16, dev_rows), 0)
    info[...] = jnp.where(which_row == 0, flat(key), flat(included)).astype(BF)
    ready()

    def act(which, to, slot):
        at = pl.ds(pl.multiple_of((s * n_x + to) * cols, cols), cols)
        src = (hid_ref.at[:, :, at], cot_ref.at[:, :, at], info)[which]
        dst = (h_all, c_all, i_all)[which].at[slot]
        return src, dst

    def a_copy(which, to, slot):
        src, dst = act(which, to, slot)
        return remote(src, dst, asend.at[which, to], arecv.at[which, slot], (s, z, to))

    split = cols // 2
    half = (slice(0, split), slice(split, cols + 16))

    def view(block, piece):
        return column.at[block, half[piece]]

    ring = Ring(n_z, z, lambda to: (s, to, x), view, 2, (rs, rr, ls, lr))
    ring.start()
    for which in range(3):
        for k in range(1, n_x):
            a_copy(which, lax.rem(x + k, n_x), x).start()
    for which in range(3):
        src, dst = act(which, x, x)
        pltpu.make_async_copy(src, dst, lsem.at[which]).start()

    def y_copy(block, slot, piece):
        return remote(
            column.at[block, half[piece]], w_all.at[slot, half[piece]],
            ys.at[block, piece], yr.at[slot, piece], (block, z, x),
        )

    def keep(piece):
        return pltpu.make_async_copy(
            column.at[s, half[piece]], w_all.at[s, half[piece]], lsem.at[3 + piece]
        )

    def onward(block, piece):
        @pl.when(block == s)
        def _():
            keep(piece).start()

        @pl.when(block != s)
        def _():
            y_copy(block, s, piece).start()

    for piece in (0, 1):
        onward(z, piece)
    ring.run(onward)
    for which in range(3):
        src, dst = act(which, x, x)
        pltpu.make_async_copy(src, dst, lsem.at[which]).wait()
        for k in range(1, n_x):
            a_copy(which, x, lax.rem(x + n_x - k, n_x)).wait_recv()

    def not_me(fn):
        def body(k):
            for piece in (0, 1):
                fn(lax.rem(s + 1 + k, n_s), piece)

        loop(n_s - 1, body)

    for piece in (0, 1):
        keep(piece).wait()
    not_me(lambda k, piece: y_copy(s, k, piece).wait_recv())

    def drain():
        not_me(lambda k, piece: y_copy(k, s, piece).wait_send())
        for which in range(3):
            for k in range(1, n_x):
                a_copy(which, lax.rem(x + k, n_x), x).wait_send()
        ring.finish()

    return drain


class Plane:
    def __init__(self, sizes):
        n_s, n_z, n_x = sizes
        self.n_x = n_x
        self.chips = (n_s // 2) * n_x
        self.s, self.z, self.x = where_am_i()
        self.core = lax.rem(self.s, 2)
        self.chip = (self.s // 2) * n_x + self.x
        self.partner = (self.s + 1 - 2 * self.core, self.z, self.x)

    def peer(self, chip):
        return (2 * (chip // self.n_x) + self.core, self.z, lax.rem(chip, self.n_x))

    def ahead(self, k):
        return lax.rem(self.chip + k, self.chips)

    def behind(self, k):
        return lax.rem(self.chip + self.chips - k, self.chips)

    def others(self, fn):
        loop(self.chips - 1, lambda k: fn(k + 1))

    def greet_all(self, barrier):
        def one(chip):
            s2, z2, x2 = self.peer(chip)
            pl.semaphore_signal(barrier, inc=1, device_id=(s2, z2, x2), device_id_type=MESH)
            pl.semaphore_signal(
                barrier, inc=1, device_id=(s2 + 1 - 2 * self.core, z2, x2), device_id_type=MESH
            )

        self.others(lambda k: one(self.ahead(k)))
        pl.semaphore_signal(barrier, inc=1, device_id=self.partner, device_id_type=MESH)
        return 2 * self.chips - 1


class Cast:
    def __init__(self, plane, view, sems):
        self.p, self.view, self.sems = plane, view, sems

    def far(self, chip, owner):
        send, recv = self.sems[0].at[chip], self.sems[1].at[owner]
        ref = self.view(owner, self.p.core)
        return remote(ref, ref, send, recv, self.p.peer(chip))

    def near(self, chip, core):
        ref = self.view(chip, core)
        return remote(ref, ref, self.sems[2].at[chip], self.sems[3].at[chip], self.p.partner)

    def start(self):
        p = self.p
        p.others(lambda k: self.far(p.ahead(k), p.chip).start())
        self.near(p.chip, p.core).start()

    def relay(self):
        p = self.p

        def one(k):
            chip = p.behind(k)
            self.far(chip, chip).wait_recv()
            self.near(chip, p.core).start()

        p.others(one)

    def finish(self):
        p = self.p
        loop(p.chips, lambda i: self.near(i, 1 - p.core).wait_recv())
        loop(p.chips, lambda i: self.near(i, p.core).wait_send())
        p.others(lambda k: self.far(p.ahead(k), p.chip).wait_send())


def solve_phase(
    sizes, dims, w_all, h_all, c_all, low_out, err_out,
    gsend, grecv, gram, pbuf, prev, psum, crev, state, snap, full, rin,
    gs, gr, rs, rr, ls, lr, ns, nr, ps, pr, cs, cr, m0, m1, m2, m3, l0, l1, l2, l3, e0, e1, e2, e3,
):
    n_s, n_z, n_x = sizes
    rows, cols, rank, width = dims
    layers = n_s
    own = rows // n_s
    part = rank // n_x
    p = Plane(sizes)
    mine = w_all[p.z, :cols, rank:]
    for l in range(layers):
        g = mm(mine, w_all[l, :cols], 0, 0).astype(BF)
        gsend[l] = g.reshape(n_x, part, 2 * rank)
    n_plane = 2 * p.chips
    me = p.s * n_x + p.x

    def g_copy(to, slot):
        return remote(
            gsend.at[to // n_x, lax.rem(to, n_x)], grecv.at[slot], gs.at[to], gr.at[slot],
            (to // n_x, p.z, lax.rem(to, n_x)),
        )

    loop(n_plane - 1, lambda k: g_copy(lax.rem(me + 1 + k, n_plane), me).start())
    for l in range(layers):
        for i in range(n_x):
            zy = mm(h_all[i].reshape(rows, cols), w_all[l, :cols], 1, 0).astype(BF)
            ct = mm(c_all[i].reshape(rows, cols), w_all[l, :cols, rank:], 1, 0).astype(BF)
            at = slice(i * n_s, (i + 1) * n_s)
            for c, value in enumerate((zy[:, :rank], zy[:, rank:], ct)):
                r0 = (c * layers + l) * own
                pbuf[at, r0 : r0 + own, :] = value.reshape(n_s, own, rank)
    for i in range(n_x):
        xf = h_all[i].reshape(rows, cols).astype(F32)
        sq = jnp.broadcast_to(jnp.sum(xf * xf, -1, keepdims=True), (rows, rank)).astype(BF)
        pbuf[i * n_s : (i + 1) * n_s, 3 * layers * own :, :] = sq.reshape(n_s, own, rank)

    def block(chip, core):
        return (2 * (chip // n_x) + core) * n_x + lax.rem(chip, n_x)

    def pre(i):
        return remote(pbuf.at[block(i, 1 - p.core)], prev.at[i], ps.at[i], pr.at[i], p.partner)

    def pre_wait(i):
        return remote(pbuf.at[block(i, p.core)], prev.at[i], ps.at[i], pr.at[i], p.partner)

    def c_copy(to, slot):
        return remote(psum.at[to], crev.at[slot], cs.at[to], cr.at[slot], p.peer(to))

    loop(p.chips, lambda k: pre(p.ahead(k)).start())

    early = (p.chips - 1) // 4

    def pair(k):
        i = p.ahead(k)
        pre_wait(i).wait_recv()
        total = pbuf[block(i, p.core)].astype(F32) + prev[i].astype(F32)
        psum[i] = total.astype(BF)

        @pl.when(jnp.logical_and(k >= 1, k <= early))
        def _():
            c_copy(i, p.chip).start()

    loop(p.chips, lambda k: pair(lax.rem(k + 1, p.chips)))

    loop(n_plane - 1, lambda k: g_copy(me, lax.rem(me + n_plane - 1 - k, n_plane)).wait_recv())
    grecv[me] = gsend[p.s, p.x]
    gsum = grecv[0].astype(F32)
    for k in range(1, n_plane):
        gsum = gsum + grecv[k].astype(F32)
    gram[0, p.z, p.s, p.x] = gsum[:, :rank].astype(BF)
    gram[1, p.z, p.s, p.x] = gsum[:, rank:].astype(BF)

    def gram_view(chip, core):
        return gram.at[:, p.z, 2 * (chip // n_x) + core, lax.rem(chip, n_x)]

    spread = Cast(p, gram_view, (m0, m1, m2, m3))
    spread.start()
    spread.relay()
    spread.finish()

    def gram_part(layer, piece, core):
        return gram.at[lax.rem(piece, 2), layer, 2 * (piece // 2) + core]

    def wanted(layer, piece, core):
        other = 2 * (piece // 2) + core
        upper = layer < other
        last = jnp.where(lax.rem(piece, 2) == 0, layer > other, layer == other)
        return jnp.logical_or(upper, last)

    ring = Ring(
        n_z, p.z, lambda to: (p.s, to, p.x), lambda layer, piece: gram_part(layer, piece, p.core),
        layers, (rs, rr, ls, lr), lambda layer, piece: wanted(layer, piece, p.core),
    )
    ring.start()

    loop(p.chips - 1 - early, lambda k: c_copy(p.ahead(k + 1 + early), p.chip).start())

    def share(layer, piece, core):
        ref = gram_part(layer, piece, core)
        return remote(ref, ref, ns.at[layer, piece], nr.at[layer, piece], p.partner)

    ring.run(lambda layer, piece: share(layer, piece, p.core).start())
    p.others(lambda k: c_copy(p.chip, p.behind(k)).wait_recv())
    crev[p.chip] = psum[p.chip]
    total = crev[0].astype(F32)
    for k in range(1, p.chips):
        total = total + crev[k].astype(F32)
    state[...] = total.reshape(3 * layers + 1, own, rank)

    def each_share(core, fn):
        def body(k):
            layer = lax.rem(p.z + 1 + k // layers, n_z)
            piece = lax.rem(k, layers)
            pl.when(wanted(layer, piece, core))(lambda: fn(share(layer, piece, core)))

        loop((n_z - 1) * layers, body)

    each_share(1 - p.core, lambda copy: copy.wait_recv())

    def low_view(chip, core):
        dev = block(chip, core)
        return low_out.at[:, pl.ds(pl.multiple_of(dev * own, own), own), :]

    def err_view(chip, core):
        dev = block(chip, core)
        return err_out.at[:, pl.ds(pl.multiple_of(dev * own, own), own), :]

    here = pl.ds(pl.multiple_of(me * own, own), own)
    square = state[3 * layers]
    zero = jnp.zeros((own, rank), F32)
    lane = lax.broadcasted_iota(jnp.int32, (own, rank), 1)
    scal = zero
    for l in range(layers):
        rinv = lax.rsqrt(square / width + 1e-05)
        u = state[l] * rinv
        low = u.astype(BF)
        full[l] = u
        rin[l] = rinv
        low_out[l, here, :] = low
        before = state[layers + l]
        for j in range(layers):
            snap[l, j] = state[layers + j]
            if j > l:
                pair_gram = jnp.concatenate(
                    [gram[0, l, j].reshape(rank, rank), gram[1, l, j].reshape(rank, rank)], 1
                )
                both = mm(low, pair_gram, 1, 0)
                state[j] = state[j] + both[:, :rank]
                state[layers + j] = state[layers + j] + both[:, rank:]
            else:
                one = mm(low, gram[1, j, l].reshape(rank, rank), 1, 1)
                state[layers + j] = state[layers + j] + one
        after = state[layers + l]
        square = square + jnp.sum(low.astype(F32) * (before + after), -1, keepdims=True)
        high = rinv.astype(BF).astype(F32)
        scal = jnp.where(lane == l, high, scal)
        scal = jnp.where(lane == layers + l, rinv - high, scal)
    low_out[layers, here, :] = scal.astype(BF)
    lows = Cast(p, low_view, (l0, l1, l2, l3))
    lows.start()
    scal = zero
    for l in range(layers - 1, -1, -1):
        err = state[2 * layers + l].astype(BF)
        mean = jnp.sum(err.astype(F32) * full[l], -1, keepdims=True) / width
        rinv = rin[l]
        cor = rinv * rinv * mean
        for j in range(l):
            back = mm(err, gram[0, j, l].reshape(rank, rank), 1, 1)
            state[2 * layers + j] = state[2 * layers + j] + rinv * back - cor * snap[l, j]
        err_out[l, here, :] = err
        scal = jnp.where(lane == l, cor, scal)
    err_out[layers, here, :] = scal.astype(BF)
    errs = Cast(p, err_view, (e0, e1, e2, e3))
    errs.start()
    lows.relay()
    lows.finish()

    def drain():
        loop(n_plane - 1, lambda k: g_copy(lax.rem(me + 1 + k, n_plane), me).wait_send())
        ring.finish()
        each_share(p.core, lambda copy: copy.wait_send())
        loop(p.chips, lambda k: pre(p.ahead(k)).wait_send())
        p.others(lambda k: c_copy(p.ahead(k), p.chip).wait_send())

    return drain, errs


def finish_phase(
    sizes, dims, bound, w_all, h_all, c_all, i_all, low_ref, err_ref, errs, grad_out, row_out,
    normed, deltas, hold, tot, gbuf, mid, acc, rbuf, lbuf, ts, tr, gs, gr, zs, zr, us, ur, lsem,
):
    n_s, n_z, n_x = sizes
    rows, cols, rank, width = dims
    layers = n_s
    p = Plane(sizes)
    s, z, x = p.s, p.z, p.x
    def factor(ref, i, l):
        return ref[layers, i * rows : (i + 1) * rows, l : l + 1].astype(F32)

    def rinv_of(i, l):
        return factor(low_ref, i, l) + factor(low_ref, i, layers + l)

    for i in range(n_x):
        at = slice(i * rows, (i + 1) * rows)
        h = h_all[i].reshape(rows, cols).astype(F32)
        for l in range(layers):
            gain = w_all[l, cols : cols + 8].astype(F32)[0:1, :]
            normed[l, at] = (h * rinv_of(i, l) * gain).astype(BF)
            hold[l, at] = h.astype(BF)
            if l + 1 < layers:
                h = h + mm(low_ref[l, at], w_all[l, :cols, rank:], 1, 1)
    errs.relay()
    errs.finish()
    sums = []
    for i in range(n_x):
        at = slice(i * rows, (i + 1) * rows)
        keyrow = i_all[i].astype(F32)[0:1, :]
        keys = jnp.broadcast_to(keyrow, (rows, rows))
        same = keys == keys.T
        pairs = jnp.zeros((rows, rows), F32)
        d = c_all[i].reshape(rows, cols).astype(F32)
        for l in range(layers - 1, -1, -1):
            db = d.astype(BF)
            deltas[l, at] = db
            lo, n, e = low_ref[l, at], normed[l, at], err_ref[l, at]
            pairs = pairs + mm(lo, lo, 1, 1) * mm(db, db, 1, 1)
            pairs = pairs + mm(n, n, 1, 1) * mm(e, e, 1, 1)
            if l > 0:
                d = d + rinv_of(i, l) * mm(e, w_all[l, :cols, :rank], 1, 1)
                d = d - factor(err_ref, i, l) * hold[l, at].astype(F32)
        pairs = jnp.where(same, pairs, 0.0)
        rowsum = jnp.broadcast_to(jnp.sum(pairs, -1, keepdims=True), (rows, rows))
        sums.append(jnp.sum(jnp.where(same, rowsum, 0.0), 0, keepdims=True))
    me = s * n_x + x
    n_plane = n_s * n_x
    pad = [jnp.zeros((8 - n_x, rows), F32)] if n_x < 8 else []
    tot[me] = jnp.concatenate(sums + pad, 0)

    def t_copy(to, slot):
        return remote(
            tot.at[slot], tot.at[slot], ts.at[to], tr.at[slot], (to // n_x, z, lax.rem(to, n_x))
        )

    loop(n_plane - 1, lambda k: t_copy(lax.rem(me + 1 + k, n_plane), me).start())
    loop(n_plane - 1, lambda k: t_copy(me, lax.rem(me + n_plane - 1 - k, n_plane)).wait_recv())
    total = tot[0]
    for k in range(1, n_plane):
        total = total + tot[k]
    clip = bound / jnp.maximum(jnp.sqrt(total), bound)

    weights = []
    for i in range(n_x):
        inc = i_all[i].astype(F32)[1:2, :]
        w = jnp.broadcast_to(inc * clip[i : i + 1], (rows, rows))
        weights.append(w.T[:, :rank])

        @pl.when(x == i)
        def _(w=w, i=i):
            row_out[0:1, :] = w[0:1, :]
            row_out[1:2, :] = i_all[i].astype(F32)[0:1, :]

    weight = jnp.concatenate(weights, 0)

    def g_copy(to, slot):
        return remote(gbuf.at[to], mid.at[slot], gs.at[to], gr.at[slot], (to, z, x))

    def keep():
        return pltpu.make_async_copy(gbuf.at[s], mid.at[s], lsem.at[0])

    def gradient(k):
        l = lax.rem(s + 1 + k, n_s)
        we = (weight * err_ref[l].astype(F32)).astype(BF)
        wl = (weight * low_ref[l].astype(F32)).astype(BF)
        gbuf[l, :, :rank] = mm(normed[l], we, 0, 0).astype(BF)
        gbuf[l, :, rank:] = mm(deltas[l], wl, 0, 0).astype(BF)

        @pl.when(s != l)
        def _():
            g_copy(l, s).start()

        @pl.when(s == l)
        def _():
            keep().start()

    loop(layers, gradient)

    def have(slot):
        @pl.when(slot == s)
        def _():
            keep().wait()

        @pl.when(slot != s)
        def _():
            g_copy(s, slot).wait_recv()

    far = n_z // 2
    halves = (slice(0, cols // 2), slice(cols // 2, cols))

    def hops(way, piece):
        return far if way == piece else far - 1

    def hop(way, step, piece, src):
        part = halves[piece]
        if step + 1 == hops(way, piece):
            dst = grad_out.at[1 + way, part]
        else:
            dst = (rbuf, lbuf)[way].at[step, part]
        send, recv = ((zs, zr), (us, ur))[way]
        to = lax.rem(z + (1, n_z - 1)[way], n_z)
        return remote(src, dst, send.at[step, piece], recv.at[step, piece], (s, to, x))

    def source(way, step, piece, slot):
        part = halves[piece]
        return mid.at[slot, part] if step == 0 else acc.at[way, step - 1, part]

    def slot_of(way, gap):
        return lax.rem(z + (gap if way == 0 else n_z - gap), n_z)

    seen = set()

    def need(gap):
        if gap % n_z not in seen:
            seen.add(gap % n_z)
            have(lax.rem(z + gap + n_z, n_z))

    for step in range(far):
        for piece in (0, 1):
            for way in (0, 1):
                if step >= hops(way, piece):
                    continue
                gap = hops(way, piece) - step
                need(gap if way == 0 else -gap)
                slot = slot_of(way, gap)
                part = halves[piece]
                src = source(way, step, piece, slot)
                if step > 0:
                    hop(way, step - 1, piece, source(way, step - 1, piece, slot)).wait_recv()
                    came = (rbuf, lbuf)[way][step - 1, part].astype(F32)
                    acc[way, step - 1, part] = (came + mid[slot, part].astype(F32)).astype(BF)
                hop(way, step, piece, src).start()
    need(0)
    grad_out[0] = mid[z]
    for way in (0, 1):
        for piece in (0, 1):
            step = hops(way, piece) - 1
            hop(way, step, piece, source(way, step, piece, z)).wait_recv()

    def drain():
        for way in (0, 1):
            for piece in (0, 1):
                for step in range(hops(way, piece)):
                    hop(way, step, piece, source(way, step, piece, z)).wait_send()
        loop(n_s - 1, lambda k: g_copy(lax.rem(s + 1 + k, n_s), s).wait_send())
        loop(n_plane - 1, lambda k: t_copy(lax.rem(me + 1 + k, n_plane), me).wait_send())

    return drain


def main_kernel(
    sizes, dims, bound, n_ex, n_so, a_ref, b_ref, g_ref, hid_ref, cot_ref, user_ref, inc_ref,
    grad_out, row_out, w_all, h_all, c_all, i_all, low, err, *scratch,
):
    n_s, n_z, n_x = sizes
    p = Plane(sizes)
    barrier = pltpu.get_barrier_semaphore()
    count = p.greet_all(barrier)
    for k in (1, n_z - 1):
        pl.semaphore_signal(
            barrier, inc=1, device_id=(p.s, lax.rem(p.z + k, n_z), p.x), device_id_type=MESH
        )
    first = exchange_phase(
        sizes, a_ref, b_ref, g_ref, hid_ref, cot_ref, user_ref, inc_ref, w_all, h_all, c_all, i_all,
        lambda: pl.semaphore_wait(barrier, count + 2), *scratch[:n_ex],
    )
    second, errs = solve_phase(sizes, dims, w_all, h_all, c_all, low, err, *scratch[n_ex : n_ex + n_so])
    third = finish_phase(
        sizes, dims, bound, w_all, h_all, c_all, i_all, low, err, errs, grad_out, row_out,
        *scratch[n_ex + n_so :],
    )
    first()
    second()
    third()


def main(sizes, dims, bound, a, b, g, hidden, cot, users, inc):
    n_s, n_z, n_x = sizes
    rows, cols, rank, width = dims
    layers = n_s
    chips = (n_s // 2) * n_x
    plane = n_s * n_x
    own = rows // n_s
    group = rows * n_x
    part = rank // n_x
    high = (3 * layers + 1) * own
    dma = pltpu.SemaphoreType.DMA
    v = pltpu.VMEM
    slab = (n_x, *hidden.shape[:2], cols)
    shared = [
        v((n_s, cols + 16, 2 * rank), BF),
        v(slab, BF),
        v(slab, BF),
        v((n_x, 16, rows), BF),
        v((layers + 1, group, rank), BF),
        v((layers + 1, group, rank), BF),
    ]
    ex = [
        v((n_z, cols + 16, 2 * rank), BF),
        v((16, rows), BF),
        dma((n_z, 2)), dma((n_z, 2)), dma((n_z, 2)), dma((n_z, 2)),
        dma((n_z, 2)), dma((n_s, 2)), dma((3, n_x)), dma((3, n_x)), dma((5,)),
    ]
    so = [
        v((n_s, n_x, part, 2 * rank), BF),
        v((plane, part, 2 * rank), BF),
        v((2, n_z, n_s, n_x, part, rank), BF),
        v((plane, high, rank), BF),
        v((chips, high, rank), BF),
        v((chips, high, rank), BF),
        v((chips, high, rank), BF),
        v((3 * layers + 1, own, rank), F32),
        v((layers, layers, own, rank), F32),
        v((layers, own, rank), F32),
        v((layers, own, rank), F32),
        dma((plane,)), dma((plane,)),
    ]
    so += [dma((n_z, layers))] * 6 + [dma((chips,))] * 16
    fi = [
        v((layers, group, cols), BF),
        v((layers, group, cols), BF),
        v((layers, group, cols), BF),
        v((plane, 8, rows), F32),
        v((layers, cols, 2 * rank), BF),
        v((n_s, cols, 2 * rank), BF),
        v((2, n_z // 2, cols, 2 * rank), BF),
        v((n_z // 2, cols, 2 * rank), BF),
        v((n_z // 2, cols, 2 * rank), BF),
        dma((plane,)), dma((plane,)), dma((n_s,)), dma((n_s,)),
    ]
    fi += [dma((n_z // 2, 2))] * 4 + [dma((1,))]
    return pl.pallas_call(
        functools.partial(main_kernel, sizes, dims, bound, len(ex), len(so)),
        out_shape=(
            jax.ShapeDtypeStruct((3, cols, 2 * rank), BF),
            jax.ShapeDtypeStruct((8, rows), F32),
        ),
        in_specs=[VMEM, VMEM, VMEM, ANY, ANY, VMEM, VMEM],
        out_specs=(VMEM, VMEM),
        scratch_shapes=shared + ex + so + fi,
        compiler_params=params(0),
        name="main",
    )(a, b, g, hidden, cot, users, inc)


def close_kernel(parts, row, gi_out, go_out, uw_out):
    rank = gi_out.shape[1]
    grad = parts[0].astype(F32) + parts[1].astype(F32) + parts[2].astype(F32)
    gi_out[...] = grad[:, :rank]
    go_out[...] = grad[:, rank:].T
    users, micro = uw_out.shape
    width = row.shape[1]
    weight = jnp.broadcast_to(row[0:1, :], (users, width))
    key = jnp.broadcast_to(row[1:2, :], (users, width))
    user = lax.broadcasted_iota(jnp.int32, (users, width), 0).astype(F32)
    lane = lax.broadcasted_iota(jnp.int32, (users, micro), 1)
    result = jnp.zeros((users, micro), F32)
    for m in range(micro):
        most = jnp.max(jnp.where(key == user + m * users, weight, 0.0), -1, keepdims=True)
        result = jnp.where(lane == m, most, result)
    uw_out[...] = result


def shards(hidden_in, cotangent, adapter_in, adapter_out, norm_gain, user_of_row, included):
    sizes = tuple(lax.axis_size(a) for a in ("section", "z", "x"))
    n_s = sizes[0]
    micro, rows, width = hidden_in.shape
    cols, rank = adapter_in.shape[1:]
    users = included.shape[1]
    bound = 0.8 * math.sqrt(n_s * (rows // users) * width * width)
    parts, row = main(
        sizes, (micro * rows, cols, rank, width), bound, adapter_in[0], adapter_out[0], norm_gain,
        hidden_in, cotangent, user_of_row, included.T,
    )
    gi, go, uw = pl.pallas_call(
        close_kernel,
        out_shape=(
            jax.ShapeDtypeStruct((cols, rank), F32),
            jax.ShapeDtypeStruct((rank, cols), F32),
            jax.ShapeDtypeStruct((users, micro), F32),
        ),
        in_specs=[VMEM, VMEM],
        out_specs=(VMEM,) * 3,
        name="close",
    )(parts, row)
    return (gi[None], go[None], uw.T)


def build(torus):
    dp = ("z", "x")
    return jax.shard_map(
        shards,
        mesh=torus,
        in_specs=(
            P(None, dp, None),
            P(None, dp, None),
            P("section", dp, None),
            P("section", None, dp),
            P("section", dp),
            P(None, dp),
            P(None, dp),
        ),
        out_specs=(P("section", dp, None), P("section", None, dp), P(None, dp)),
        check_vma=False,
    )


def solution(mesh):
    return build(Mesh(mesh.devices.reshape(mesh.shape["section"], 8, 4), ("section", "z", "x")))
```

```python
import functools
import math

import jax
import jax.numpy as jnp
from jax import lax
from jax.experimental import pallas as pl
from jax.experimental.pallas import tpu as pltpu
from jax.sharding import Mesh
from jax.sharding import PartitionSpec as P

F32 = jnp.float32
BF = jnp.bfloat16
MESH = pl.DeviceIdType.MESH
VMEM = pl.BlockSpec(memory_space=pltpu.VMEM)
ANY = pl.BlockSpec(memory_space=pl.ANY)
LIMIT = 60 * 1024 * 1024


def mm(a, b, ca, cb):
    return lax.dot_general(a, b, (((ca,), (cb,)), ((), ())), preferred_element_type=F32)


def loop(n, body):
    lax.fori_loop(0, n, lambda i, c: (body(i), c)[1], 0)


def remote(src, dst, send, recv, device):
    return pltpu.make_async_remote_copy(
        src_ref=src, dst_ref=dst, send_sem=send, recv_sem=recv, device_id=device, device_id_type=MESH
    )


def params(cid):
    return pltpu.CompilerParams(collective_id=cid, has_side_effects=True, vmem_limit_bytes=LIMIT)


def where_am_i():
    return tuple(lax.axis_index(a) for a in ("section", "z", "x"))


class Ring:
    def __init__(self, n, me, place, view, pieces, sems, want=None):
        self.n, self.me, self.place, self.view, self.pieces, self.sems = n, me, place, view, pieces, sems
        self.want = want
        self.far = n // 2

    def block(self, way, step):
        sign = 1 - 2 * way
        return lax.rem(self.me - sign * step + 2 * self.n, self.n)

    def copy(self, way, step, piece, block):
        sign = 1 - 2 * way
        ref = self.view(block, piece)
        send, recv = self.sems[2 * way].at[step, piece], self.sems[2 * way + 1].at[step, piece]
        return remote(ref, ref, send, recv, self.place(lax.rem(self.me + sign + self.n, self.n)))

    def guard(self, block, piece, fn):
        if self.want is None:
            fn()
        else:
            pl.when(self.want(block, piece))(fn)

    def each(self, step, fn):
        half = self.pieces // 2

        def body(i):
            if step + 1 < self.far:
                for way in (0, 1):
                    fn(way, i)
            else:
                fn(0, i)
                fn(1, i + half)

        count = self.pieces if step + 1 < self.far else half
        if self.want is None:
            for i in range(count):
                body(i)
        else:
            loop(count, body)

    def send(self, way, step, piece):
        block = self.block(way, step)
        self.guard(block, piece, lambda: self.copy(way, step, piece, block).start())

    def start(self):
        self.each(0, lambda way, piece: self.send(way, 0, piece))

    def run(self, arrived):
        half = self.pieces // 2

        def one(step, way, piece):
            block = self.block(way, step + 1)

            def take():
                self.copy(way, step, piece, block).wait_recv()
                if step + 2 < self.far:
                    self.copy(way, step + 1, piece, block).start()
                elif step + 2 == self.far:
                    onward = piece < half if way == 0 else piece >= half
                    if isinstance(onward, bool):
                        if onward:
                            self.copy(way, step + 1, piece, block).start()
                    else:
                        pl.when(onward)(lambda: self.copy(way, step + 1, piece, block).start())
                arrived(block, piece)

            self.guard(block, piece, take)

        for step in range(self.far):
            self.each(step, lambda way, piece: one(step, way, piece))

    def finish(self):
        def one(step, way, piece):
            block = self.block(way, step)
            self.guard(block, piece, lambda: self.copy(way, step, piece, block).wait_send())

        for step in range(self.far):
            self.each(step, lambda way, piece: one(step, way, piece))


def exchange_phase(
    sizes, a_ref, b_ref, g_ref, hid_ref, cot_ref, user_ref, inc_ref, w_all, h_all, c_all, i_all, ready,
    column, info, rs, rr, ls, lr, ys, yr, asend, arecv, lsem,
):
    n_s, n_z, n_x = sizes
    s, z, x = where_am_i()
    cols, rank = a_ref.shape
    micro, rows = user_ref.shape
    users = inc_ref.shape[0]
    gain = jnp.broadcast_to(g_ref[...].astype(F32), (rank, cols))
    column[z, :cols, :rank] = (a_ref[...].astype(F32) * gain.T).astype(BF)
    column[z, :cols, rank:] = b_ref[...].astype(F32).T.astype(BF)
    column[z, cols:, :] = jnp.broadcast_to(g_ref[...].astype(F32), (16, cols)).astype(BF)
    local = user_ref[...] - (z * n_x + x) * users
    included = jnp.zeros((micro, rows), F32)
    level = lax.broadcasted_iota(jnp.int32, (micro, rows), 0)
    for u in range(users):
        for m in range(micro):
            here = jnp.logical_and(local == u, level == m)
            included = jnp.where(here, inc_ref[u : u + 1, m : m + 1].astype(F32), included)
    key = (local + users * level).astype(F32)
    dev_rows = micro * rows
    lane = lax.broadcasted_iota(jnp.int32, (rows, dev_rows), 1)
    row = lax.broadcasted_iota(jnp.int32, (rows, dev_rows), 0)
    place = sum(jnp.where(lane == row + m * rows, 1.0, 0.0) for m in range(micro)).astype(BF)
    top = lax.broadcasted_iota(jnp.int32, (micro, dev_rows), 0)
    along = lax.broadcasted_iota(jnp.int32, (micro, dev_rows), 1)
    mine = jnp.logical_and(along >= top * rows, along < (top + 1) * rows)

    def flat(v):
        wide = mm(v.astype(BF), place, 1, 0)
        return jnp.sum(jnp.where(mine, wide, 0.0), 0, keepdims=True)

    which_row = lax.broadcasted_iota(jnp.int32, (16, dev_rows), 0)
    info[...] = jnp.where(which_row == 0, flat(key), flat(included)).astype(BF)
    ready()

    def act(which, to, slot):
        at = pl.ds(pl.multiple_of((s * n_x + to) * cols, cols), cols)
        src = (hid_ref.at[:, :, at], cot_ref.at[:, :, at], info)[which]
        dst = (h_all, c_all, i_all)[which].at[slot]
        return src, dst

    def a_copy(which, to, slot):
        src, dst = act(which, to, slot)
        return remote(src, dst, asend.at[which, to], arecv.at[which, slot], (s, z, to))

    split = cols // 2
    half = (slice(0, split), slice(split, cols + 16))

    def view(block, piece):
        return column.at[block, half[piece]]

    ring = Ring(n_z, z, lambda to: (s, to, x), view, 2, (rs, rr, ls, lr))
    ring.start()
    for which in range(3):
        for k in range(1, n_x):
            a_copy(which, lax.rem(x + k, n_x), x).start()
    for which in range(3):
        src, dst = act(which, x, x)
        pltpu.make_async_copy(src, dst, lsem.at[which]).start()

    def y_copy(block, slot, piece):
        return remote(
            column.at[block, half[piece]], w_all.at[slot, half[piece]],
            ys.at[block, piece], yr.at[slot, piece], (block, z, x),
        )

    def keep(piece):
        return pltpu.make_async_copy(
            column.at[s, half[piece]], w_all.at[s, half[piece]], lsem.at[3 + piece]
        )

    def onward(block, piece):
        @pl.when(block == s)
        def _():
            keep(piece).start()

        @pl.when(block != s)
        def _():
            y_copy(block, s, piece).start()

    for piece in (0, 1):
        onward(z, piece)
    ring.run(onward)
    for which in range(3):
        src, dst = act(which, x, x)
        pltpu.make_async_copy(src, dst, lsem.at[which]).wait()
        for k in range(1, n_x):
            a_copy(which, x, lax.rem(x + n_x - k, n_x)).wait_recv()

    def not_me(fn):
        def body(k):
            for piece in (0, 1):
                fn(lax.rem(s + 1 + k, n_s), piece)

        loop(n_s - 1, body)

    for piece in (0, 1):
        keep(piece).wait()
    not_me(lambda k, piece: y_copy(s, k, piece).wait_recv())

    def drain():
        not_me(lambda k, piece: y_copy(k, s, piece).wait_send())
        for which in range(3):
            for k in range(1, n_x):
                a_copy(which, lax.rem(x + k, n_x), x).wait_send()
        ring.finish()

    return drain


class Plane:
    def __init__(self, sizes):
        n_s, n_z, n_x = sizes
        self.n_x = n_x
        self.chips = (n_s // 2) * n_x
        self.s, self.z, self.x = where_am_i()
        self.core = lax.rem(self.s, 2)
        self.chip = (self.s // 2) * n_x + self.x
        self.partner = (self.s + 1 - 2 * self.core, self.z, self.x)

    def peer(self, chip):
        return (2 * (chip // self.n_x) + self.core, self.z, lax.rem(chip, self.n_x))

    def ahead(self, k):
        return lax.rem(self.chip + k, self.chips)

    def behind(self, k):
        return lax.rem(self.chip + self.chips - k, self.chips)

    def others(self, fn):
        loop(self.chips - 1, lambda k: fn(k + 1))

    def greet_all(self, barrier):
        def one(chip):
            s2, z2, x2 = self.peer(chip)
            pl.semaphore_signal(barrier, inc=1, device_id=(s2, z2, x2), device_id_type=MESH)
            pl.semaphore_signal(
                barrier, inc=1, device_id=(s2 + 1 - 2 * self.core, z2, x2), device_id_type=MESH
            )

        self.others(lambda k: one(self.ahead(k)))
        pl.semaphore_signal(barrier, inc=1, device_id=self.partner, device_id_type=MESH)
        return 2 * self.chips - 1


class Cast:
    def __init__(self, plane, view, sems):
        self.p, self.view, self.sems = plane, view, sems

    def far(self, chip, owner):
        send, recv = self.sems[0].at[chip], self.sems[1].at[owner]
        ref = self.view(owner, self.p.core)
        return remote(ref, ref, send, recv, self.p.peer(chip))

    def near(self, chip, core):
        ref = self.view(chip, core)
        return remote(ref, ref, self.sems[2].at[chip], self.sems[3].at[chip], self.p.partner)

    def start(self):
        p = self.p
        p.others(lambda k: self.far(p.ahead(k), p.chip).start())
        self.near(p.chip, p.core).start()

    def relay(self):
        p = self.p

        def one(k):
            chip = p.behind(k)
            self.far(chip, chip).wait_recv()
            self.near(chip, p.core).start()

        p.others(one)

    def finish(self):
        p = self.p
        loop(p.chips, lambda i: self.near(i, 1 - p.core).wait_recv())
        loop(p.chips, lambda i: self.near(i, p.core).wait_send())
        p.others(lambda k: self.far(p.ahead(k), p.chip).wait_send())


def solve_phase(
    sizes, dims, w_all, h_all, c_all, low_out, err_out,
    gsend, grecv, gram, pbuf, prev, psum, crev, state, snap, full, rin,
    gs, gr, rs, rr, ls, lr, ns, nr, ps, pr, cs, cr, m0, m1, m2, m3, k0, k1, k2, k3, l0, l1, l2, l3, e0, e1, e2, e3,
):
    n_s, n_z, n_x = sizes
    rows, cols, rank, width = dims
    layers = n_s
    own = rows // n_s
    part = rank // n_x
    split = (2 * layers + 1) * own
    p = Plane(sizes)
    mine = w_all[p.z, :cols, rank:]
    for l in range(layers):
        g = mm(mine, w_all[l, :cols], 0, 0).astype(BF)
        gsend[l] = g.reshape(n_x, part, 2 * rank)
    n_plane = 2 * p.chips
    me = p.s * n_x + p.x

    def g_copy(to, slot):
        return remote(
            gsend.at[to // n_x, lax.rem(to, n_x)], grecv.at[slot], gs.at[to], gr.at[slot],
            (to // n_x, p.z, lax.rem(to, n_x)),
        )

    loop(n_plane - 1, lambda k: g_copy(lax.rem(me + 1 + k, n_plane), me).start())
    for l in range(layers):
        for i in range(n_x):
            zy = mm(h_all[i].reshape(rows, cols), w_all[l, :cols], 1, 0).astype(BF)
            ct = mm(c_all[i].reshape(rows, cols), w_all[l, :cols, rank:], 1, 0).astype(BF)
            at = slice(i * n_s, (i + 1) * n_s)
            for c, value in enumerate((zy[:, :rank], zy[:, rank:], ct)):
                r0 = (c * layers + l + c // 2) * own
                pbuf[at, r0 : r0 + own, :] = value.reshape(n_s, own, rank)
    for i in range(n_x):
        xf = h_all[i].reshape(rows, cols).astype(F32)
        sq = jnp.broadcast_to(jnp.sum(xf * xf, -1, keepdims=True), (rows, rank)).astype(BF)
        pbuf[i * n_s : (i + 1) * n_s, 2 * layers * own : split, :] = sq.reshape(n_s, own, rank)

    def block(chip, core):
        return (2 * (chip // n_x) + core) * n_x + lax.rem(chip, n_x)

    def pre(i):
        return remote(pbuf.at[block(i, 1 - p.core)], prev.at[i], ps.at[i], pr.at[i], p.partner)

    def pre_wait(i):
        return remote(pbuf.at[block(i, p.core)], prev.at[i], ps.at[i], pr.at[i], p.partner)

    halves = (slice(0, split), slice(split, (3 * layers + 1) * own))

    def c_copy(to, slot, piece):
        return remote(
            psum.at[to, halves[piece]], crev.at[slot, halves[piece]],
            cs.at[to, piece], cr.at[slot, piece], p.peer(to),
        )

    loop(p.chips, lambda k: pre(p.ahead(k)).start())

    loop(n_plane - 1, lambda k: g_copy(me, lax.rem(me + n_plane - 1 - k, n_plane)).wait_recv())
    grecv[me] = gsend[p.s, p.x]
    gsum = grecv[0].astype(F32)
    for k in range(1, n_plane):
        gsum = gsum + grecv[k].astype(F32)
    gram[0, p.z, p.s, p.x] = gsum[:, :rank].astype(BF)
    gram[1, p.z, p.s, p.x] = gsum[:, rank:].astype(BF)

    def gram_view(chip, core):
        return gram.at[:, p.z, 2 * (chip // n_x) + core, lax.rem(chip, n_x)]

    spread = Cast(p, gram_view, (m0, m1, m2, m3))
    spread.start()
    spread.relay()
    spread.finish()

    def gram_part(layer, piece, core):
        return gram.at[lax.rem(piece, 2), layer, 2 * (piece // 2) + core]

    def wanted(layer, piece, core):
        other = 2 * (piece // 2) + core
        upper = layer < other
        last = jnp.where(lax.rem(piece, 2) == 0, layer > other, layer == other)
        return jnp.logical_or(upper, last)

    ring = Ring(
        n_z, p.z, lambda to: (p.s, to, p.x), lambda layer, piece: gram_part(layer, piece, p.core),
        layers, (rs, rr, ls, lr), lambda layer, piece: wanted(layer, piece, p.core),
    )
    ring.start()

    def pair(k):
        i = p.ahead(k)
        pre_wait(i).wait_recv()
        total = pbuf[block(i, p.core)].astype(F32) + prev[i].astype(F32)
        psum[i] = total.astype(BF)

        @pl.when(i != p.chip)
        def _():
            c_copy(i, p.chip, 0).start()

    loop(p.chips, lambda k: pair(lax.rem(k + 1, p.chips)))
    p.others(lambda k: c_copy(p.ahead(k), p.chip, 1).start())

    def share(layer, piece, core):
        ref = gram_part(layer, piece, core)
        return remote(ref, ref, ns.at[layer, piece], nr.at[layer, piece], p.partner)

    ring.run(lambda layer, piece: share(layer, piece, p.core).start())
    crev[p.chip] = psum[p.chip]

    def collect(piece, at):
        p.others(lambda k: c_copy(p.chip, p.behind(k), piece).wait_recv())
        total = crev[0, halves[piece]].astype(F32)
        for k in range(1, p.chips):
            total = total + crev[k, halves[piece]].astype(F32)
        state[at] = total.reshape(-1, own, rank)

    collect(0, slice(0, 2 * layers + 1))

    def each_share(core, fn):
        def body(k):
            layer = lax.rem(p.z + 1 + k // layers, n_z)
            piece = lax.rem(k, layers)
            pl.when(wanted(layer, piece, core))(lambda: fn(share(layer, piece, core)))

        loop((n_z - 1) * layers, body)

    each_share(1 - p.core, lambda copy: copy.wait_recv())

    mid = layers // 2

    def low_view(first, last):
        def view(chip, core):
            dev = block(chip, core)
            return low_out.at[first:last, pl.ds(pl.multiple_of(dev * own, own), own), :]

        return view

    early = Cast(p, low_view(0, mid), (k0, k1, k2, k3))
    lows = Cast(p, low_view(mid, layers + 1), (l0, l1, l2, l3))

    def err_view(chip, core):
        dev = block(chip, core)
        return err_out.at[:, pl.ds(pl.multiple_of(dev * own, own), own), :]

    here = pl.ds(pl.multiple_of(me * own, own), own)
    square = state[2 * layers]
    zero = jnp.zeros((own, rank), F32)
    lane = lax.broadcasted_iota(jnp.int32, (own, rank), 1)
    scal = zero
    for l in range(layers):
        rinv = lax.rsqrt(square / width + 1e-05)
        u = state[l] * rinv
        low = u.astype(BF)
        full[l] = u
        rin[l] = rinv
        low_out[l, here, :] = low
        before = state[layers + l]
        for j in range(layers):
            snap[l, j] = state[layers + j]
            if j > l:
                pair_gram = jnp.concatenate(
                    [gram[0, l, j].reshape(rank, rank), gram[1, l, j].reshape(rank, rank)], 1
                )
                both = mm(low, pair_gram, 1, 0)
                state[j] = state[j] + both[:, :rank]
                state[layers + j] = state[layers + j] + both[:, rank:]
            else:
                one = mm(low, gram[1, j, l].reshape(rank, rank), 1, 1)
                state[layers + j] = state[layers + j] + one
        after = state[layers + l]
        square = square + jnp.sum(low.astype(F32) * (before + after), -1, keepdims=True)
        high = rinv.astype(BF).astype(F32)
        scal = jnp.where(lane == l, high, scal)
        scal = jnp.where(lane == layers + l, rinv - high, scal)
        if l == mid - 1:
            early.start()
    low_out[layers, here, :] = scal.astype(BF)
    lows.start()
    early.relay()
    collect(1, slice(2 * layers + 1, 3 * layers + 1))
    scal = zero
    for l in range(layers - 1, -1, -1):
        err = state[2 * layers + 1 + l].astype(BF)
        mean = jnp.sum(err.astype(F32) * full[l], -1, keepdims=True) / width
        rinv = rin[l]
        cor = rinv * rinv * mean
        for j in range(l):
            back = mm(err, gram[0, j, l].reshape(rank, rank), 1, 1)
            state[2 * layers + 1 + j] = state[2 * layers + 1 + j] + rinv * back - cor * snap[l, j]
        err_out[l, here, :] = err
        scal = jnp.where(lane == l, cor, scal)
    err_out[layers, here, :] = scal.astype(BF)
    errs = Cast(p, err_view, (e0, e1, e2, e3))
    errs.start()
    lows.relay()
    early.finish()
    lows.finish()

    def drain():
        loop(n_plane - 1, lambda k: g_copy(lax.rem(me + 1 + k, n_plane), me).wait_send())
        ring.finish()
        each_share(p.core, lambda copy: copy.wait_send())
        loop(p.chips, lambda k: pre(p.ahead(k)).wait_send())
        p.others(lambda k: c_copy(p.ahead(k), p.chip, 0).wait_send())
        p.others(lambda k: c_copy(p.ahead(k), p.chip, 1).wait_send())

    return drain, errs


def finish_phase(
    sizes, dims, bound, w_all, h_all, c_all, i_all, low_ref, err_ref, errs, grad_out, row_out,
    normed, deltas, hold, tot, gbuf, mid, acc, rbuf, lbuf, ts, tr, gs, gr, zs, zr, us, ur, lsem,
):
    n_s, n_z, n_x = sizes
    rows, cols, rank, width = dims
    layers = n_s
    p = Plane(sizes)
    s, z, x = p.s, p.z, p.x
    def factor(ref, i, l):
        return ref[layers, i * rows : (i + 1) * rows, l : l + 1].astype(F32)

    def rinv_of(i, l):
        return factor(low_ref, i, l) + factor(low_ref, i, layers + l)

    errs.relay()
    errs.finish()
    for i in range(n_x):
        at = slice(i * rows, (i + 1) * rows)
        h = h_all[i].reshape(rows, cols).astype(F32)
        for l in range(layers):
            gain = w_all[l, cols : cols + 8].astype(F32)[0:1, :]
            normed[l, at] = (h * rinv_of(i, l) * gain).astype(BF)
            hold[l, at] = h.astype(BF)
            if l + 1 < layers:
                h = h + mm(low_ref[l, at], w_all[l, :cols, rank:], 1, 1)
    sums = []
    for i in range(n_x):
        at = slice(i * rows, (i + 1) * rows)
        keyrow = i_all[i].astype(F32)[0:1, :]
        keys = jnp.broadcast_to(keyrow, (rows, rows))
        same = keys == keys.T
        pairs = jnp.zeros((rows, rows), F32)
        d = c_all[i].reshape(rows, cols).astype(F32)
        for l in range(layers - 1, -1, -1):
            db = d.astype(BF)
            deltas[l, at] = db
            lo, n, e = low_ref[l, at], normed[l, at], err_ref[l, at]
            pairs = pairs + mm(lo, lo, 1, 1) * mm(db, db, 1, 1)
            pairs = pairs + mm(n, n, 1, 1) * mm(e, e, 1, 1)
            if l > 0:
                d = d + rinv_of(i, l) * mm(e, w_all[l, :cols, :rank], 1, 1)
                d = d - factor(err_ref, i, l) * hold[l, at].astype(F32)
        pairs = jnp.where(same, pairs, 0.0)
        rowsum = jnp.broadcast_to(jnp.sum(pairs, -1, keepdims=True), (rows, rows))
        sums.append(jnp.sum(jnp.where(same, rowsum, 0.0), 0, keepdims=True))
    me = s * n_x + x
    n_plane = n_s * n_x
    pad = [jnp.zeros((8 - n_x, rows), F32)] if n_x < 8 else []
    tot[me] = jnp.concatenate(sums + pad, 0)

    def t_copy(to, slot):
        return remote(
            tot.at[slot], tot.at[slot], ts.at[to], tr.at[slot], (to // n_x, z, lax.rem(to, n_x))
        )

    loop(n_plane - 1, lambda k: t_copy(lax.rem(me + 1 + k, n_plane), me).start())
    loop(n_plane - 1, lambda k: t_copy(me, lax.rem(me + n_plane - 1 - k, n_plane)).wait_recv())
    total = tot[0]
    for k in range(1, n_plane):
        total = total + tot[k]
    clip = bound / jnp.maximum(jnp.sqrt(total), bound)

    weights = []
    for i in range(n_x):
        inc = i_all[i].astype(F32)[1:2, :]
        w = jnp.broadcast_to(inc * clip[i : i + 1], (rows, rows))
        weights.append(w.T[:, :rank])

        @pl.when(x == i)
        def _(w=w, i=i):
            row_out[0:1, :] = w[0:1, :]
            row_out[1:2, :] = i_all[i].astype(F32)[0:1, :]

    weight = jnp.concatenate(weights, 0)

    def g_copy(to, slot):
        return remote(gbuf.at[to], mid.at[slot], gs.at[to], gr.at[slot], (to, z, x))

    def keep():
        return pltpu.make_async_copy(gbuf.at[s], mid.at[s], lsem.at[0])

    gap_here = lax.rem(s + n_z - z, n_z)
    soon = jnp.logical_and(gap_here >= n_z // 2 - 1, gap_here <= n_z // 2 + 1)

    def gradient(l):
        we = (weight * err_ref[l].astype(F32)).astype(BF)
        wl = (weight * low_ref[l].astype(F32)).astype(BF)
        gbuf[l, :, :rank] = mm(normed[l], we, 0, 0).astype(BF)
        gbuf[l, :, rank:] = mm(deltas[l], wl, 0, 0).astype(BF)

        @pl.when(s != l)
        def _():
            g_copy(l, s).start()

        @pl.when(s == l)
        def _():
            keep().start()

    loop(layers, gradient)

    def have(slot):
        @pl.when(slot == s)
        def _():
            keep().wait()

        @pl.when(slot != s)
        def _():
            g_copy(s, slot).wait_recv()

    far = n_z // 2
    halves = (slice(0, cols // 2), slice(cols // 2, cols))

    def hops(way, piece):
        return far if way == piece else far - 1

    def hop(way, step, piece, src):
        part = halves[piece]
        if step + 1 == hops(way, piece):
            dst = grad_out.at[1 + way, part]
        else:
            dst = (rbuf, lbuf)[way].at[step, part]
        send, recv = ((zs, zr), (us, ur))[way]
        to = lax.rem(z + (1, n_z - 1)[way], n_z)
        return remote(src, dst, send.at[step, piece], recv.at[step, piece], (s, to, x))

    def source(way, step, piece, slot):
        part = halves[piece]
        return mid.at[slot, part] if step == 0 else acc.at[way, step - 1, part]

    def slot_of(way, gap):
        return lax.rem(z + (gap if way == 0 else n_z - gap), n_z)

    seen = set()

    def need(gap):
        if gap % n_z not in seen:
            seen.add(gap % n_z)
            have(lax.rem(z + gap + n_z, n_z))

    for step in range(far):
        for piece in (0, 1):
            for way in (0, 1):
                if step >= hops(way, piece):
                    continue
                gap = hops(way, piece) - step
                need(gap if way == 0 else -gap)
                slot = slot_of(way, gap)
                part = halves[piece]
                src = source(way, step, piece, slot)
                if step > 0:
                    hop(way, step - 1, piece, source(way, step - 1, piece, slot)).wait_recv()
                    came = (rbuf, lbuf)[way][step - 1, part].astype(F32)
                    acc[way, step - 1, part] = (came + mid[slot, part].astype(F32)).astype(BF)
                hop(way, step, piece, src).start()
        if step == 0:

            pass

    need(0)
    grad_out[0] = mid[z]
    for way in (0, 1):
        for piece in (0, 1):
            step = hops(way, piece) - 1
            hop(way, step, piece, source(way, step, piece, z)).wait_recv()

    def drain():
        for way in (0, 1):
            for piece in (0, 1):
                for step in range(hops(way, piece)):
                    hop(way, step, piece, source(way, step, piece, z)).wait_send()
        loop(n_s - 1, lambda k: g_copy(lax.rem(s + 1 + k, n_s), s).wait_send())
        loop(n_plane - 1, lambda k: t_copy(lax.rem(me + 1 + k, n_plane), me).wait_send())

    return drain


def main_kernel(
    sizes, dims, bound, n_ex, n_so, a_ref, b_ref, g_ref, hid_ref, cot_ref, user_ref, inc_ref,
    grad_out, row_out, w_all, h_all, c_all, i_all, low, err, *scratch,
):
    n_s, n_z, n_x = sizes
    p = Plane(sizes)
    barrier = pltpu.get_barrier_semaphore()
    count = p.greet_all(barrier)
    for k in (1, n_z - 1):
        pl.semaphore_signal(
            barrier, inc=1, device_id=(p.s, lax.rem(p.z + k, n_z), p.x), device_id_type=MESH
        )
    first = exchange_phase(
        sizes, a_ref, b_ref, g_ref, hid_ref, cot_ref, user_ref, inc_ref, w_all, h_all, c_all, i_all,
        lambda: pl.semaphore_wait(barrier, count + 2), *scratch[:n_ex],
    )
    second, errs = solve_phase(sizes, dims, w_all, h_all, c_all, low, err, *scratch[n_ex : n_ex + n_so])
    third = finish_phase(
        sizes, dims, bound, w_all, h_all, c_all, i_all, low, err, errs, grad_out, row_out,
        *scratch[n_ex + n_so :],
    )
    first()
    second()
    third()


def main(sizes, dims, bound, a, b, g, hidden, cot, users, inc):
    n_s, n_z, n_x = sizes
    rows, cols, rank, width = dims
    layers = n_s
    chips = (n_s // 2) * n_x
    plane = n_s * n_x
    own = rows // n_s
    group = rows * n_x
    part = rank // n_x
    high = (3 * layers + 1) * own
    dma = pltpu.SemaphoreType.DMA
    v = pltpu.VMEM
    slab = (n_x, *hidden.shape[:2], cols)
    shared = [
        v((n_s, cols + 16, 2 * rank), BF),
        v(slab, BF),
        v(slab, BF),
        v((n_x, 16, rows), BF),
        v((layers + 1, group, rank), BF),
        v((layers + 1, group, rank), BF),
    ]
    ex = [
        v((n_z, cols + 16, 2 * rank), BF),
        v((16, rows), BF),
        dma((n_z, 2)), dma((n_z, 2)), dma((n_z, 2)), dma((n_z, 2)),
        dma((n_z, 2)), dma((n_s, 2)), dma((3, n_x)), dma((3, n_x)), dma((5,)),
    ]
    so = [
        v((n_s, n_x, part, 2 * rank), BF),
        v((plane, part, 2 * rank), BF),
        v((2, n_z, n_s, n_x, part, rank), BF),
        v((plane, high, rank), BF),
        v((chips, high, rank), BF),
        v((chips, high, rank), BF),
        v((chips, high, rank), BF),
        v((3 * layers + 1, own, rank), F32),
        v((layers, layers, own, rank), F32),
        v((layers, own, rank), F32),
        v((layers, own, rank), F32),
        dma((plane,)), dma((plane,)),
    ]
    so += [dma((n_z, layers))] * 6 + [dma((chips,))] * 2 + [dma((chips, 2))] * 2 + [dma((chips,))] * 16
    fi = [
        v((layers, group, cols), BF),
        v((layers, group, cols), BF),
        v((layers, group, cols), BF),
        v((plane, 8, rows), F32),
        v((layers, cols, 2 * rank), BF),
        v((n_s, cols, 2 * rank), BF),
        v((2, n_z // 2, cols, 2 * rank), BF),
        v((n_z // 2, cols, 2 * rank), BF),
        v((n_z // 2, cols, 2 * rank), BF),
        dma((plane,)), dma((plane,)), dma((n_s,)), dma((n_s,)),
    ]
    fi += [dma((n_z // 2, 2))] * 4 + [dma((1,))]
    return pl.pallas_call(
        functools.partial(main_kernel, sizes, dims, bound, len(ex), len(so)),
        out_shape=(
            jax.ShapeDtypeStruct((3, cols, 2 * rank), BF),
            jax.ShapeDtypeStruct((8, rows), F32),
        ),
        in_specs=[VMEM, VMEM, VMEM, ANY, ANY, VMEM, VMEM],
        out_specs=(VMEM, VMEM),
        scratch_shapes=shared + ex + so + fi,
        compiler_params=params(0),
        name="main",
    )(a, b, g, hidden, cot, users, inc)


def close_kernel(parts, row, gi_out, go_out, uw_out):
    rank = gi_out.shape[1]
    grad = parts[0].astype(F32) + parts[1].astype(F32) + parts[2].astype(F32)
    gi_out[...] = grad[:, :rank]
    go_out[...] = grad[:, rank:].T
    users, micro = uw_out.shape
    width = row.shape[1]
    weight = jnp.broadcast_to(row[0:1, :], (users, width))
    key = jnp.broadcast_to(row[1:2, :], (users, width))
    user = lax.broadcasted_iota(jnp.int32, (users, width), 0).astype(F32)
    lane = lax.broadcasted_iota(jnp.int32, (users, micro), 1)
    result = jnp.zeros((users, micro), F32)
    for m in range(micro):
        most = jnp.max(jnp.where(key == user + m * users, weight, 0.0), -1, keepdims=True)
        result = jnp.where(lane == m, most, result)
    uw_out[...] = result


def shards(hidden_in, cotangent, adapter_in, adapter_out, norm_gain, user_of_row, included):
    sizes = tuple(lax.axis_size(a) for a in ("section", "z", "x"))
    n_s = sizes[0]
    micro, rows, width = hidden_in.shape
    cols, rank = adapter_in.shape[1:]
    users = included.shape[1]
    bound = 0.8 * math.sqrt(n_s * (rows // users) * width * width)
    parts, row = main(
        sizes, (micro * rows, cols, rank, width), bound, adapter_in[0], adapter_out[0], norm_gain,
        hidden_in, cotangent, user_of_row, included.T,
    )
    gi, go, uw = pl.pallas_call(
        close_kernel,
        out_shape=(
            jax.ShapeDtypeStruct((cols, rank), F32),
            jax.ShapeDtypeStruct((rank, cols), F32),
            jax.ShapeDtypeStruct((users, micro), F32),
        ),
        in_specs=[VMEM, VMEM],
        out_specs=(VMEM,) * 3,
        name="close",
    )(parts, row)
    return (gi[None], go[None], uw.T)


def build(torus):
    dp = ("z", "x")
    return jax.shard_map(
        shards,
        mesh=torus,
        in_specs=(
            P(None, dp, None),
            P(None, dp, None),
            P("section", dp, None),
            P("section", None, dp),
            P("section", dp),
            P(None, dp),
            P(None, dp),
        ),
        out_specs=(P("section", dp, None), P("section", None, dp), P(None, dp)),
        check_vma=False,
    )


def solution(mesh):
    return build(Mesh(mesh.devices.reshape(mesh.shape["section"], 8, 4), ("section", "z", "x")))
```

```python
import functools
import math

import jax
import jax.numpy as jnp
from jax import lax
from jax.experimental import pallas as pl
from jax.experimental.pallas import tpu as pltpu
from jax.sharding import Mesh
from jax.sharding import PartitionSpec as P

F32 = jnp.float32
BF = jnp.bfloat16
MESH = pl.DeviceIdType.MESH
VMEM = pl.BlockSpec(memory_space=pltpu.VMEM)
ANY = pl.BlockSpec(memory_space=pl.ANY)
LIMIT = 60 * 1024 * 1024
PIECES = 4
WAVES = 2


def mm(a, b, ca, cb):
    return lax.dot_general(a, b, (((ca,), (cb,)), ((), ())), preferred_element_type=F32)


def loop(n, body):
    lax.fori_loop(0, n, lambda i, c: (body(i), c)[1], 0)


def remote(src, dst, send, recv, device):
    return pltpu.make_async_remote_copy(
        src_ref=src, dst_ref=dst, send_sem=send, recv_sem=recv, device_id=device, device_id_type=MESH
    )


def params(cid):
    return pltpu.CompilerParams(collective_id=cid, has_side_effects=True, vmem_limit_bytes=LIMIT)


def where_am_i():
    return tuple(lax.axis_index(a) for a in ("section", "z", "x"))


class Ring:
    def __init__(self, n, me, place, view, pieces, sems, want=None):
        self.n, self.me, self.place, self.view, self.pieces, self.sems = n, me, place, view, pieces, sems
        self.want = want
        self.far = n // 2

    def block(self, way, step):
        sign = 1 - 2 * way
        return lax.rem(self.me - sign * step + 2 * self.n, self.n)

    def copy(self, way, step, piece, block):
        sign = 1 - 2 * way
        ref = self.view(block, piece)
        send, recv = self.sems[2 * way].at[step, piece], self.sems[2 * way + 1].at[step, piece]
        return remote(ref, ref, send, recv, self.place(lax.rem(self.me + sign + self.n, self.n)))

    def guard(self, block, piece, fn):
        if self.want is None:
            fn()
        else:
            pl.when(self.want(block, piece))(fn)

    def each(self, step, fn):
        half = self.pieces // 2

        def body(i):
            if step + 1 < self.far:
                for way in (0, 1):
                    fn(way, i)
            else:
                fn(0, i)
                fn(1, i + half)

        count = self.pieces if step + 1 < self.far else half
        if self.want is None:
            for i in range(count):
                body(i)
        else:
            loop(count, body)

    def send(self, way, step, piece):
        block = self.block(way, step)
        self.guard(block, piece, lambda: self.copy(way, step, piece, block).start())

    def start(self):
        self.each(0, lambda way, piece: self.send(way, 0, piece))

    def run(self, arrived):
        half = self.pieces // 2

        def one(step, way, piece):
            block = self.block(way, step + 1)

            def take():
                self.copy(way, step, piece, block).wait_recv()
                if step + 2 < self.far:
                    self.copy(way, step + 1, piece, block).start()
                elif step + 2 == self.far:
                    onward = piece < half if way == 0 else piece >= half
                    if isinstance(onward, bool):
                        if onward:
                            self.copy(way, step + 1, piece, block).start()
                    else:
                        pl.when(onward)(lambda: self.copy(way, step + 1, piece, block).start())
                arrived(block, piece)

            self.guard(block, piece, take)

        for step in range(self.far):
            self.each(step, lambda way, piece: one(step, way, piece))

    def finish(self):
        def one(step, way, piece):
            block = self.block(way, step)
            self.guard(block, piece, lambda: self.copy(way, step, piece, block).wait_send())

        for step in range(self.far):
            self.each(step, lambda way, piece: one(step, way, piece))


def exchange_phase(
    sizes, a_ref, b_ref, g_ref, hid_ref, cot_ref, user_ref, inc_ref, w_all, h_all, c_all, i_all, ready,
    column, info, rs, rr, ls, lr, ys, yr, asend, arecv, lsem,
):
    n_s, n_z, n_x = sizes
    s, z, x = where_am_i()
    cols, rank = a_ref.shape
    micro, rows = user_ref.shape
    users = inc_ref.shape[0]
    gain = jnp.broadcast_to(g_ref[...].astype(F32), (rank, cols))
    column[z, :cols, :rank] = (a_ref[...].astype(F32) * gain.T).astype(BF)
    column[z, :cols, rank:] = b_ref[...].astype(F32).T.astype(BF)
    column[z, cols:, :] = jnp.broadcast_to(g_ref[...].astype(F32), (16, cols)).astype(BF)
    local = user_ref[...] - (z * n_x + x) * users
    included = jnp.zeros((micro, rows), F32)
    level = lax.broadcasted_iota(jnp.int32, (micro, rows), 0)
    for u in range(users):
        for m in range(micro):
            here = jnp.logical_and(local == u, level == m)
            included = jnp.where(here, inc_ref[u : u + 1, m : m + 1].astype(F32), included)
    key = (local + users * level).astype(F32)
    dev_rows = micro * rows
    lane = lax.broadcasted_iota(jnp.int32, (rows, dev_rows), 1)
    row = lax.broadcasted_iota(jnp.int32, (rows, dev_rows), 0)
    place = sum(jnp.where(lane == row + m * rows, 1.0, 0.0) for m in range(micro)).astype(BF)
    top = lax.broadcasted_iota(jnp.int32, (micro, dev_rows), 0)
    along = lax.broadcasted_iota(jnp.int32, (micro, dev_rows), 1)
    mine = jnp.logical_and(along >= top * rows, along < (top + 1) * rows)

    def flat(v):
        wide = mm(v.astype(BF), place, 1, 0)
        return jnp.sum(jnp.where(mine, wide, 0.0), 0, keepdims=True)

    which_row = lax.broadcasted_iota(jnp.int32, (16, dev_rows), 0)
    info[...] = jnp.where(which_row == 0, flat(key), flat(included)).astype(BF)
    ready()

    def act(which, to, slot):
        at = pl.ds(pl.multiple_of((s * n_x + to) * cols, cols), cols)
        src = (hid_ref.at[:, :, at], cot_ref.at[:, :, at], info)[which]
        dst = (h_all, c_all, i_all)[which].at[slot]
        return src, dst

    def a_copy(which, to, slot):
        src, dst = act(which, to, slot)
        return remote(src, dst, asend.at[which, to], arecv.at[which, slot], (s, z, to))

    step = cols // PIECES
    half = [slice(i * step, (i + 1) * step) for i in range(PIECES - 1)]
    half.append(slice((PIECES - 1) * step, cols + 16))

    def view(block, piece):
        return column.at[block, half[piece]]

    ring = Ring(n_z, z, lambda to: (s, to, x), view, PIECES, (rs, rr, ls, lr))
    ring.start()
    for which in range(3):
        for k in range(1, n_x):
            a_copy(which, lax.rem(x + k, n_x), x).start()
    for which in range(3):
        src, dst = act(which, x, x)
        pltpu.make_async_copy(src, dst, lsem.at[which]).start()

    def y_copy(block, slot, piece):
        return remote(
            column.at[block, half[piece]], w_all.at[slot, half[piece]],
            ys.at[block, piece], yr.at[slot, piece], (block, z, x),
        )

    def keep(piece):
        return pltpu.make_async_copy(
            column.at[s, half[piece]], w_all.at[s, half[piece]], lsem.at[3 + piece]
        )

    def onward(block, piece):
        @pl.when(block == s)
        def _():
            keep(piece).start()

        @pl.when(block != s)
        def _():
            y_copy(block, s, piece).start()

    for piece in range(PIECES):
        onward(z, piece)
    ring.run(onward)
    for which in range(3):
        src, dst = act(which, x, x)
        pltpu.make_async_copy(src, dst, lsem.at[which]).wait()
        for k in range(1, n_x):
            a_copy(which, x, lax.rem(x + n_x - k, n_x)).wait_recv()

    def not_me(fn):
        def body(k):
            for piece in range(PIECES):
                fn(lax.rem(s + 1 + k, n_s), piece)

        loop(n_s - 1, body)

    for piece in range(PIECES):
        keep(piece).wait()
    not_me(lambda k, piece: y_copy(s, k, piece).wait_recv())

    def drain():
        not_me(lambda k, piece: y_copy(k, s, piece).wait_send())
        for which in range(3):
            for k in range(1, n_x):
                a_copy(which, lax.rem(x + k, n_x), x).wait_send()
        ring.finish()

    return drain


class Plane:
    def __init__(self, sizes):
        n_s, n_z, n_x = sizes
        self.n_x = n_x
        self.chips = (n_s // 2) * n_x
        self.s, self.z, self.x = where_am_i()
        self.core = lax.rem(self.s, 2)
        self.chip = (self.s // 2) * n_x + self.x
        self.partner = (self.s + 1 - 2 * self.core, self.z, self.x)

    def peer(self, chip):
        return (2 * (chip // self.n_x) + self.core, self.z, lax.rem(chip, self.n_x))

    def ahead(self, k):
        return lax.rem(self.chip + k, self.chips)

    def behind(self, k):
        return lax.rem(self.chip + self.chips - k, self.chips)

    def others(self, fn):
        loop(self.chips - 1, lambda k: fn(k + 1))

    def greet_all(self, barrier):
        def one(chip):
            s2, z2, x2 = self.peer(chip)
            pl.semaphore_signal(barrier, inc=1, device_id=(s2, z2, x2), device_id_type=MESH)
            pl.semaphore_signal(
                barrier, inc=1, device_id=(s2 + 1 - 2 * self.core, z2, x2), device_id_type=MESH
            )

        self.others(lambda k: one(self.ahead(k)))
        pl.semaphore_signal(barrier, inc=1, device_id=self.partner, device_id_type=MESH)
        return 2 * self.chips - 1


class Cast:
    def __init__(self, plane, view, sems):
        self.p, self.view, self.sems = plane, view, sems

    def far(self, chip, owner):
        send, recv = self.sems[0].at[chip], self.sems[1].at[owner]
        ref = self.view(owner, self.p.core)
        return remote(ref, ref, send, recv, self.p.peer(chip))

    def near(self, chip, core):
        ref = self.view(chip, core)
        return remote(ref, ref, self.sems[2].at[chip], self.sems[3].at[chip], self.p.partner)

    def start(self):
        p = self.p
        p.others(lambda k: self.far(p.ahead(k), p.chip).start())
        self.near(p.chip, p.core).start()

    def relay(self):
        p = self.p

        def one(k):
            chip = p.behind(k)
            self.far(chip, chip).wait_recv()
            self.near(chip, p.core).start()

        p.others(one)

    def finish(self):
        p = self.p
        loop(p.chips, lambda i: self.near(i, 1 - p.core).wait_recv())
        loop(p.chips, lambda i: self.near(i, p.core).wait_send())
        p.others(lambda k: self.far(p.ahead(k), p.chip).wait_send())


def solve_phase(
    sizes, dims, w_all, h_all, c_all, low_out, err_out,
    gsend, grecv, gram, pbuf, prev, psum, crev, state, snap, full, rin,
    gs, gr, rs, rr, ls, lr, ns, nr, ps, pr, cs, cr, m0, m1, m2, m3, k0, k1, k2, k3, l0, l1, l2, l3, e0, e1, e2, e3,
):
    n_s, n_z, n_x = sizes
    rows, cols, rank, width = dims
    layers = n_s
    own = rows // n_s
    part = rank // n_x
    split = (2 * layers + 1) * own
    p = Plane(sizes)
    mine = w_all[p.z, :cols, rank:]
    for l in range(layers):
        g = mm(mine, w_all[l, :cols], 0, 0).astype(BF)
        gsend[l] = g.reshape(n_x, part, 2 * rank)
    n_plane = 2 * p.chips
    me = p.s * n_x + p.x

    def g_copy(to, slot):
        return remote(
            gsend.at[to // n_x, lax.rem(to, n_x)], grecv.at[slot], gs.at[to], gr.at[slot],
            (to // n_x, p.z, lax.rem(to, n_x)),
        )

    loop(n_plane - 1, lambda k: g_copy(lax.rem(me + 1 + k, n_plane), me).start())
    for l in range(layers):
        for i in range(n_x):
            zy = mm(h_all[i].reshape(rows, cols), w_all[l, :cols], 1, 0).astype(BF)
            ct = mm(c_all[i].reshape(rows, cols), w_all[l, :cols, rank:], 1, 0).astype(BF)
            at = slice(i * n_s, (i + 1) * n_s)
            for c, value in enumerate((zy[:, :rank], zy[:, rank:], ct)):
                r0 = (c * layers + l + c // 2) * own
                pbuf[at, r0 : r0 + own, :] = value.reshape(n_s, own, rank)
    for i in range(n_x):
        xf = h_all[i].reshape(rows, cols).astype(F32)
        sq = jnp.broadcast_to(jnp.sum(xf * xf, -1, keepdims=True), (rows, rank)).astype(BF)
        pbuf[i * n_s : (i + 1) * n_s, 2 * layers * own : split, :] = sq.reshape(n_s, own, rank)

    def block(chip, core):
        return (2 * (chip // n_x) + core) * n_x + lax.rem(chip, n_x)

    def pre(i):
        return remote(pbuf.at[block(i, 1 - p.core)], prev.at[i], ps.at[i], pr.at[i], p.partner)

    def pre_wait(i):
        return remote(pbuf.at[block(i, p.core)], prev.at[i], ps.at[i], pr.at[i], p.partner)

    halves = (slice(0, split), slice(split, (3 * layers + 1) * own))

    def c_copy(to, slot, piece):
        return remote(
            psum.at[to, halves[piece]], crev.at[slot, halves[piece]],
            cs.at[to, piece], cr.at[slot, piece], p.peer(to),
        )

    loop(p.chips, lambda k: pre(p.ahead(k)).start())

    loop(n_plane - 1, lambda k: g_copy(me, lax.rem(me + n_plane - 1 - k, n_plane)).wait_recv())
    grecv[me] = gsend[p.s, p.x]
    gsum = grecv[0].astype(F32)
    for k in range(1, n_plane):
        gsum = gsum + grecv[k].astype(F32)
    gram[0, p.z, p.s, p.x] = gsum[:, :rank].astype(BF)
    gram[1, p.z, p.s, p.x] = gsum[:, rank:].astype(BF)

    def gram_view(chip, core):
        return gram.at[:, p.z, 2 * (chip // n_x) + core, lax.rem(chip, n_x)]

    spread = Cast(p, gram_view, (m0, m1, m2, m3))
    spread.start()
    spread.relay()
    spread.finish()

    def gram_part(layer, piece, core):
        return gram.at[lax.rem(piece, 2), layer, 2 * (piece // 2) + core]

    def wanted(layer, piece, core):
        other = 2 * (piece // 2) + core
        upper = layer < other
        last = jnp.where(lax.rem(piece, 2) == 0, layer > other, layer == other)
        return jnp.logical_or(upper, last)

    ring = Ring(
        n_z, p.z, lambda to: (p.s, to, p.x), lambda layer, piece: gram_part(layer, piece, p.core),
        layers, (rs, rr, ls, lr), lambda layer, piece: wanted(layer, piece, p.core),
    )
    ring.start()

    def pair(k):
        i = p.ahead(k)
        pre_wait(i).wait_recv()
        total = pbuf[block(i, p.core)].astype(F32) + prev[i].astype(F32)
        psum[i] = total.astype(BF)

        @pl.when(i != p.chip)
        def _():
            c_copy(i, p.chip, 0).start()

    loop(p.chips, lambda k: pair(lax.rem(k + 1, p.chips)))
    p.others(lambda k: c_copy(p.ahead(k), p.chip, 1).start())

    def share(layer, piece, core):
        ref = gram_part(layer, piece, core)
        return remote(ref, ref, ns.at[layer, piece], nr.at[layer, piece], p.partner)

    ring.run(lambda layer, piece: share(layer, piece, p.core).start())
    crev[p.chip] = psum[p.chip]

    def collect(piece, at):
        p.others(lambda k: c_copy(p.chip, p.behind(k), piece).wait_recv())
        total = crev[0, halves[piece]].astype(F32)
        for k in range(1, p.chips):
            total = total + crev[k, halves[piece]].astype(F32)
        state[at] = total.reshape(-1, own, rank)

    collect(0, slice(0, 2 * layers + 1))

    def each_share(core, fn):
        def body(k):
            layer = lax.rem(p.z + 1 + k // layers, n_z)
            piece = lax.rem(k, layers)
            pl.when(wanted(layer, piece, core))(lambda: fn(share(layer, piece, core)))

        loop((n_z - 1) * layers, body)

    each_share(1 - p.core, lambda copy: copy.wait_recv())

    mid = layers // 2

    def low_view(first, last):
        def view(chip, core):
            dev = block(chip, core)
            return low_out.at[first:last, pl.ds(pl.multiple_of(dev * own, own), own), :]

        return view

    early = Cast(p, low_view(0, mid), (k0, k1, k2, k3))
    lows = Cast(p, low_view(mid, layers + 1), (l0, l1, l2, l3))

    def err_view(chip, core):
        dev = block(chip, core)
        return err_out.at[:, pl.ds(pl.multiple_of(dev * own, own), own), :]

    here = pl.ds(pl.multiple_of(me * own, own), own)
    square = state[2 * layers]
    zero = jnp.zeros((own, rank), F32)
    lane = lax.broadcasted_iota(jnp.int32, (own, rank), 1)
    scal = zero
    for l in range(layers):
        rinv = lax.rsqrt(square / width + 1e-05)
        u = state[l] * rinv
        low = u.astype(BF)
        full[l] = u
        rin[l] = rinv
        low_out[l, here, :] = low
        before = state[layers + l]
        for j in range(layers):
            snap[l, j] = state[layers + j]
            if j > l:
                pair_gram = jnp.concatenate(
                    [gram[0, l, j].reshape(rank, rank), gram[1, l, j].reshape(rank, rank)], 1
                )
                both = mm(low, pair_gram, 1, 0)
                state[j] = state[j] + both[:, :rank]
                state[layers + j] = state[layers + j] + both[:, rank:]
            else:
                one = mm(low, gram[1, j, l].reshape(rank, rank), 1, 1)
                state[layers + j] = state[layers + j] + one
        after = state[layers + l]
        square = square + jnp.sum(low.astype(F32) * (before + after), -1, keepdims=True)
        high = rinv.astype(BF).astype(F32)
        scal = jnp.where(lane == l, high, scal)
        scal = jnp.where(lane == layers + l, rinv - high, scal)
        if l == mid - 1:
            early.start()
    low_out[layers, here, :] = scal.astype(BF)
    lows.start()
    collect(1, slice(2 * layers + 1, 3 * layers + 1))
    scal = zero
    for l in range(layers - 1, -1, -1):
        err = state[2 * layers + 1 + l].astype(BF)
        mean = jnp.sum(err.astype(F32) * full[l], -1, keepdims=True) / width
        rinv = rin[l]
        cor = rinv * rinv * mean
        for j in range(l):
            back = mm(err, gram[0, j, l].reshape(rank, rank), 1, 1)
            state[2 * layers + 1 + j] = state[2 * layers + 1 + j] + rinv * back - cor * snap[l, j]
        err_out[l, here, :] = err
        scal = jnp.where(lane == l, cor, scal)
    err_out[layers, here, :] = scal.astype(BF)
    errs = Cast(p, err_view, (e0, e1, e2, e3))
    errs.start()
    early.relay()
    lows.relay()
    early.finish()
    lows.finish()

    def drain():
        loop(n_plane - 1, lambda k: g_copy(lax.rem(me + 1 + k, n_plane), me).wait_send())
        ring.finish()
        each_share(p.core, lambda copy: copy.wait_send())
        loop(p.chips, lambda k: pre(p.ahead(k)).wait_send())
        p.others(lambda k: c_copy(p.ahead(k), p.chip, 0).wait_send())
        p.others(lambda k: c_copy(p.ahead(k), p.chip, 1).wait_send())

    return drain, errs


def finish_phase(
    sizes, dims, bound, w_all, h_all, c_all, i_all, low_ref, err_ref, errs, grad_out, row_out,
    normed, deltas, hold, tot, gbuf, mid, acc, rbuf, lbuf, ts, tr, gs, gr, zs, zr, us, ur, lsem,
):
    n_s, n_z, n_x = sizes
    rows, cols, rank, width = dims
    layers = n_s
    p = Plane(sizes)
    s, z, x = p.s, p.z, p.x
    def factor(ref, i, l):
        return ref[layers, i * rows : (i + 1) * rows, l : l + 1].astype(F32)

    def rinv_of(i, l):
        return factor(low_ref, i, l) + factor(low_ref, i, layers + l)

    errs.relay()
    errs.finish()
    for i in range(n_x):
        at = slice(i * rows, (i + 1) * rows)
        h = h_all[i].reshape(rows, cols).astype(F32)
        for l in range(layers):
            gain = w_all[l, cols : cols + 8].astype(F32)[0:1, :]
            normed[l, at] = (h * rinv_of(i, l) * gain).astype(BF)
            hold[l, at] = h.astype(BF)
            if l + 1 < layers:
                h = h + mm(low_ref[l, at], w_all[l, :cols, rank:], 1, 1)
    sums = []
    for i in range(n_x):
        at = slice(i * rows, (i + 1) * rows)
        keyrow = i_all[i].astype(F32)[0:1, :]
        keys = jnp.broadcast_to(keyrow, (rows, rows))
        same = keys == keys.T
        pairs = jnp.zeros((rows, rows), F32)
        d = c_all[i].reshape(rows, cols).astype(F32)
        for l in range(layers - 1, -1, -1):
            db = d.astype(BF)
            deltas[l, at] = db
            lo, n, e = low_ref[l, at], normed[l, at], err_ref[l, at]
            pairs = pairs + mm(lo, lo, 1, 1) * mm(db, db, 1, 1)
            pairs = pairs + mm(n, n, 1, 1) * mm(e, e, 1, 1)
            if l > 0:
                d = d + rinv_of(i, l) * mm(e, w_all[l, :cols, :rank], 1, 1)
                d = d - factor(err_ref, i, l) * hold[l, at].astype(F32)
        pairs = jnp.where(same, pairs, 0.0)
        rowsum = jnp.broadcast_to(jnp.sum(pairs, -1, keepdims=True), (rows, rows))
        sums.append(jnp.sum(jnp.where(same, rowsum, 0.0), 0, keepdims=True))
    me = s * n_x + x
    n_plane = n_s * n_x
    pad = [jnp.zeros((8 - n_x, rows), F32)] if n_x < 8 else []
    tot[me] = jnp.concatenate(sums + pad, 0)

    def t_copy(to, slot):
        return remote(
            tot.at[slot], tot.at[slot], ts.at[to], tr.at[slot], (to // n_x, z, lax.rem(to, n_x))
        )

    loop(n_plane - 1, lambda k: t_copy(lax.rem(me + 1 + k, n_plane), me).start())
    loop(n_plane - 1, lambda k: t_copy(me, lax.rem(me + n_plane - 1 - k, n_plane)).wait_recv())
    total = tot[0]
    for k in range(1, n_plane):
        total = total + tot[k]
    clip = bound / jnp.maximum(jnp.sqrt(total), bound)

    weights = []
    for i in range(n_x):
        inc = i_all[i].astype(F32)[1:2, :]
        w = jnp.broadcast_to(inc * clip[i : i + 1], (rows, rows))
        weights.append(w.T[:, :rank])

        @pl.when(x == i)
        def _(w=w, i=i):
            row_out[0:1, :] = w[0:1, :]
            row_out[1:2, :] = i_all[i].astype(F32)[0:1, :]

    weight = jnp.concatenate(weights, 0)

    step_rows = cols // WAVES
    waves = [slice(i * step_rows, (i + 1) * step_rows) for i in range(WAVES)]

    def g_copy(to, slot, piece):
        part = waves[piece]
        return remote(
            gbuf.at[to, part], mid.at[slot, part], gs.at[to, piece], gr.at[slot, piece], (to, z, x)
        )

    def keep():
        return pltpu.make_async_copy(gbuf.at[s], mid.at[s], lsem.at[0])

    def gradient(l):
        we = (weight * err_ref[l].astype(F32)).astype(BF)
        wl = (weight * low_ref[l].astype(F32)).astype(BF)
        gbuf[l, :, :rank] = mm(normed[l], we, 0, 0).astype(BF)
        gbuf[l, :, rank:] = mm(deltas[l], wl, 0, 0).astype(BF)

        @pl.when(s != l)
        def _():
            g_copy(l, s, 0).start()

        @pl.when(s == l)
        def _():
            keep().start()

    loop(layers, gradient)
    for piece in range(1, WAVES):
        loop(n_s - 1, lambda k, piece=piece: g_copy(lax.rem(s + 1 + k, n_s), s, piece).start())
    keep().wait()

    def have(slot, piece):
        @pl.when(slot != s)
        def _():
            g_copy(s, slot, piece).wait_recv()

    far = n_z // 2

    def hops(way, piece):
        return far if way == (piece * 2) // WAVES else far - 1

    def hop(way, step, piece, src):
        part = waves[piece]
        if step + 1 == hops(way, piece):
            dst = grad_out.at[1 + way, part]
        else:
            dst = (rbuf, lbuf)[way].at[step, part]
        send, recv = ((zs, zr), (us, ur))[way]
        to = lax.rem(z + (1, n_z - 1)[way], n_z)
        return remote(src, dst, send.at[step, piece], recv.at[step, piece], (s, to, x))

    def source(way, step, piece, slot):
        part = waves[piece]
        return mid.at[slot, part] if step == 0 else acc.at[way, step - 1, part]

    def slot_of(way, gap):
        return lax.rem(z + (gap if way == 0 else n_z - gap), n_z)

    seen = set()

    def need(gap, piece):
        if (gap % n_z, piece) not in seen:
            seen.add((gap % n_z, piece))
            have(lax.rem(z + gap + n_z, n_z), piece)

    order = sorted((step + piece, piece, step) for step in range(far) for piece in range(WAVES))
    for _, piece, step in order:
        for way in (0, 1):
            if step >= hops(way, piece):
                continue
            gap = hops(way, piece) - step
            need(gap if way == 0 else -gap, piece)
            slot = slot_of(way, gap)
            part = waves[piece]
            src = source(way, step, piece, slot)
            if step > 0:
                hop(way, step - 1, piece, source(way, step - 1, piece, slot)).wait_recv()
                came = (rbuf, lbuf)[way][step - 1, part].astype(F32)
                acc[way, step - 1, part] = (came + mid[slot, part].astype(F32)).astype(BF)
            hop(way, step, piece, src).start()
    for piece in range(WAVES):
        need(0, piece)
    grad_out[0] = mid[z]
    for way in (0, 1):
        for piece in range(WAVES):
            step = hops(way, piece) - 1
            hop(way, step, piece, source(way, step, piece, z)).wait_recv()

    def drain():
        for way in (0, 1):
            for piece in range(WAVES):
                for step in range(hops(way, piece)):
                    hop(way, step, piece, source(way, step, piece, z)).wait_send()
        for piece in range(WAVES):
            loop(n_s - 1, lambda k, piece=piece: g_copy(lax.rem(s + 1 + k, n_s), s, piece).wait_send())
        loop(n_plane - 1, lambda k: t_copy(lax.rem(me + 1 + k, n_plane), me).wait_send())

    return drain


def main_kernel(
    sizes, dims, bound, n_ex, n_so, a_ref, b_ref, g_ref, hid_ref, cot_ref, user_ref, inc_ref,
    grad_out, row_out, w_all, h_all, c_all, i_all, low, err, *scratch,
):
    n_s, n_z, n_x = sizes
    p = Plane(sizes)
    barrier = pltpu.get_barrier_semaphore()
    count = p.greet_all(barrier)
    for k in (1, n_z - 1):
        pl.semaphore_signal(
            barrier, inc=1, device_id=(p.s, lax.rem(p.z + k, n_z), p.x), device_id_type=MESH
        )
    first = exchange_phase(
        sizes, a_ref, b_ref, g_ref, hid_ref, cot_ref, user_ref, inc_ref, w_all, h_all, c_all, i_all,
        lambda: pl.semaphore_wait(barrier, count + 2), *scratch[:n_ex],
    )
    second, errs = solve_phase(sizes, dims, w_all, h_all, c_all, low, err, *scratch[n_ex : n_ex + n_so])
    third = finish_phase(
        sizes, dims, bound, w_all, h_all, c_all, i_all, low, err, errs, grad_out, row_out,
        *scratch[n_ex + n_so :],
    )
    first()
    second()
    third()


def main(sizes, dims, bound, a, b, g, hidden, cot, users, inc):
    n_s, n_z, n_x = sizes
    rows, cols, rank, width = dims
    layers = n_s
    chips = (n_s // 2) * n_x
    plane = n_s * n_x
    own = rows // n_s
    group = rows * n_x
    part = rank // n_x
    high = (3 * layers + 1) * own
    dma = pltpu.SemaphoreType.DMA
    v = pltpu.VMEM
    slab = (n_x, *hidden.shape[:2], cols)
    shared = [
        v((n_s, cols + 16, 2 * rank), BF),
        v(slab, BF),
        v(slab, BF),
        v((n_x, 16, rows), BF),
        v((layers + 1, group, rank), BF),
        v((layers + 1, group, rank), BF),
    ]
    ex = [
        v((n_z, cols + 16, 2 * rank), BF),
        v((16, rows), BF),
        dma((n_z, PIECES)), dma((n_z, PIECES)), dma((n_z, PIECES)), dma((n_z, PIECES)),
        dma((n_z, PIECES)), dma((n_s, PIECES)), dma((3, n_x)), dma((3, n_x)), dma((3 + PIECES,)),
    ]
    so = [
        v((n_s, n_x, part, 2 * rank), BF),
        v((plane, part, 2 * rank), BF),
        v((2, n_z, n_s, n_x, part, rank), BF),
        v((plane, high, rank), BF),
        v((chips, high, rank), BF),
        v((chips, high, rank), BF),
        v((chips, high, rank), BF),
        v((3 * layers + 1, own, rank), F32),
        v((layers, layers, own, rank), F32),
        v((layers, own, rank), F32),
        v((layers, own, rank), F32),
        dma((plane,)), dma((plane,)),
    ]
    so += [dma((n_z, layers))] * 6 + [dma((chips,))] * 2 + [dma((chips, 2))] * 2 + [dma((chips,))] * 16
    fi = [
        v((layers, group, cols), BF),
        v((layers, group, cols), BF),
        v((layers, group, cols), BF),
        v((plane, 8, rows), F32),
        v((layers, cols, 2 * rank), BF),
        v((n_s, cols, 2 * rank), BF),
        v((2, n_z // 2, cols, 2 * rank), BF),
        v((n_z // 2, cols, 2 * rank), BF),
        v((n_z // 2, cols, 2 * rank), BF),
        dma((plane,)), dma((plane,)), dma((n_s, WAVES)), dma((n_s, WAVES)),
    ]
    fi += [dma((n_z // 2, WAVES))] * 4 + [dma((1,))]
    return pl.pallas_call(
        functools.partial(main_kernel, sizes, dims, bound, len(ex), len(so)),
        out_shape=(
            jax.ShapeDtypeStruct((3, cols, 2 * rank), BF),
            jax.ShapeDtypeStruct((8, rows), F32),
        ),
        in_specs=[VMEM, VMEM, VMEM, ANY, ANY, VMEM, VMEM],
        out_specs=(VMEM, VMEM),
        scratch_shapes=shared + ex + so + fi,
        compiler_params=params(0),
        name="main",
    )(a, b, g, hidden, cot, users, inc)


def close_kernel(parts, row, gi_out, go_out, uw_out):
    rank = gi_out.shape[1]
    grad = parts[0].astype(F32) + parts[1].astype(F32) + parts[2].astype(F32)
    gi_out[...] = grad[:, :rank]
    go_out[...] = grad[:, rank:].T
    users, micro = uw_out.shape
    width = row.shape[1]
    weight = jnp.broadcast_to(row[0:1, :], (users, width))
    key = jnp.broadcast_to(row[1:2, :], (users, width))
    user = lax.broadcasted_iota(jnp.int32, (users, width), 0).astype(F32)
    lane = lax.broadcasted_iota(jnp.int32, (users, micro), 1)
    result = jnp.zeros((users, micro), F32)
    for m in range(micro):
        most = jnp.max(jnp.where(key == user + m * users, weight, 0.0), -1, keepdims=True)
        result = jnp.where(lane == m, most, result)
    uw_out[...] = result


def shards(hidden_in, cotangent, adapter_in, adapter_out, norm_gain, user_of_row, included):
    sizes = tuple(lax.axis_size(a) for a in ("section", "z", "x"))
    n_s = sizes[0]
    micro, rows, width = hidden_in.shape
    cols, rank = adapter_in.shape[1:]
    users = included.shape[1]
    bound = 0.8 * math.sqrt(n_s * (rows // users) * width * width)
    parts, row = main(
        sizes, (micro * rows, cols, rank, width), bound, adapter_in[0], adapter_out[0], norm_gain,
        hidden_in, cotangent, user_of_row, included.T,
    )
    gi, go, uw = pl.pallas_call(
        close_kernel,
        out_shape=(
            jax.ShapeDtypeStruct((cols, rank), F32),
            jax.ShapeDtypeStruct((rank, cols), F32),
            jax.ShapeDtypeStruct((users, micro), F32),
        ),
        in_specs=[VMEM, VMEM],
        out_specs=(VMEM,) * 3,
        name="close",
    )(parts, row)
    return (gi[None], go[None], uw.T)


def build(torus):
    dp = ("z", "x")
    return jax.shard_map(
        shards,
        mesh=torus,
        in_specs=(
            P(None, dp, None),
            P(None, dp, None),
            P("section", dp, None),
            P("section", None, dp),
            P("section", dp),
            P(None, dp),
            P(None, dp),
        ),
        out_specs=(P("section", dp, None), P("section", None, dp), P(None, dp)),
        check_vma=False,
    )


def solution(mesh):
    return build(Mesh(mesh.devices.reshape(mesh.shape["section"], 8, 4), ("section", "z", "x")))
```

```python
import functools
import math

import jax
import jax.numpy as jnp
from jax import lax
from jax.experimental import pallas as pl
from jax.experimental.pallas import tpu as pltpu
from jax.sharding import Mesh
from jax.sharding import PartitionSpec as P

F32 = jnp.float32
BF = jnp.bfloat16
MESH = pl.DeviceIdType.MESH
VMEM = pl.BlockSpec(memory_space=pltpu.VMEM)
ANY = pl.BlockSpec(memory_space=pl.ANY)
LIMIT = 60 * 1024 * 1024
PIECES = 4
WAVES = 2


def mm(a, b, ca, cb):
    return lax.dot_general(a, b, (((ca,), (cb,)), ((), ())), preferred_element_type=F32)


def loop(n, body):
    lax.fori_loop(0, n, lambda i, c: (body(i), c)[1], 0)


def remote(src, dst, send, recv, device):
    return pltpu.make_async_remote_copy(
        src_ref=src, dst_ref=dst, send_sem=send, recv_sem=recv, device_id=device, device_id_type=MESH
    )


def params(cid):
    return pltpu.CompilerParams(collective_id=cid, has_side_effects=True, vmem_limit_bytes=LIMIT)


def where_am_i():
    return tuple(lax.axis_index(a) for a in ("section", "z", "x"))


class Ring:
    def __init__(self, n, me, place, view, pieces, sems, want=None):
        self.n, self.me, self.place, self.view, self.pieces, self.sems = n, me, place, view, pieces, sems
        self.want = want
        self.far = n // 2

    def block(self, way, step):
        sign = 1 - 2 * way
        return lax.rem(self.me - sign * step + 2 * self.n, self.n)

    def copy(self, way, step, piece, block):
        sign = 1 - 2 * way
        ref = self.view(block, piece)
        send, recv = self.sems[2 * way].at[step, piece], self.sems[2 * way + 1].at[step, piece]
        return remote(ref, ref, send, recv, self.place(lax.rem(self.me + sign + self.n, self.n)))

    def guard(self, block, piece, fn):
        if self.want is None:
            fn()
        else:
            pl.when(self.want(block, piece))(fn)

    def each(self, step, fn):
        half = self.pieces // 2

        def body(i):
            if step + 1 < self.far:
                for way in (0, 1):
                    fn(way, i)
            else:
                fn(0, i)
                fn(1, i + half)

        count = self.pieces if step + 1 < self.far else half
        if self.want is None:
            for i in range(count):
                body(i)
        else:
            loop(count, body)

    def send(self, way, step, piece):
        block = self.block(way, step)
        self.guard(block, piece, lambda: self.copy(way, step, piece, block).start())

    def start(self):
        self.each(0, lambda way, piece: self.send(way, 0, piece))

    def run(self, arrived):
        half = self.pieces // 2

        def one(step, way, piece):
            block = self.block(way, step + 1)

            def take():
                self.copy(way, step, piece, block).wait_recv()
                if step + 2 < self.far:
                    self.copy(way, step + 1, piece, block).start()
                elif step + 2 == self.far:
                    onward = piece < half if way == 0 else piece >= half
                    if isinstance(onward, bool):
                        if onward:
                            self.copy(way, step + 1, piece, block).start()
                    else:
                        pl.when(onward)(lambda: self.copy(way, step + 1, piece, block).start())
                arrived(block, piece)

            self.guard(block, piece, take)

        for step in range(self.far):
            self.each(step, lambda way, piece: one(step, way, piece))

    def finish(self):
        def one(step, way, piece):
            block = self.block(way, step)
            self.guard(block, piece, lambda: self.copy(way, step, piece, block).wait_send())

        for step in range(self.far):
            self.each(step, lambda way, piece: one(step, way, piece))


def exchange_phase(
    sizes, a_ref, b_ref, g_ref, hid_ref, cot_ref, user_ref, inc_ref, w_all, h_all, c_all, i_all, ready,
    column, info, rs, rr, ls, lr, ys, yr, asend, arecv, lsem,
):
    n_s, n_z, n_x = sizes
    s, z, x = where_am_i()
    cols, rank = a_ref.shape
    micro, rows = user_ref.shape
    users = inc_ref.shape[0]
    gain = jnp.broadcast_to(g_ref[...].astype(F32), (rank, cols))
    column[z, :cols, :rank] = (a_ref[...].astype(F32) * gain.T).astype(BF)
    column[z, :cols, rank:] = b_ref[...].astype(F32).T.astype(BF)
    column[z, cols:, :] = jnp.broadcast_to(g_ref[...].astype(F32), (16, cols)).astype(BF)
    local = user_ref[...] - (z * n_x + x) * users
    included = jnp.zeros((micro, rows), F32)
    level = lax.broadcasted_iota(jnp.int32, (micro, rows), 0)
    for u in range(users):
        for m in range(micro):
            here = jnp.logical_and(local == u, level == m)
            included = jnp.where(here, inc_ref[u : u + 1, m : m + 1].astype(F32), included)
    key = (local + users * level).astype(F32)
    dev_rows = micro * rows
    lane = lax.broadcasted_iota(jnp.int32, (rows, dev_rows), 1)
    row = lax.broadcasted_iota(jnp.int32, (rows, dev_rows), 0)
    place = sum(jnp.where(lane == row + m * rows, 1.0, 0.0) for m in range(micro)).astype(BF)
    top = lax.broadcasted_iota(jnp.int32, (micro, dev_rows), 0)
    along = lax.broadcasted_iota(jnp.int32, (micro, dev_rows), 1)
    mine = jnp.logical_and(along >= top * rows, along < (top + 1) * rows)

    def flat(v):
        wide = mm(v.astype(BF), place, 1, 0)
        return jnp.sum(jnp.where(mine, wide, 0.0), 0, keepdims=True)

    which_row = lax.broadcasted_iota(jnp.int32, (16, dev_rows), 0)
    info[...] = jnp.where(which_row == 0, flat(key), flat(included)).astype(BF)
    ready()

    def act(which, to, slot):
        at = pl.ds(pl.multiple_of((s * n_x + to) * cols, cols), cols)
        src = (hid_ref.at[:, :, at], cot_ref.at[:, :, at], info)[which]
        dst = (h_all, c_all, i_all)[which].at[slot]
        return src, dst

    def a_copy(which, to, slot):
        src, dst = act(which, to, slot)
        return remote(src, dst, asend.at[which, to], arecv.at[which, slot], (s, z, to))

    step = cols // PIECES
    half = [slice(i * step, (i + 1) * step) for i in range(PIECES - 1)]
    half.append(slice((PIECES - 1) * step, cols + 16))

    def view(block, piece):
        return column.at[block, half[piece]]

    ring = Ring(n_z, z, lambda to: (s, to, x), view, PIECES, (rs, rr, ls, lr))
    ring.start()
    for which in range(3):
        for k in range(1, n_x):
            a_copy(which, lax.rem(x + k, n_x), x).start()
    for which in range(3):
        src, dst = act(which, x, x)
        pltpu.make_async_copy(src, dst, lsem.at[which]).start()

    def y_copy(block, slot, piece):
        return remote(
            column.at[block, half[piece]], w_all.at[slot, half[piece]],
            ys.at[block, piece], yr.at[slot, piece], (block, z, x),
        )

    def keep(piece):
        return pltpu.make_async_copy(
            column.at[s, half[piece]], w_all.at[s, half[piece]], lsem.at[3 + piece]
        )

    def onward(block, piece):
        @pl.when(block == s)
        def _():
            keep(piece).start()

        @pl.when(block != s)
        def _():
            y_copy(block, s, piece).start()

    for piece in range(PIECES):
        onward(z, piece)
    ring.run(onward)
    for which in range(3):
        src, dst = act(which, x, x)
        pltpu.make_async_copy(src, dst, lsem.at[which]).wait()
        for k in range(1, n_x):
            a_copy(which, x, lax.rem(x + n_x - k, n_x)).wait_recv()

    def not_me(fn):
        def body(k):
            for piece in range(PIECES):
                fn(lax.rem(s + 1 + k, n_s), piece)

        loop(n_s - 1, body)

    for piece in range(PIECES):
        keep(piece).wait()
    not_me(lambda k, piece: y_copy(s, k, piece).wait_recv())

    def drain():
        not_me(lambda k, piece: y_copy(k, s, piece).wait_send())
        for which in range(3):
            for k in range(1, n_x):
                a_copy(which, lax.rem(x + k, n_x), x).wait_send()
        ring.finish()

    return drain


class Plane:
    def __init__(self, sizes):
        n_s, n_z, n_x = sizes
        self.n_x = n_x
        self.chips = (n_s // 2) * n_x
        self.s, self.z, self.x = where_am_i()
        self.core = lax.rem(self.s, 2)
        self.chip = (self.s // 2) * n_x + self.x
        self.partner = (self.s + 1 - 2 * self.core, self.z, self.x)

    def peer(self, chip):
        return (2 * (chip // self.n_x) + self.core, self.z, lax.rem(chip, self.n_x))

    def ahead(self, k):
        return lax.rem(self.chip + k, self.chips)

    def behind(self, k):
        return lax.rem(self.chip + self.chips - k, self.chips)

    def others(self, fn):
        loop(self.chips - 1, lambda k: fn(k + 1))

    def greet_all(self, barrier):
        def one(chip):
            s2, z2, x2 = self.peer(chip)
            pl.semaphore_signal(barrier, inc=1, device_id=(s2, z2, x2), device_id_type=MESH)
            pl.semaphore_signal(
                barrier, inc=1, device_id=(s2 + 1 - 2 * self.core, z2, x2), device_id_type=MESH
            )

        self.others(lambda k: one(self.ahead(k)))
        pl.semaphore_signal(barrier, inc=1, device_id=self.partner, device_id_type=MESH)
        return 2 * self.chips - 1


class Cast:
    def __init__(self, plane, view, sems):
        self.p, self.view, self.sems = plane, view, sems

    def far(self, chip, owner):
        send, recv = self.sems[0].at[chip], self.sems[1].at[owner]
        ref = self.view(owner, self.p.core)
        return remote(ref, ref, send, recv, self.p.peer(chip))

    def near(self, chip, core):
        ref = self.view(chip, core)
        return remote(ref, ref, self.sems[2].at[chip], self.sems[3].at[chip], self.p.partner)

    def start(self):
        p = self.p
        p.others(lambda k: self.far(p.ahead(k), p.chip).start())
        self.near(p.chip, p.core).start()

    def relay(self):
        p = self.p

        def one(k):
            chip = p.behind(k)
            self.far(chip, chip).wait_recv()
            self.near(chip, p.core).start()

        p.others(one)

    def finish(self):
        p = self.p
        loop(p.chips, lambda i: self.near(i, 1 - p.core).wait_recv())
        loop(p.chips, lambda i: self.near(i, p.core).wait_send())
        p.others(lambda k: self.far(p.ahead(k), p.chip).wait_send())


def solve_phase(
    sizes, dims, w_all, h_all, c_all, low_out, err_out,
    gsend, grecv, gram, pbuf, prev, psum, crev, state, snap, full, rin,
    gs, gr, rs, rr, ls, lr, ns, nr, ps, pr, cs, cr, m0, m1, m2, m3, k0, k1, k2, k3, l0, l1, l2, l3, e0, e1, e2, e3,
):
    n_s, n_z, n_x = sizes
    rows, cols, rank, width = dims
    layers = n_s
    own = rows // n_s
    part = rank // n_x
    split = (2 * layers + 1) * own
    p = Plane(sizes)
    mine = w_all[p.z, :cols, rank:]
    for l in range(layers):
        g = mm(mine, w_all[l, :cols], 0, 0).astype(BF)
        gsend[l] = g.reshape(n_x, part, 2 * rank)
    n_plane = 2 * p.chips
    me = p.s * n_x + p.x

    def g_copy(to, slot):
        return remote(
            gsend.at[to // n_x, lax.rem(to, n_x)], grecv.at[slot], gs.at[to], gr.at[slot],
            (to // n_x, p.z, lax.rem(to, n_x)),
        )

    loop(n_plane - 1, lambda k: g_copy(lax.rem(me + 1 + k, n_plane), me).start())
    for l in range(layers):
        for i in range(n_x):
            zy = mm(h_all[i].reshape(rows, cols), w_all[l, :cols], 1, 0).astype(BF)
            ct = mm(c_all[i].reshape(rows, cols), w_all[l, :cols, rank:], 1, 0).astype(BF)
            at = slice(i * n_s, (i + 1) * n_s)
            for c, value in enumerate((zy[:, :rank], zy[:, rank:], ct)):
                r0 = (c * layers + l + c // 2) * own
                pbuf[at, r0 : r0 + own, :] = value.reshape(n_s, own, rank)
    for i in range(n_x):
        xf = h_all[i].reshape(rows, cols).astype(F32)
        sq = jnp.broadcast_to(jnp.sum(xf * xf, -1, keepdims=True), (rows, rank)).astype(BF)
        pbuf[i * n_s : (i + 1) * n_s, 2 * layers * own : split, :] = sq.reshape(n_s, own, rank)

    def block(chip, core):
        return (2 * (chip // n_x) + core) * n_x + lax.rem(chip, n_x)

    def pre(i):
        return remote(pbuf.at[block(i, 1 - p.core)], prev.at[i], ps.at[i], pr.at[i], p.partner)

    def pre_wait(i):
        return remote(pbuf.at[block(i, p.core)], prev.at[i], ps.at[i], pr.at[i], p.partner)

    halves = (slice(0, split), slice(split, (3 * layers + 1) * own))

    def c_copy(to, slot, piece):
        return remote(
            psum.at[to, halves[piece]], crev.at[slot, halves[piece]],
            cs.at[to, piece], cr.at[slot, piece], p.peer(to),
        )

    loop(p.chips, lambda k: pre(p.ahead(k)).start())

    loop(n_plane - 1, lambda k: g_copy(me, lax.rem(me + n_plane - 1 - k, n_plane)).wait_recv())
    grecv[me] = gsend[p.s, p.x]
    gsum = grecv[0].astype(F32)
    for k in range(1, n_plane):
        gsum = gsum + grecv[k].astype(F32)
    gram[0, p.z, p.s, p.x] = gsum[:, :rank].astype(BF)
    gram[1, p.z, p.s, p.x] = gsum[:, rank:].astype(BF)

    def gram_view(chip, core):
        return gram.at[:, p.z, 2 * (chip // n_x) + core, lax.rem(chip, n_x)]

    spread = Cast(p, gram_view, (m0, m1, m2, m3))
    spread.start()
    spread.relay()

    def gram_part(layer, piece, core):
        return gram.at[lax.rem(piece, 2), layer, 2 * (piece // 2) + core]

    def wanted(layer, piece, core):
        other = 2 * (piece // 2) + core
        upper = layer < other
        last = jnp.where(lax.rem(piece, 2) == 0, layer > other, layer == other)
        return jnp.logical_or(upper, last)

    ring = Ring(
        n_z, p.z, lambda to: (p.s, to, p.x), lambda layer, piece: gram_part(layer, piece, p.core),
        layers, (rs, rr, ls, lr), lambda layer, piece: wanted(layer, piece, p.core),
    )
    ring.start()

    def pair(k):
        i = p.ahead(k)
        pre_wait(i).wait_recv()
        total = pbuf[block(i, p.core)].astype(F32) + prev[i].astype(F32)
        psum[i] = total.astype(BF)

        @pl.when(i != p.chip)
        def _():
            c_copy(i, p.chip, 0).start()

    loop(p.chips, lambda k: pair(lax.rem(k + 1, p.chips)))
    p.others(lambda k: c_copy(p.ahead(k), p.chip, 1).start())

    def share(layer, piece, core):
        ref = gram_part(layer, piece, core)
        return remote(ref, ref, ns.at[layer, piece], nr.at[layer, piece], p.partner)

    ring.run(lambda layer, piece: share(layer, piece, p.core).start())
    spread.finish()
    crev[p.chip] = psum[p.chip]

    def collect(piece, at):
        p.others(lambda k: c_copy(p.chip, p.behind(k), piece).wait_recv())
        total = crev[0, halves[piece]].astype(F32)
        for k in range(1, p.chips):
            total = total + crev[k, halves[piece]].astype(F32)
        state[at] = total.reshape(-1, own, rank)

    collect(0, slice(0, 2 * layers + 1))

    def each_share(core, fn):
        def body(k):
            layer = lax.rem(p.z + 1 + k // layers, n_z)
            piece = lax.rem(k, layers)
            pl.when(wanted(layer, piece, core))(lambda: fn(share(layer, piece, core)))

        loop((n_z - 1) * layers, body)

    each_share(1 - p.core, lambda copy: copy.wait_recv())

    mid = layers // 2

    def low_view(first, last):
        def view(chip, core):
            dev = block(chip, core)
            return low_out.at[first:last, pl.ds(pl.multiple_of(dev * own, own), own), :]

        return view

    early = Cast(p, low_view(0, mid), (k0, k1, k2, k3))
    lows = Cast(p, low_view(mid, layers + 1), (l0, l1, l2, l3))

    def err_view(chip, core):
        dev = block(chip, core)
        return err_out.at[:, pl.ds(pl.multiple_of(dev * own, own), own), :]

    here = pl.ds(pl.multiple_of(me * own, own), own)
    square = state[2 * layers]
    zero = jnp.zeros((own, rank), F32)
    lane = lax.broadcasted_iota(jnp.int32, (own, rank), 1)
    scal = zero
    for l in range(layers):
        rinv = lax.rsqrt(square / width + 1e-05)
        u = state[l] * rinv
        low = u.astype(BF)
        full[l] = u
        rin[l] = rinv
        low_out[l, here, :] = low
        before = state[layers + l]
        for j in range(layers):
            snap[l, j] = state[layers + j]
            if j > l:
                pair_gram = jnp.concatenate(
                    [gram[0, l, j].reshape(rank, rank), gram[1, l, j].reshape(rank, rank)], 1
                )
                both = mm(low, pair_gram, 1, 0)
                state[j] = state[j] + both[:, :rank]
                state[layers + j] = state[layers + j] + both[:, rank:]
            else:
                one = mm(low, gram[1, j, l].reshape(rank, rank), 1, 1)
                state[layers + j] = state[layers + j] + one
        after = state[layers + l]
        square = square + jnp.sum(low.astype(F32) * (before + after), -1, keepdims=True)
        high = rinv.astype(BF).astype(F32)
        scal = jnp.where(lane == l, high, scal)
        scal = jnp.where(lane == layers + l, rinv - high, scal)
        if l == mid - 1:
            early.start()
    low_out[layers, here, :] = scal.astype(BF)
    lows.start()
    collect(1, slice(2 * layers + 1, 3 * layers + 1))
    scal = zero
    for l in range(layers - 1, -1, -1):
        err = state[2 * layers + 1 + l].astype(BF)
        mean = jnp.sum(err.astype(F32) * full[l], -1, keepdims=True) / width
        rinv = rin[l]
        cor = rinv * rinv * mean
        for j in range(l):
            back = mm(err, gram[0, j, l].reshape(rank, rank), 1, 1)
            state[2 * layers + 1 + j] = state[2 * layers + 1 + j] + rinv * back - cor * snap[l, j]
        err_out[l, here, :] = err
        scal = jnp.where(lane == l, cor, scal)
    err_out[layers, here, :] = scal.astype(BF)
    errs = Cast(p, err_view, (e0, e1, e2, e3))
    errs.start()
    early.relay()
    lows.relay()
    early.finish()
    lows.finish()

    def drain():
        loop(n_plane - 1, lambda k: g_copy(lax.rem(me + 1 + k, n_plane), me).wait_send())
        ring.finish()
        each_share(p.core, lambda copy: copy.wait_send())
        loop(p.chips, lambda k: pre(p.ahead(k)).wait_send())
        p.others(lambda k: c_copy(p.ahead(k), p.chip, 0).wait_send())
        p.others(lambda k: c_copy(p.ahead(k), p.chip, 1).wait_send())

    return drain, errs


def finish_phase(
    sizes, dims, bound, w_all, h_all, c_all, i_all, low_ref, err_ref, errs, grad_out, row_out,
    normed, deltas, hold, tot, gbuf, mid, acc, rbuf, lbuf, ts, tr, gs, gr, zs, zr, us, ur, lsem,
):
    n_s, n_z, n_x = sizes
    rows, cols, rank, width = dims
    layers = n_s
    p = Plane(sizes)
    s, z, x = p.s, p.z, p.x
    def factor(ref, i, l):
        return ref[layers, i * rows : (i + 1) * rows, l : l + 1].astype(F32)

    def rinv_of(i, l):
        return factor(low_ref, i, l) + factor(low_ref, i, layers + l)

    errs.relay()
    errs.finish()
    for i in range(n_x):
        at = slice(i * rows, (i + 1) * rows)
        h = h_all[i].reshape(rows, cols).astype(F32)
        for l in range(layers):
            gain = w_all[l, cols : cols + 8].astype(F32)[0:1, :]
            normed[l, at] = (h * rinv_of(i, l) * gain).astype(BF)
            hold[l, at] = h.astype(BF)
            if l + 1 < layers:
                h = h + mm(low_ref[l, at], w_all[l, :cols, rank:], 1, 1)
    sums = []
    for i in range(n_x):
        at = slice(i * rows, (i + 1) * rows)
        keyrow = i_all[i].astype(F32)[0:1, :]
        keys = jnp.broadcast_to(keyrow, (rows, rows))
        same = keys == keys.T
        pairs = jnp.zeros((rows, rows), F32)
        d = c_all[i].reshape(rows, cols).astype(F32)
        for l in range(layers - 1, -1, -1):
            db = d.astype(BF)
            deltas[l, at] = db
            lo, n, e = low_ref[l, at], normed[l, at], err_ref[l, at]
            pairs = pairs + mm(lo, lo, 1, 1) * mm(db, db, 1, 1)
            pairs = pairs + mm(n, n, 1, 1) * mm(e, e, 1, 1)
            if l > 0:
                d = d + rinv_of(i, l) * mm(e, w_all[l, :cols, :rank], 1, 1)
                d = d - factor(err_ref, i, l) * hold[l, at].astype(F32)
        pairs = jnp.where(same, pairs, 0.0)
        rowsum = jnp.broadcast_to(jnp.sum(pairs, -1, keepdims=True), (rows, rows))
        sums.append(jnp.sum(jnp.where(same, rowsum, 0.0), 0, keepdims=True))
    me = s * n_x + x
    n_plane = n_s * n_x
    pad = [jnp.zeros((8 - n_x, rows), F32)] if n_x < 8 else []
    tot[me] = jnp.concatenate(sums + pad, 0)

    def t_copy(to, slot):
        return remote(
            tot.at[slot], tot.at[slot], ts.at[to], tr.at[slot], (to // n_x, z, lax.rem(to, n_x))
        )

    loop(n_plane - 1, lambda k: t_copy(lax.rem(me + 1 + k, n_plane), me).start())
    loop(n_plane - 1, lambda k: t_copy(me, lax.rem(me + n_plane - 1 - k, n_plane)).wait_recv())
    total = tot[0]
    for k in range(1, n_plane):
        total = total + tot[k]
    clip = bound / jnp.maximum(jnp.sqrt(total), bound)

    weights = []
    for i in range(n_x):
        inc = i_all[i].astype(F32)[1:2, :]
        w = jnp.broadcast_to(inc * clip[i : i + 1], (rows, rows))
        weights.append(w.T[:, :rank])

        @pl.when(x == i)
        def _(w=w, i=i):
            row_out[0:1, :] = w[0:1, :]
            row_out[1:2, :] = i_all[i].astype(F32)[0:1, :]

    weight = jnp.concatenate(weights, 0)

    step_rows = cols // WAVES
    waves = [slice(i * step_rows, (i + 1) * step_rows) for i in range(WAVES)]

    def g_copy(to, slot, piece):
        part = waves[piece]
        return remote(
            gbuf.at[to, part], mid.at[slot, part], gs.at[to, piece], gr.at[slot, piece], (to, z, x)
        )

    def keep():
        return pltpu.make_async_copy(gbuf.at[s], mid.at[s], lsem.at[0])

    def gradient(l):
        we = (weight * err_ref[l].astype(F32)).astype(BF)
        wl = (weight * low_ref[l].astype(F32)).astype(BF)
        gbuf[l, :, :rank] = mm(normed[l], we, 0, 0).astype(BF)
        gbuf[l, :, rank:] = mm(deltas[l], wl, 0, 0).astype(BF)

        @pl.when(s != l)
        def _():
            g_copy(l, s, 0).start()

        @pl.when(s == l)
        def _():
            keep().start()

    loop(layers, gradient)
    for piece in range(1, WAVES):
        loop(n_s - 1, lambda k, piece=piece: g_copy(lax.rem(s + 1 + k, n_s), s, piece).start())
    keep().wait()

    def have(slot, piece):
        @pl.when(slot != s)
        def _():
            g_copy(s, slot, piece).wait_recv()

    far = n_z // 2

    def hops(way, piece):
        return far if way == (piece * 2) // WAVES else far - 1

    def hop(way, step, piece, src):
        part = waves[piece]
        if step + 1 == hops(way, piece):
            dst = grad_out.at[1 + way, part]
        else:
            dst = (rbuf, lbuf)[way].at[step, part]
        send, recv = ((zs, zr), (us, ur))[way]
        to = lax.rem(z + (1, n_z - 1)[way], n_z)
        return remote(src, dst, send.at[step, piece], recv.at[step, piece], (s, to, x))

    def source(way, step, piece, slot):
        part = waves[piece]
        return mid.at[slot, part] if step == 0 else acc.at[way, step - 1, part]

    def slot_of(way, gap):
        return lax.rem(z + (gap if way == 0 else n_z - gap), n_z)

    seen = set()

    def need(gap, piece):
        if (gap % n_z, piece) not in seen:
            seen.add((gap % n_z, piece))
            have(lax.rem(z + gap + n_z, n_z), piece)

    order = sorted((step + piece, piece, step) for step in range(far) for piece in range(WAVES))
    for _, piece, step in order:
        for way in (0, 1):
            if step >= hops(way, piece):
                continue
            gap = hops(way, piece) - step
            need(gap if way == 0 else -gap, piece)
            slot = slot_of(way, gap)
            part = waves[piece]
            src = source(way, step, piece, slot)
            if step > 0:
                hop(way, step - 1, piece, source(way, step - 1, piece, slot)).wait_recv()
                came = (rbuf, lbuf)[way][step - 1, part].astype(F32)
                acc[way, step - 1, part] = (came + mid[slot, part].astype(F32)).astype(BF)
            hop(way, step, piece, src).start()
    for piece in range(WAVES):
        need(0, piece)
    grad_out[0] = mid[z]
    for way in (0, 1):
        for piece in range(WAVES):
            step = hops(way, piece) - 1
            hop(way, step, piece, source(way, step, piece, z)).wait_recv()

    def drain():
        for way in (0, 1):
            for piece in range(WAVES):
                for step in range(hops(way, piece)):
                    hop(way, step, piece, source(way, step, piece, z)).wait_send()
        for piece in range(WAVES):
            loop(n_s - 1, lambda k, piece=piece: g_copy(lax.rem(s + 1 + k, n_s), s, piece).wait_send())
        loop(n_plane - 1, lambda k: t_copy(lax.rem(me + 1 + k, n_plane), me).wait_send())

    return drain


def main_kernel(
    sizes, dims, bound, n_ex, n_so, a_ref, b_ref, g_ref, hid_ref, cot_ref, user_ref, inc_ref,
    grad_out, row_out, w_all, h_all, c_all, i_all, low, err, *scratch,
):
    n_s, n_z, n_x = sizes
    p = Plane(sizes)
    barrier = pltpu.get_barrier_semaphore()
    count = p.greet_all(barrier)
    for k in (1, n_z - 1):
        pl.semaphore_signal(
            barrier, inc=1, device_id=(p.s, lax.rem(p.z + k, n_z), p.x), device_id_type=MESH
        )
    first = exchange_phase(
        sizes, a_ref, b_ref, g_ref, hid_ref, cot_ref, user_ref, inc_ref, w_all, h_all, c_all, i_all,
        lambda: pl.semaphore_wait(barrier, count + 2), *scratch[:n_ex],
    )
    second, errs = solve_phase(sizes, dims, w_all, h_all, c_all, low, err, *scratch[n_ex : n_ex + n_so])
    third = finish_phase(
        sizes, dims, bound, w_all, h_all, c_all, i_all, low, err, errs, grad_out, row_out,
        *scratch[n_ex + n_so :],
    )
    first()
    second()
    third()


def main(sizes, dims, bound, a, b, g, hidden, cot, users, inc):
    n_s, n_z, n_x = sizes
    rows, cols, rank, width = dims
    layers = n_s
    chips = (n_s // 2) * n_x
    plane = n_s * n_x
    own = rows // n_s
    group = rows * n_x
    part = rank // n_x
    high = (3 * layers + 1) * own
    dma = pltpu.SemaphoreType.DMA
    v = pltpu.VMEM
    slab = (n_x, *hidden.shape[:2], cols)
    shared = [
        v((n_s, cols + 16, 2 * rank), BF),
        v(slab, BF),
        v(slab, BF),
        v((n_x, 16, rows), BF),
        v((layers + 1, group, rank), BF),
        v((layers + 1, group, rank), BF),
    ]
    ex = [
        v((n_z, cols + 16, 2 * rank), BF),
        v((16, rows), BF),
        dma((n_z, PIECES)), dma((n_z, PIECES)), dma((n_z, PIECES)), dma((n_z, PIECES)),
        dma((n_z, PIECES)), dma((n_s, PIECES)), dma((3, n_x)), dma((3, n_x)), dma((3 + PIECES,)),
    ]
    so = [
        v((n_s, n_x, part, 2 * rank), BF),
        v((plane, part, 2 * rank), BF),
        v((2, n_z, n_s, n_x, part, rank), BF),
        v((plane, high, rank), BF),
        v((chips, high, rank), BF),
        v((chips, high, rank), BF),
        v((chips, high, rank), BF),
        v((3 * layers + 1, own, rank), F32),
        v((layers, layers, own, rank), F32),
        v((layers, own, rank), F32),
        v((layers, own, rank), F32),
        dma((plane,)), dma((plane,)),
    ]
    so += [dma((n_z, layers))] * 6 + [dma((chips,))] * 2 + [dma((chips, 2))] * 2 + [dma((chips,))] * 16
    fi = [
        v((layers, group, cols), BF),
        v((layers, group, cols), BF),
        v((layers, group, cols), BF),
        v((plane, 8, rows), F32),
        v((layers, cols, 2 * rank), BF),
        v((n_s, cols, 2 * rank), BF),
        v((2, n_z // 2, cols, 2 * rank), BF),
        v((n_z // 2, cols, 2 * rank), BF),
        v((n_z // 2, cols, 2 * rank), BF),
        dma((plane,)), dma((plane,)), dma((n_s, WAVES)), dma((n_s, WAVES)),
    ]
    fi += [dma((n_z // 2, WAVES))] * 4 + [dma((1,))]
    return pl.pallas_call(
        functools.partial(main_kernel, sizes, dims, bound, len(ex), len(so)),
        out_shape=(
            jax.ShapeDtypeStruct((3, cols, 2 * rank), BF),
            jax.ShapeDtypeStruct((8, rows), F32),
        ),
        in_specs=[VMEM, VMEM, VMEM, ANY, ANY, VMEM, VMEM],
        out_specs=(VMEM, VMEM),
        scratch_shapes=shared + ex + so + fi,
        compiler_params=params(0),
        name="main",
    )(a, b, g, hidden, cot, users, inc)


def close_kernel(parts, row, gi_out, go_out, uw_out):
    rank = gi_out.shape[1]
    grad = parts[0].astype(F32) + parts[1].astype(F32) + parts[2].astype(F32)
    gi_out[...] = grad[:, :rank]
    go_out[...] = grad[:, rank:].T
    users, micro = uw_out.shape
    width = row.shape[1]
    weight = jnp.broadcast_to(row[0:1, :], (users, width))
    key = jnp.broadcast_to(row[1:2, :], (users, width))
    user = lax.broadcasted_iota(jnp.int32, (users, width), 0).astype(F32)
    lane = lax.broadcasted_iota(jnp.int32, (users, micro), 1)
    result = jnp.zeros((users, micro), F32)
    for m in range(micro):
        most = jnp.max(jnp.where(key == user + m * users, weight, 0.0), -1, keepdims=True)
        result = jnp.where(lane == m, most, result)
    uw_out[...] = result


def shards(hidden_in, cotangent, adapter_in, adapter_out, norm_gain, user_of_row, included):
    sizes = tuple(lax.axis_size(a) for a in ("section", "z", "x"))
    n_s = sizes[0]
    micro, rows, width = hidden_in.shape
    cols, rank = adapter_in.shape[1:]
    users = included.shape[1]
    bound = 0.8 * math.sqrt(n_s * (rows // users) * width * width)
    parts, row = main(
        sizes, (micro * rows, cols, rank, width), bound, adapter_in[0], adapter_out[0], norm_gain,
        hidden_in, cotangent, user_of_row, included.T,
    )
    gi, go, uw = pl.pallas_call(
        close_kernel,
        out_shape=(
            jax.ShapeDtypeStruct((cols, rank), F32),
            jax.ShapeDtypeStruct((rank, cols), F32),
            jax.ShapeDtypeStruct((users, micro), F32),
        ),
        in_specs=[VMEM, VMEM],
        out_specs=(VMEM,) * 3,
        name="close",
    )(parts, row)
    return (gi[None], go[None], uw.T)


def build(torus):
    dp = ("z", "x")
    return jax.shard_map(
        shards,
        mesh=torus,
        in_specs=(
            P(None, dp, None),
            P(None, dp, None),
            P("section", dp, None),
            P("section", None, dp),
            P("section", dp),
            P(None, dp),
            P(None, dp),
        ),
        out_specs=(P("section", dp, None), P("section", None, dp), P(None, dp)),
        check_vma=False,
    )


def solution(mesh):
    return build(Mesh(mesh.devices.reshape(mesh.shape["section"], 8, 4), ("section", "z", "x")))
```

```python
import functools
import math

import jax
import jax.numpy as jnp
from jax import lax
from jax.experimental import pallas as pl
from jax.experimental.pallas import tpu as pltpu
from jax.sharding import Mesh
from jax.sharding import PartitionSpec as P

F32 = jnp.float32
BF = jnp.bfloat16
MESH = pl.DeviceIdType.MESH
VMEM = pl.BlockSpec(memory_space=pltpu.VMEM)
ANY = pl.BlockSpec(memory_space=pl.ANY)
LIMIT = 60 * 1024 * 1024
PIECES = 4
WAVES = 2


def mm(a, b, ca, cb):
    return lax.dot_general(a, b, (((ca,), (cb,)), ((), ())), preferred_element_type=F32)


def loop(n, body):
    lax.fori_loop(0, n, lambda i, c: (body(i), c)[1], 0)


def remote(src, dst, send, recv, device):
    return pltpu.make_async_remote_copy(
        src_ref=src, dst_ref=dst, send_sem=send, recv_sem=recv, device_id=device, device_id_type=MESH
    )


def params(cid):
    return pltpu.CompilerParams(collective_id=cid, has_side_effects=True, vmem_limit_bytes=LIMIT)


def where_am_i():
    return tuple(lax.axis_index(a) for a in ("section", "z", "x"))


class Ring:
    def __init__(self, n, me, place, view, pieces, sems, want=None):
        self.n, self.me, self.place, self.view, self.pieces, self.sems = n, me, place, view, pieces, sems
        self.want = want
        self.far = n // 2

    def block(self, way, step):
        sign = 1 - 2 * way
        return lax.rem(self.me - sign * step + 2 * self.n, self.n)

    def copy(self, way, step, piece, block):
        sign = 1 - 2 * way
        ref = self.view(block, piece)
        send, recv = self.sems[2 * way].at[step, piece], self.sems[2 * way + 1].at[step, piece]
        return remote(ref, ref, send, recv, self.place(lax.rem(self.me + sign + self.n, self.n)))

    def guard(self, block, piece, fn):
        if self.want is None:
            fn()
        else:
            pl.when(self.want(block, piece))(fn)

    def each(self, step, fn):
        half = self.pieces // 2

        def body(i):
            if step + 1 < self.far:
                for way in (0, 1):
                    fn(way, i)
            else:
                fn(0, i)
                fn(1, i + half)

        count = self.pieces if step + 1 < self.far else half
        if self.want is None:
            for i in range(count):
                body(i)
        else:
            loop(count, body)

    def send(self, way, step, piece):
        block = self.block(way, step)
        self.guard(block, piece, lambda: self.copy(way, step, piece, block).start())

    def start(self):
        self.each(0, lambda way, piece: self.send(way, 0, piece))

    def run(self, arrived):
        half = self.pieces // 2

        def one(step, way, piece):
            block = self.block(way, step + 1)

            def take():
                self.copy(way, step, piece, block).wait_recv()
                if step + 2 < self.far:
                    self.copy(way, step + 1, piece, block).start()
                elif step + 2 == self.far:
                    onward = piece < half if way == 0 else piece >= half
                    if isinstance(onward, bool):
                        if onward:
                            self.copy(way, step + 1, piece, block).start()
                    else:
                        pl.when(onward)(lambda: self.copy(way, step + 1, piece, block).start())
                arrived(block, piece)

            self.guard(block, piece, take)

        for step in range(self.far):
            self.each(step, lambda way, piece: one(step, way, piece))

    def finish(self):
        def one(step, way, piece):
            block = self.block(way, step)
            self.guard(block, piece, lambda: self.copy(way, step, piece, block).wait_send())

        for step in range(self.far):
            self.each(step, lambda way, piece: one(step, way, piece))


def exchange_phase(
    sizes, a_ref, b_ref, g_ref, hid_ref, cot_ref, user_ref, inc_ref, w_all, h_all, c_all, i_all, ready,
    column, info, rs, rr, ls, lr, ys, yr, asend, arecv, lsem,
):
    n_s, n_z, n_x = sizes
    s, z, x = where_am_i()
    cols, rank = a_ref.shape
    micro, rows = user_ref.shape
    users = inc_ref.shape[0]
    gain = jnp.broadcast_to(g_ref[...].astype(F32), (rank, cols))
    column[z, :cols, :rank] = (a_ref[...].astype(F32) * gain.T).astype(BF)
    column[z, :cols, rank:] = b_ref[...].astype(F32).T.astype(BF)
    column[z, cols:, :] = jnp.broadcast_to(g_ref[...].astype(F32), (16, cols)).astype(BF)
    local = user_ref[...] - (z * n_x + x) * users
    included = jnp.zeros((micro, rows), F32)
    level = lax.broadcasted_iota(jnp.int32, (micro, rows), 0)
    for u in range(users):
        for m in range(micro):
            here = jnp.logical_and(local == u, level == m)
            included = jnp.where(here, inc_ref[u : u + 1, m : m + 1].astype(F32), included)
    key = (local + users * level).astype(F32)
    dev_rows = micro * rows
    lane = lax.broadcasted_iota(jnp.int32, (rows, dev_rows), 1)
    row = lax.broadcasted_iota(jnp.int32, (rows, dev_rows), 0)
    place = sum(jnp.where(lane == row + m * rows, 1.0, 0.0) for m in range(micro)).astype(BF)
    top = lax.broadcasted_iota(jnp.int32, (micro, dev_rows), 0)
    along = lax.broadcasted_iota(jnp.int32, (micro, dev_rows), 1)
    mine = jnp.logical_and(along >= top * rows, along < (top + 1) * rows)

    def flat(v):
        wide = mm(v.astype(BF), place, 1, 0)
        return jnp.sum(jnp.where(mine, wide, 0.0), 0, keepdims=True)

    which_row = lax.broadcasted_iota(jnp.int32, (16, dev_rows), 0)
    info[...] = jnp.where(which_row == 0, flat(key), flat(included)).astype(BF)
    ready()

    def act(which, to, slot):
        at = pl.ds(pl.multiple_of((s * n_x + to) * cols, cols), cols)
        src = (hid_ref.at[:, :, at], cot_ref.at[:, :, at], info)[which]
        dst = (h_all, c_all, i_all)[which].at[slot]
        return src, dst

    def a_copy(which, to, slot):
        src, dst = act(which, to, slot)
        return remote(src, dst, asend.at[which, to], arecv.at[which, slot], (s, z, to))

    step = cols // PIECES
    half = [slice(i * step, (i + 1) * step) for i in range(PIECES - 1)]
    half.append(slice((PIECES - 1) * step, cols + 16))

    def view(block, piece):
        return column.at[block, half[piece]]

    ring = Ring(n_z, z, lambda to: (s, to, x), view, PIECES, (rs, rr, ls, lr))
    ring.start()
    for which in range(3):
        for k in range(1, n_x):
            a_copy(which, lax.rem(x + k, n_x), x).start()
    for which in range(3):
        src, dst = act(which, x, x)
        pltpu.make_async_copy(src, dst, lsem.at[which]).start()

    def y_copy(block, slot, piece):
        return remote(
            column.at[block, half[piece]], w_all.at[slot, half[piece]],
            ys.at[block, piece], yr.at[slot, piece], (block, z, x),
        )

    def keep(piece):
        return pltpu.make_async_copy(
            column.at[s, half[piece]], w_all.at[s, half[piece]], lsem.at[3 + piece]
        )

    def onward(block, piece):
        @pl.when(block == s)
        def _():
            keep(piece).start()

        @pl.when(block != s)
        def _():
            y_copy(block, s, piece).start()

    for piece in range(PIECES):
        onward(z, piece)
    ring.run(onward)
    for which in range(3):
        src, dst = act(which, x, x)
        pltpu.make_async_copy(src, dst, lsem.at[which]).wait()
        for k in range(1, n_x):
            a_copy(which, x, lax.rem(x + n_x - k, n_x)).wait_recv()

    def not_me(fn):
        def body(k):
            for piece in range(PIECES):
                fn(lax.rem(s + 1 + k, n_s), piece)

        loop(n_s - 1, body)

    for piece in range(PIECES):
        keep(piece).wait()
    not_me(lambda k, piece: y_copy(s, k, piece).wait_recv())

    def drain():
        not_me(lambda k, piece: y_copy(k, s, piece).wait_send())
        for which in range(3):
            for k in range(1, n_x):
                a_copy(which, lax.rem(x + k, n_x), x).wait_send()
        ring.finish()

    return drain


class Plane:
    def __init__(self, sizes):
        n_s, n_z, n_x = sizes
        self.n_x = n_x
        self.chips = (n_s // 2) * n_x
        self.s, self.z, self.x = where_am_i()
        self.core = lax.rem(self.s, 2)
        self.chip = (self.s // 2) * n_x + self.x
        self.partner = (self.s + 1 - 2 * self.core, self.z, self.x)

    def peer(self, chip):
        return (2 * (chip // self.n_x) + self.core, self.z, lax.rem(chip, self.n_x))

    def ahead(self, k):
        return lax.rem(self.chip + k, self.chips)

    def behind(self, k):
        return lax.rem(self.chip + self.chips - k, self.chips)

    def others(self, fn):
        loop(self.chips - 1, lambda k: fn(k + 1))

    def greet_all(self, barrier):
        def one(chip):
            s2, z2, x2 = self.peer(chip)
            pl.semaphore_signal(barrier, inc=1, device_id=(s2, z2, x2), device_id_type=MESH)
            pl.semaphore_signal(
                barrier, inc=1, device_id=(s2 + 1 - 2 * self.core, z2, x2), device_id_type=MESH
            )

        self.others(lambda k: one(self.ahead(k)))
        pl.semaphore_signal(barrier, inc=1, device_id=self.partner, device_id_type=MESH)
        return 2 * self.chips - 1


class Cast:
    def __init__(self, plane, view, sems):
        self.p, self.view, self.sems = plane, view, sems

    def far(self, chip, owner):
        send, recv = self.sems[0].at[chip], self.sems[1].at[owner]
        ref = self.view(owner, self.p.core)
        return remote(ref, ref, send, recv, self.p.peer(chip))

    def near(self, chip, core):
        ref = self.view(chip, core)
        return remote(ref, ref, self.sems[2].at[chip], self.sems[3].at[chip], self.p.partner)

    def start(self):
        p = self.p
        p.others(lambda k: self.far(p.ahead(k), p.chip).start())
        self.near(p.chip, p.core).start()

    def relay(self):
        p = self.p

        def one(k):
            chip = p.behind(k)
            self.far(chip, chip).wait_recv()
            self.near(chip, p.core).start()

        p.others(one)

    def finish(self):
        p = self.p
        loop(p.chips, lambda i: self.near(i, 1 - p.core).wait_recv())
        loop(p.chips, lambda i: self.near(i, p.core).wait_send())
        p.others(lambda k: self.far(p.ahead(k), p.chip).wait_send())


def solve_phase(
    sizes, dims, w_all, h_all, c_all, low_out, err_out,
    gsend, grecv, gram, pbuf, prev, psum, crev, state, snap, full, rin,
    gs, gr, rs, rr, ls, lr, ns, nr, ps, pr, cs, cr, m0, m1, m2, m3, k0, k1, k2, k3, l0, l1, l2, l3, e0, e1, e2, e3,
):
    n_s, n_z, n_x = sizes
    rows, cols, rank, width = dims
    layers = n_s
    own = rows // n_s
    part = rank // n_x
    split = (2 * layers + 1) * own
    p = Plane(sizes)
    mine = w_all[p.z, :cols, rank:]
    for l in range(layers):
        g = mm(mine, w_all[l, :cols], 0, 0).astype(BF)
        gsend[l] = g.reshape(n_x, part, 2 * rank)
    n_plane = 2 * p.chips
    me = p.s * n_x + p.x

    def g_copy(to, slot):
        return remote(
            gsend.at[to // n_x, lax.rem(to, n_x)], grecv.at[slot], gs.at[to], gr.at[slot],
            (to // n_x, p.z, lax.rem(to, n_x)),
        )

    loop(n_plane - 1, lambda k: g_copy(lax.rem(me + 1 + k, n_plane), me).start())
    for l in range(layers):
        for i in range(n_x):
            zy = mm(h_all[i].reshape(rows, cols), w_all[l, :cols], 1, 0).astype(BF)
            ct = mm(c_all[i].reshape(rows, cols), w_all[l, :cols, rank:], 1, 0).astype(BF)
            at = slice(i * n_s, (i + 1) * n_s)
            for c, value in enumerate((zy[:, :rank], zy[:, rank:], ct)):
                r0 = (c * layers + l + c // 2) * own
                pbuf[at, r0 : r0 + own, :] = value.reshape(n_s, own, rank)
    for i in range(n_x):
        xf = h_all[i].reshape(rows, cols).astype(F32)
        sq = jnp.broadcast_to(jnp.sum(xf * xf, -1, keepdims=True), (rows, rank)).astype(BF)
        pbuf[i * n_s : (i + 1) * n_s, 2 * layers * own : split, :] = sq.reshape(n_s, own, rank)

    def block(chip, core):
        return (2 * (chip // n_x) + core) * n_x + lax.rem(chip, n_x)

    def pre(i):
        return remote(pbuf.at[block(i, 1 - p.core)], prev.at[i], ps.at[i], pr.at[i], p.partner)

    def pre_wait(i):
        return remote(pbuf.at[block(i, p.core)], prev.at[i], ps.at[i], pr.at[i], p.partner)

    halves = (slice(0, split), slice(split, (3 * layers + 1) * own))

    def c_copy(to, slot, piece):
        return remote(
            psum.at[to, halves[piece]], crev.at[slot, halves[piece]],
            cs.at[to, piece], cr.at[slot, piece], p.peer(to),
        )

    loop(p.chips, lambda k: pre(p.ahead(k)).start())

    loop(n_plane - 1, lambda k: g_copy(me, lax.rem(me + n_plane - 1 - k, n_plane)).wait_recv())
    grecv[me] = gsend[p.s, p.x]
    gsum = grecv[0].astype(F32)
    for k in range(1, n_plane):
        gsum = gsum + grecv[k].astype(F32)
    gram[0, p.z, p.s, p.x] = gsum[:, :rank].astype(BF)
    gram[1, p.z, p.s, p.x] = gsum[:, rank:].astype(BF)

    def gram_view(chip, core):
        return gram.at[:, p.z, 2 * (chip // n_x) + core, lax.rem(chip, n_x)]

    spread = Cast(p, gram_view, (m0, m1, m2, m3))
    spread.start()
    spread.relay()

    def gram_part(layer, piece, core):
        return gram.at[lax.rem(piece, 2), layer, 2 * (piece // 2) + core]

    def wanted(layer, piece, core):
        other = 2 * (piece // 2) + core
        upper = layer < other
        last = jnp.where(lax.rem(piece, 2) == 0, layer > other, layer == other)
        return jnp.logical_or(upper, last)

    ring = Ring(
        n_z, p.z, lambda to: (p.s, to, p.x), lambda layer, piece: gram_part(layer, piece, p.core),
        layers, (rs, rr, ls, lr), lambda layer, piece: wanted(layer, piece, p.core),
    )
    ring.start()

    def pair(k):
        i = p.ahead(k)
        pre_wait(i).wait_recv()
        total = pbuf[block(i, p.core)].astype(F32) + prev[i].astype(F32)
        psum[i] = total.astype(BF)

        @pl.when(i != p.chip)
        def _():
            c_copy(i, p.chip, 0).start()

    loop(p.chips, lambda k: pair(lax.rem(k + 1, p.chips)))
    p.others(lambda k: c_copy(p.ahead(k), p.chip, 1).start())

    def share(layer, piece, core):
        ref = gram_part(layer, piece, core)
        return remote(ref, ref, ns.at[layer, piece], nr.at[layer, piece], p.partner)

    ring.run(lambda layer, piece: share(layer, piece, p.core).start())
    spread.finish()
    crev[p.chip] = psum[p.chip]

    def collect(piece, at):
        p.others(lambda k: c_copy(p.chip, p.behind(k), piece).wait_recv())
        total = crev[0, halves[piece]].astype(F32)
        for k in range(1, p.chips):
            total = total + crev[k, halves[piece]].astype(F32)
        state[at] = total.reshape(-1, own, rank)

    collect(0, slice(0, 2 * layers + 1))

    def each_share(core, fn):
        def body(k):
            layer = lax.rem(p.z + 1 + k // layers, n_z)
            piece = lax.rem(k, layers)
            pl.when(wanted(layer, piece, core))(lambda: fn(share(layer, piece, core)))

        loop((n_z - 1) * layers, body)

    each_share(1 - p.core, lambda copy: copy.wait_recv())

    mid = layers // 2

    def low_view(first, last):
        def view(chip, core):
            dev = block(chip, core)
            return low_out.at[first:last, pl.ds(pl.multiple_of(dev * own, own), own), :]

        return view

    early = Cast(p, low_view(0, mid), (k0, k1, k2, k3))
    lows = Cast(p, low_view(mid, layers + 1), (l0, l1, l2, l3))

    def err_view(chip, core):
        dev = block(chip, core)
        return err_out.at[:, pl.ds(pl.multiple_of(dev * own, own), own), :]

    here = pl.ds(pl.multiple_of(me * own, own), own)
    square = state[2 * layers]
    zero = jnp.zeros((own, rank), F32)
    lane = lax.broadcasted_iota(jnp.int32, (own, rank), 1)
    scal = zero
    for l in range(layers):
        rinv = lax.rsqrt(square / width + 1e-05)
        u = state[l] * rinv
        low = u.astype(BF)
        full[l] = u
        rin[l] = rinv
        low_out[l, here, :] = low
        before = state[layers + l]
        for j in range(layers):
            snap[l, j] = state[layers + j]
            if j > l:
                pair_gram = jnp.concatenate(
                    [gram[0, l, j].reshape(rank, rank), gram[1, l, j].reshape(rank, rank)], 1
                )
                both = mm(low, pair_gram, 1, 0)
                state[j] = state[j] + both[:, :rank]
                state[layers + j] = state[layers + j] + both[:, rank:]
            else:
                one = mm(low, gram[1, j, l].reshape(rank, rank), 1, 1)
                state[layers + j] = state[layers + j] + one
        after = state[layers + l]
        square = square + jnp.sum(low.astype(F32) * (before + after), -1, keepdims=True)
        high = rinv.astype(BF).astype(F32)
        scal = jnp.where(lane == l, high, scal)
        scal = jnp.where(lane == layers + l, rinv - high, scal)
        if l == mid - 1:
            early.start()
    low_out[layers, here, :] = scal.astype(BF)
    lows.start()
    collect(1, slice(2 * layers + 1, 3 * layers + 1))
    scal = zero
    for l in range(layers - 1, -1, -1):
        err = state[2 * layers + 1 + l].astype(BF)
        mean = jnp.sum(err.astype(F32) * full[l], -1, keepdims=True) / width
        rinv = rin[l]
        cor = rinv * rinv * mean
        for j in range(l):
            back = mm(err, gram[0, j, l].reshape(rank, rank), 1, 1)
            state[2 * layers + 1 + j] = state[2 * layers + 1 + j] + rinv * back - cor * snap[l, j]
        err_out[l, here, :] = err
        scal = jnp.where(lane == l, cor, scal)
    err_out[layers, here, :] = scal.astype(BF)
    errs = Cast(p, err_view, (e0, e1, e2, e3))
    errs.start()
    early.relay()
    lows.relay()
    errs.relay()
    early.finish()
    lows.finish()

    def drain():
        loop(n_plane - 1, lambda k: g_copy(lax.rem(me + 1 + k, n_plane), me).wait_send())
        ring.finish()
        each_share(p.core, lambda copy: copy.wait_send())
        loop(p.chips, lambda k: pre(p.ahead(k)).wait_send())
        p.others(lambda k: c_copy(p.ahead(k), p.chip, 0).wait_send())
        p.others(lambda k: c_copy(p.ahead(k), p.chip, 1).wait_send())

    return drain, errs


def finish_phase(
    sizes, dims, bound, w_all, h_all, c_all, i_all, low_ref, err_ref, errs, grad_out, row_out,
    normed, deltas, hold, tot, gbuf, mid, acc, rbuf, lbuf, ts, tr, gs, gr, zs, zr, us, ur, lsem,
):
    n_s, n_z, n_x = sizes
    rows, cols, rank, width = dims
    layers = n_s
    p = Plane(sizes)
    s, z, x = p.s, p.z, p.x
    def factor(ref, i, l):
        return ref[layers, i * rows : (i + 1) * rows, l : l + 1].astype(F32)

    def rinv_of(i, l):
        return factor(low_ref, i, l) + factor(low_ref, i, layers + l)

    errs.finish()
    for i in range(n_x):
        at = slice(i * rows, (i + 1) * rows)
        h = h_all[i].reshape(rows, cols).astype(F32)
        for l in range(layers):
            gain = w_all[l, cols : cols + 8].astype(F32)[0:1, :]
            normed[l, at] = (h * rinv_of(i, l) * gain).astype(BF)
            hold[l, at] = h.astype(BF)
            if l + 1 < layers:
                h = h + mm(low_ref[l, at], w_all[l, :cols, rank:], 1, 1)
    sums = []
    for i in range(n_x):
        at = slice(i * rows, (i + 1) * rows)
        keyrow = i_all[i].astype(F32)[0:1, :]
        keys = jnp.broadcast_to(keyrow, (rows, rows))
        same = keys == keys.T
        pairs = jnp.zeros((rows, rows), F32)
        d = c_all[i].reshape(rows, cols).astype(F32)
        for l in range(layers - 1, -1, -1):
            db = d.astype(BF)
            deltas[l, at] = db
            lo, n, e = low_ref[l, at], normed[l, at], err_ref[l, at]
            pairs = pairs + mm(lo, lo, 1, 1) * mm(db, db, 1, 1)
            pairs = pairs + mm(n, n, 1, 1) * mm(e, e, 1, 1)
            if l > 0:
                d = d + rinv_of(i, l) * mm(e, w_all[l, :cols, :rank], 1, 1)
                d = d - factor(err_ref, i, l) * hold[l, at].astype(F32)
        pairs = jnp.where(same, pairs, 0.0)
        rowsum = jnp.broadcast_to(jnp.sum(pairs, -1, keepdims=True), (rows, rows))
        sums.append(jnp.sum(jnp.where(same, rowsum, 0.0), 0, keepdims=True))
    me = s * n_x + x
    n_plane = n_s * n_x
    pad = [jnp.zeros((8 - n_x, rows), F32)] if n_x < 8 else []
    tot[me] = jnp.concatenate(sums + pad, 0)

    def t_copy(to, slot):
        return remote(
            tot.at[slot], tot.at[slot], ts.at[to], tr.at[slot], (to // n_x, z, lax.rem(to, n_x))
        )

    loop(n_plane - 1, lambda k: t_copy(lax.rem(me + 1 + k, n_plane), me).start())
    loop(n_plane - 1, lambda k: t_copy(me, lax.rem(me + n_plane - 1 - k, n_plane)).wait_recv())
    total = tot[0]
    for k in range(1, n_plane):
        total = total + tot[k]
    clip = bound / jnp.maximum(jnp.sqrt(total), bound)

    weights = []
    for i in range(n_x):
        inc = i_all[i].astype(F32)[1:2, :]
        w = jnp.broadcast_to(inc * clip[i : i + 1], (rows, rows))
        weights.append(w.T[:, :rank])

        @pl.when(x == i)
        def _(w=w, i=i):
            row_out[0:1, :] = w[0:1, :]
            row_out[1:2, :] = i_all[i].astype(F32)[0:1, :]

    weight = jnp.concatenate(weights, 0)

    step_rows = cols // WAVES
    waves = [slice(i * step_rows, (i + 1) * step_rows) for i in range(WAVES)]

    def g_copy(to, slot, piece):
        part = waves[piece]
        return remote(
            gbuf.at[to, part], mid.at[slot, part], gs.at[to, piece], gr.at[slot, piece], (to, z, x)
        )

    def keep():
        return pltpu.make_async_copy(gbuf.at[s], mid.at[s], lsem.at[0])

    def gradient(l):
        we = (weight * err_ref[l].astype(F32)).astype(BF)
        wl = (weight * low_ref[l].astype(F32)).astype(BF)
        gbuf[l, :, :rank] = mm(normed[l], we, 0, 0).astype(BF)
        gbuf[l, :, rank:] = mm(deltas[l], wl, 0, 0).astype(BF)

        @pl.when(s != l)
        def _():
            g_copy(l, s, 0).start()

        @pl.when(s == l)
        def _():
            keep().start()

    loop(layers, gradient)
    for piece in range(1, WAVES):
        loop(n_s - 1, lambda k, piece=piece: g_copy(lax.rem(s + 1 + k, n_s), s, piece).start())
    keep().wait()

    def have(slot, piece):
        @pl.when(slot != s)
        def _():
            g_copy(s, slot, piece).wait_recv()

    far = n_z // 2

    def hops(way, piece):
        return far if way == (piece * 2) // WAVES else far - 1

    def hop(way, step, piece, src):
        part = waves[piece]
        if step + 1 == hops(way, piece):
            dst = grad_out.at[1 + way, part]
        else:
            dst = (rbuf, lbuf)[way].at[step, part]
        send, recv = ((zs, zr), (us, ur))[way]
        to = lax.rem(z + (1, n_z - 1)[way], n_z)
        return remote(src, dst, send.at[step, piece], recv.at[step, piece], (s, to, x))

    def source(way, step, piece, slot):
        part = waves[piece]
        return mid.at[slot, part] if step == 0 else acc.at[way, step - 1, part]

    def slot_of(way, gap):
        return lax.rem(z + (gap if way == 0 else n_z - gap), n_z)

    seen = set()

    def need(gap, piece):
        if (gap % n_z, piece) not in seen:
            seen.add((gap % n_z, piece))
            have(lax.rem(z + gap + n_z, n_z), piece)

    order = sorted((step + piece, piece, step) for step in range(far) for piece in range(WAVES))
    for _, piece, step in order:
        for way in (0, 1):
            if step >= hops(way, piece):
                continue
            gap = hops(way, piece) - step
            need(gap if way == 0 else -gap, piece)
            slot = slot_of(way, gap)
            part = waves[piece]
            src = source(way, step, piece, slot)
            if step > 0:
                hop(way, step - 1, piece, source(way, step - 1, piece, slot)).wait_recv()
                came = (rbuf, lbuf)[way][step - 1, part].astype(F32)
                acc[way, step - 1, part] = (came + mid[slot, part].astype(F32)).astype(BF)
            hop(way, step, piece, src).start()
    for piece in range(WAVES):
        need(0, piece)
    grad_out[0] = mid[z]
    for way in (0, 1):
        for piece in range(WAVES):
            step = hops(way, piece) - 1
            hop(way, step, piece, source(way, step, piece, z)).wait_recv()

    def drain():
        for way in (0, 1):
            for piece in range(WAVES):
                for step in range(hops(way, piece)):
                    hop(way, step, piece, source(way, step, piece, z)).wait_send()
        for piece in range(WAVES):
            loop(n_s - 1, lambda k, piece=piece: g_copy(lax.rem(s + 1 + k, n_s), s, piece).wait_send())
        loop(n_plane - 1, lambda k: t_copy(lax.rem(me + 1 + k, n_plane), me).wait_send())

    return drain


def main_kernel(
    sizes, dims, bound, n_ex, n_so, a_ref, b_ref, g_ref, hid_ref, cot_ref, user_ref, inc_ref,
    grad_out, row_out, w_all, h_all, c_all, i_all, low, err, *scratch,
):
    n_s, n_z, n_x = sizes
    p = Plane(sizes)
    barrier = pltpu.get_barrier_semaphore()
    count = p.greet_all(barrier)
    for k in (1, n_z - 1):
        pl.semaphore_signal(
            barrier, inc=1, device_id=(p.s, lax.rem(p.z + k, n_z), p.x), device_id_type=MESH
        )
    first = exchange_phase(
        sizes, a_ref, b_ref, g_ref, hid_ref, cot_ref, user_ref, inc_ref, w_all, h_all, c_all, i_all,
        lambda: pl.semaphore_wait(barrier, count + 2), *scratch[:n_ex],
    )
    second, errs = solve_phase(sizes, dims, w_all, h_all, c_all, low, err, *scratch[n_ex : n_ex + n_so])
    third = finish_phase(
        sizes, dims, bound, w_all, h_all, c_all, i_all, low, err, errs, grad_out, row_out,
        *scratch[n_ex + n_so :],
    )
    first()
    second()
    third()


def main(sizes, dims, bound, a, b, g, hidden, cot, users, inc):
    n_s, n_z, n_x = sizes
    rows, cols, rank, width = dims
    layers = n_s
    chips = (n_s // 2) * n_x
    plane = n_s * n_x
    own = rows // n_s
    group = rows * n_x
    part = rank // n_x
    high = (3 * layers + 1) * own
    dma = pltpu.SemaphoreType.DMA
    v = pltpu.VMEM
    slab = (n_x, *hidden.shape[:2], cols)
    shared = [
        v((n_s, cols + 16, 2 * rank), BF),
        v(slab, BF),
        v(slab, BF),
        v((n_x, 16, rows), BF),
        v((layers + 1, group, rank), BF),
        v((layers + 1, group, rank), BF),
    ]
    ex = [
        v((n_z, cols + 16, 2 * rank), BF),
        v((16, rows), BF),
        dma((n_z, PIECES)), dma((n_z, PIECES)), dma((n_z, PIECES)), dma((n_z, PIECES)),
        dma((n_z, PIECES)), dma((n_s, PIECES)), dma((3, n_x)), dma((3, n_x)), dma((3 + PIECES,)),
    ]
    so = [
        v((n_s, n_x, part, 2 * rank), BF),
        v((plane, part, 2 * rank), BF),
        v((2, n_z, n_s, n_x, part, rank), BF),
        v((plane, high, rank), BF),
        v((chips, high, rank), BF),
        v((chips, high, rank), BF),
        v((chips, high, rank), BF),
        v((3 * layers + 1, own, rank), F32),
        v((layers, layers, own, rank), F32),
        v((layers, own, rank), F32),
        v((layers, own, rank), F32),
        dma((plane,)), dma((plane,)),
    ]
    so += [dma((n_z, layers))] * 6 + [dma((chips,))] * 2 + [dma((chips, 2))] * 2 + [dma((chips,))] * 16
    fi = [
        v((layers, group, cols), BF),
        v((layers, group, cols), BF),
        v((layers, group, cols), BF),
        v((plane, 8, rows), F32),
        v((layers, cols, 2 * rank), BF),
        v((n_s, cols, 2 * rank), BF),
        v((2, n_z // 2, cols, 2 * rank), BF),
        v((n_z // 2, cols, 2 * rank), BF),
        v((n_z // 2, cols, 2 * rank), BF),
        dma((plane,)), dma((plane,)), dma((n_s, WAVES)), dma((n_s, WAVES)),
    ]
    fi += [dma((n_z // 2, WAVES))] * 4 + [dma((1,))]
    return pl.pallas_call(
        functools.partial(main_kernel, sizes, dims, bound, len(ex), len(so)),
        out_shape=(
            jax.ShapeDtypeStruct((3, cols, 2 * rank), BF),
            jax.ShapeDtypeStruct((8, rows), F32),
        ),
        in_specs=[VMEM, VMEM, VMEM, ANY, ANY, VMEM, VMEM],
        out_specs=(VMEM, VMEM),
        scratch_shapes=shared + ex + so + fi,
        compiler_params=params(0),
        name="main",
    )(a, b, g, hidden, cot, users, inc)


def close_kernel(parts, row, gi_out, go_out, uw_out):
    rank = gi_out.shape[1]
    grad = parts[0].astype(F32) + parts[1].astype(F32) + parts[2].astype(F32)
    gi_out[...] = grad[:, :rank]
    go_out[...] = grad[:, rank:].T
    users, micro = uw_out.shape
    width = row.shape[1]
    weight = jnp.broadcast_to(row[0:1, :], (users, width))
    key = jnp.broadcast_to(row[1:2, :], (users, width))
    user = lax.broadcasted_iota(jnp.int32, (users, width), 0).astype(F32)
    lane = lax.broadcasted_iota(jnp.int32, (users, micro), 1)
    result = jnp.zeros((users, micro), F32)
    for m in range(micro):
        most = jnp.max(jnp.where(key == user + m * users, weight, 0.0), -1, keepdims=True)
        result = jnp.where(lane == m, most, result)
    uw_out[...] = result


def shards(hidden_in, cotangent, adapter_in, adapter_out, norm_gain, user_of_row, included):
    sizes = tuple(lax.axis_size(a) for a in ("section", "z", "x"))
    n_s = sizes[0]
    micro, rows, width = hidden_in.shape
    cols, rank = adapter_in.shape[1:]
    users = included.shape[1]
    bound = 0.8 * math.sqrt(n_s * (rows // users) * width * width)
    parts, row = main(
        sizes, (micro * rows, cols, rank, width), bound, adapter_in[0], adapter_out[0], norm_gain,
        hidden_in, cotangent, user_of_row, included.T,
    )
    gi, go, uw = pl.pallas_call(
        close_kernel,
        out_shape=(
            jax.ShapeDtypeStruct((cols, rank), F32),
            jax.ShapeDtypeStruct((rank, cols), F32),
            jax.ShapeDtypeStruct((users, micro), F32),
        ),
        in_specs=[VMEM, VMEM],
        out_specs=(VMEM,) * 3,
        name="close",
    )(parts, row)
    return (gi[None], go[None], uw.T)


def build(torus):
    dp = ("z", "x")
    return jax.shard_map(
        shards,
        mesh=torus,
        in_specs=(
            P(None, dp, None),
            P(None, dp, None),
            P("section", dp, None),
            P("section", None, dp),
            P("section", dp),
            P(None, dp),
            P(None, dp),
        ),
        out_specs=(P("section", dp, None), P("section", None, dp), P(None, dp)),
        check_vma=False,
    )


def solution(mesh):
    return build(Mesh(mesh.devices.reshape(mesh.shape["section"], 8, 4), ("section", "z", "x")))
```
